32 devices in a mesh: seq: 8 (over z, y), head: 4 (over x, core).
Axes of the slice: x: 2, y: 2, z: 4, core: 2. Of those that a mesh axis runs over, the one named last changes fastest.
Arguments:
- queries: bfloat16 [8192, 512], P(('seq', 'head')), may hold values from -6 to 6
- key_rows: bfloat16 [8192, 128], P(('seq', 'head')), may hold values from -6 to 6
- value_rows: bfloat16 [8192, 128], P(('seq', 'head')), may hold values from -6 to 6
- out_grad: bfloat16 [8192, 512], P(('seq', 'head')), may hold values from -6 to 6
- doc_start: int32 [32], replicated, may hold values from 0 to 255
Outputs:
- outputs: bfloat16 [8192, 512], P(('seq', 'head'))
- query_grad: bfloat16 [8192, 512], P(('seq', 'head'))
- key_grad: bfloat16 [8192, 128], P(('seq', 'head'))
- value_grad: bfloat16 [8192, 128], P(('seq', 'head'))
The draws below stay inside these ranges and needn't reach their ends.
Inputs may be any that keep to these rules, and one draw needn't show every extreme that they name: doc_start[c] is the position within span c of the first token of a new document.
All inputs are finite; a program needn't handle non-finite values.
Results may differ from the reference program's by a relative error of at most 0.0065.
Values may be sent and summed in bfloat16 or wider, within the bound.
No kernel may reach another device: no remote copies, remote signals or barrier semaphores. Data moves between devices by JAX's collectives and lax.ppermute only.
A program may use at most 128 MiB of HBM per device.

```python
import math
import jax
import jax.numpy as jnp
from jax import lax

HD = 128
GROUP = 4
QH = 4
KVH = 1
SPAN = 256
HALO = 64
SPANS = 32
TOKENS = 8192


def draw_queries(key, part):
    shape = (TOKENS, QH * HD)
    values = jnp.clip(jax.random.normal(jax.random.fold_in(key, 1), shape), -6.0, 6.0)
    return values.astype(jnp.bfloat16)


def draw_key_rows(key, part):
    shape = (TOKENS, KVH * HD)
    values = jnp.clip(jax.random.normal(jax.random.fold_in(key, 2), shape), -6.0, 6.0)
    return values.astype(jnp.bfloat16)


def set_ends(values, rng, low, top_value):
    longest = values.shape.index(max(values.shape))
    spots = []
    for shift in (0, 1):
        where = [jax.random.randint(jax.random.fold_in(rng, axis), (), 0, length) for axis, length in enumerate(values.shape)]
        where[longest] = (where[longest] + shift) % values.shape[longest]
        spots.append(tuple(where))
    return values.at[spots[0]].set(low).at[spots[1]].set(top_value)


def block_levels(rng, shape, pieces, low, high):
    def one(axis_at, blocks):
        draws = jax.random.uniform(jax.random.fold_in(jax.random.fold_in(rng, 6), axis_at), (blocks,), jnp.float32, low / len(pieces), high / len(pieces))
        return jnp.repeat(jnp.exp(draws), shape[axis_at] // blocks).reshape((-1,) + (1,) * (len(shape) - axis_at - 1))

    level = one(*pieces[0])
    for cut in pieces[1:]:
        level = level * one(*cut)
    return level


def noise(key, shape, width, bound, pieces=(), held_as=jnp.bfloat16):
    level = block_levels(key, shape, pieces, -0.22, 0.18) if pieces else 1.0
    entries = jax.random.normal(key, shape, jnp.float32) * width * level
    return jnp.minimum(jnp.maximum(entries, -bound), bound).astype(held_as)


def setup_inputs(seed: int = 0) -> dict:
    streams_of = jax.random.split(jax.random.key(seed), 6)
    queries = draw_queries(jax.random.fold_in(streams_of[5], 71), 0)
    key_rows = draw_key_rows(jax.random.fold_in(streams_of[5], 71), 0)
    value_rows = noise(streams_of[2], (TOKENS, KVH * HD), 1.0, 6.0, ((0, 32),))
    out_grad = noise(streams_of[3], (TOKENS, QH * HD), 1.0, 6.0, ((0, 32),))
    doc_start = set_ends(jax.random.randint(streams_of[4], (SPANS,), 0, SPAN), jax.random.fold_in(streams_of[4], 1), 0, SPAN - 1).astype(jnp.int32)
    return dict(queries=queries, key_rows=key_rows, value_rows=value_rows, out_grad=out_grad, doc_start=doc_start)


masked_fill = -1e+30

def allowed_mask(first_row, row_count, key_count, halo_len, span_len, span_start, prev_begin, span_index):
    row_pos = first_row + lax.broadcasted_iota(jnp.int32, (row_count, key_count), 0)
    col_pos = lax.broadcasted_iota(jnp.int32, (row_count, key_count), 1) - halo_len
    return (col_pos <= row_pos) & ((col_pos >= span_start) | (span_start > row_pos)) & (col_pos >= prev_begin - span_len) & ((col_pos >= 0) | (span_index > 0))

def attend(query_rows, grad_rows, key_block, value_block, allowed, head_dim):
    score_scale = 1.0 / math.sqrt(head_dim)
    contract = (((1,), (1,)), ((), ()))
    backward = (((0,), (0,)), ((), ()))
    scores = lax.dot_general(query_rows, key_block, contract, preferred_element_type=jnp.float32) * score_scale
    masked = jnp.where(allowed, scores, masked_fill)
    row_max = lax.optimization_barrier(jnp.max(masked, axis=1, keepdims=True))
    exp_scores = jnp.where(allowed, jnp.exp(masked - row_max), 0.0)
    weights = exp_scores / lax.optimization_barrier(jnp.sum(exp_scores, axis=1, keepdims=True))
    weights_low = weights.astype(jnp.bfloat16)
    result = jnp.dot(weights_low, value_block, preferred_element_type=jnp.float32).astype(jnp.bfloat16)
    grad_weights = lax.dot_general(grad_rows, value_block, contract, preferred_element_type=jnp.float32)
    row_delta = lax.optimization_barrier(jnp.sum(weights * grad_weights, axis=1, keepdims=True))
    grad_scores = (weights * (grad_weights - row_delta) * score_scale).astype(jnp.bfloat16)
    grad_query = jnp.dot(grad_scores, key_block, preferred_element_type=jnp.float32)
    grad_key = lax.dot_general(grad_scores, query_rows, backward, preferred_element_type=jnp.float32)
    grad_value = lax.dot_general(weights_low, grad_rows, backward, preferred_element_type=jnp.float32)
    return (result, grad_query, grad_key, grad_value)

def reference(queries, key_rows, value_rows, out_grad, doc_start):
    span_count = TOKENS // SPAN
    head_q = queries.reshape(span_count, SPAN, KVH, GROUP, HD).transpose(0, 2, 3, 1, 4)
    head_grad = out_grad.reshape(span_count, SPAN, KVH, GROUP, HD).transpose(0, 2, 3, 1, 4)
    head_k = key_rows.reshape(span_count, SPAN, KVH, HD).transpose(0, 2, 1, 3)
    head_v = value_rows.reshape(span_count, SPAN, KVH, HD).transpose(0, 2, 1, 3)
    zero_rows = jnp.zeros((1, KVH, HALO, HD), key_rows.dtype)
    prev_k = jnp.concatenate([zero_rows, head_k[:-1, :, SPAN - HALO:]], axis=0)
    prev_v = jnp.concatenate([zero_rows, head_v[:-1, :, SPAN - HALO:]], axis=0)
    prev_start = jnp.concatenate([jnp.zeros((1,), jnp.int32), doc_start[:-1].astype(jnp.int32)])
    span_ids = jnp.arange(span_count, dtype=jnp.int32)

    def per_span(span_item):
        span_q, span_grad, span_k, span_v, halo_k, halo_v, span_start, prev_begin, span_index = span_item
        allowed = allowed_mask(0, SPAN, HALO + SPAN, HALO, SPAN, span_start, prev_begin, span_index)

        def per_group(group_item):
            group_q, group_grad, own_k, own_v, edge_k, edge_v = group_item
            key_block = jnp.concatenate([edge_k, own_k], axis=0)
            value_block = jnp.concatenate([edge_v, own_v], axis=0)

            def per_head(head_item):
                result, grad_query, grad_key, grad_value = attend(head_item[0], head_item[1], key_block, value_block, allowed, HD)
                return (result, grad_query.astype(jnp.bfloat16), grad_key, grad_value)
            result, grad_query, grad_key, grad_value = lax.map(per_head, (group_q, group_grad))
            return (result, grad_query, lax.optimization_barrier(jnp.sum(grad_key, axis=0)), lax.optimization_barrier(jnp.sum(grad_value, axis=0)))
        return lax.map(per_group, (span_q, span_grad, span_k, span_v, halo_k, halo_v))
    result, grad_query, grad_key, grad_value = lax.map(per_span, (head_q, head_grad, head_k, head_v, prev_k, prev_v, doc_start.astype(jnp.int32), prev_start, span_ids))
    outputs = result.transpose(0, 3, 1, 2, 4).reshape(TOKENS, QH * HD)
    query_grad = grad_query.transpose(0, 3, 1, 2, 4).reshape(TOKENS, QH * HD)

    def combine(grad_ext):
        own_rows = grad_ext[:, :, HALO:]
        next_rows = jnp.concatenate([grad_ext[1:, :, :HALO], jnp.zeros((1, KVH, HALO, HD), jnp.float32)], axis=0)
        own_rows = jnp.concatenate([own_rows[:, :, :SPAN - HALO], own_rows[:, :, SPAN - HALO:] + next_rows], axis=2)
        return own_rows.transpose(0, 2, 1, 3).reshape(TOKENS, KVH * HD).astype(jnp.bfloat16)
    return (outputs, query_grad, combine(grad_key), combine(grad_value))
```

```python
import math

import jax
import jax.numpy as jnp
from jax import lax
from jax.experimental import pallas as pl
from jax.experimental.pallas import tpu as pltpu
from jax.sharding import PartitionSpec as P

HD = 128
GROUP = 4
SPANS_DEV = 4
SCALE = 1.0 / math.sqrt(HD)
LOG2_SCALE = SCALE * math.log2(math.e)


masked_fill = -1e30


def passed_along(value, axis, steps):
    count = lax.axis_size(axis)
    first, last = (max(0, -steps), min(count, count - steps))
    return lax.ppermute(value, axis, [(source, source + steps) for source in range(first, last)])


def allowed_mask(
    first_row, row_count, key_count, halo_len, span_len, span_start, prev_begin, span_index
):
    row_pos = first_row + lax.broadcasted_iota(jnp.int32, (row_count, key_count), 0)
    col_pos = lax.broadcasted_iota(jnp.int32, (row_count, key_count), 1) - halo_len
    return (
        (col_pos <= row_pos)
        & ((col_pos >= span_start) | (span_start > row_pos))
        & (col_pos >= prev_begin - span_len)
        & ((col_pos >= 0) | (span_index > 0))
    )


def attend(query_rows, grad_rows, key_block, value_block, allowed, head_dim):
    score_scale = 1.0 / math.sqrt(head_dim)
    contract = (((2,), (2,)), ((0,), (0,)))
    forward = (((2,), (1,)), ((0,), (0,)))
    backward = (((1,), (1,)), ((0,), (0,)))
    scores = (
        lax.dot_general(query_rows, key_block, contract, preferred_element_type=jnp.float32)
        * score_scale
    )
    masked = jnp.where(allowed, scores, masked_fill)
    row_max = jnp.max(masked, axis=2, keepdims=True)
    exp_scores = jnp.where(allowed, jnp.exp(masked - row_max), 0.0)
    weights = exp_scores / jnp.sum(exp_scores, axis=2, keepdims=True)
    weights_low = weights.astype(jnp.bfloat16)
    result = lax.dot_general(
        weights_low, value_block, forward, preferred_element_type=jnp.float32
    ).astype(jnp.bfloat16)
    grad_weights = lax.dot_general(
        grad_rows, value_block, contract, preferred_element_type=jnp.float32
    )
    row_delta = jnp.sum(weights * grad_weights, axis=2, keepdims=True)
    grad_scores = (weights * (grad_weights - row_delta) * score_scale).astype(jnp.bfloat16)
    grad_query = lax.dot_general(
        grad_scores, key_block, forward, preferred_element_type=jnp.float32
    )
    grad_key = lax.dot_general(
        grad_scores, query_rows, backward, preferred_element_type=jnp.float32
    )
    grad_value = lax.dot_general(
        weights_low, grad_rows, backward, preferred_element_type=jnp.float32
    )
    return (result, grad_query, grad_key, grad_value)


def spans_over_devices(queries, key_rows, value_rows, out_grad, doc_start):
    tok_count = queries.shape[0]
    head_count = lax.axis_size("head")
    group_rows = tok_count * head_count
    span_len = group_rows // SPANS_DEV
    halo_len = span_len // 4
    half_len = span_len // 2
    rest_len = span_len - halo_len
    head_q, head_grad = (
        lax.all_to_all(queries, "head", split_axis=1, concat_axis=0, tiled=True),
        lax.all_to_all(out_grad, "head", split_axis=1, concat_axis=0, tiled=True),
    )
    full_k, full_v = (
        lax.all_gather(key_rows, "head", axis=0, tiled=True),
        lax.all_gather(value_rows, "head", axis=0, tiled=True),
    )
    column = lax.axis_index("head") // GROUP * HD
    head_k = lax.dynamic_slice_in_dim(full_k, column, HD, 1)
    head_v = lax.dynamic_slice_in_dim(full_v, column, HD, 1)
    query_3 = head_q.reshape(SPANS_DEV, span_len, HD)
    grad_3 = head_grad.reshape(SPANS_DEV, span_len, HD)
    keys_3 = head_k.reshape(SPANS_DEV, span_len, HD)
    values_3 = head_v.reshape(SPANS_DEV, span_len, HD)
    tail_k = keys_3[:, rest_len:]
    tail_v = values_3[:, rest_len:]
    edge_last_k, edge_last_v = passed_along(
        (tail_k[SPANS_DEV - 1], tail_v[SPANS_DEV - 1]), "seq", 1
    )
    edge_k = jnp.concatenate([edge_last_k[None], tail_k[: SPANS_DEV - 1]], axis=0)
    edge_v = jnp.concatenate([edge_last_v[None], tail_v[: SPANS_DEV - 1]], axis=0)
    key_block = jnp.concatenate([edge_k, keys_3], axis=1)
    value_block = jnp.concatenate([edge_v, values_3], axis=1)
    first_span = lax.axis_index("seq") * SPANS_DEV
    span_starts = lax.dynamic_slice_in_dim(doc_start, first_span, SPANS_DEV)
    before_start = lax.dynamic_slice_in_dim(doc_start, jnp.maximum(first_span - 1, 0), 1)
    prev_starts = jnp.concatenate([before_start, span_starts[: SPANS_DEV - 1]], axis=0)
    span_ids = first_span + jnp.arange(SPANS_DEV, dtype=jnp.int32)
    span_starts = span_starts.reshape(SPANS_DEV, 1, 1)
    prev_starts = prev_starts.reshape(SPANS_DEV, 1, 1)
    span_ids = span_ids.reshape(SPANS_DEV, 1, 1)
    grad_key = jnp.zeros((SPANS_DEV, halo_len + span_len, HD), jnp.float32)
    grad_value = jnp.zeros((SPANS_DEV, halo_len + span_len, HD), jnp.float32)
    results = []
    query_grads = []
    for block_index in range(2):
        first_row = block_index * half_len
        key_count = halo_len + first_row + half_len
        allowed = allowed_mask(
            first_row, half_len, key_count, halo_len, span_len, span_starts, prev_starts, span_ids
        )
        result, grad_query, part_key, part_value = attend(
            query_3[:, first_row : first_row + half_len],
            grad_3[:, first_row : first_row + half_len],
            key_block[:, :key_count],
            value_block[:, :key_count],
            allowed,
            HD,
        )
        results.append(result)
        query_grads.append(grad_query.astype(jnp.bfloat16))
        grad_key = grad_key.at[:, :key_count].add(part_key)
        grad_value = grad_value.at[:, :key_count].add(part_value)
    next_last_k, next_last_v = passed_along(
        (grad_key[0, :halo_len], grad_value[0, :halo_len]), "seq", -1
    )
    next_k = jnp.concatenate([grad_key[1:, :halo_len], next_last_k[None]], axis=0)
    next_v = jnp.concatenate([grad_value[1:, :halo_len], next_last_v[None]], axis=0)
    own_k = jnp.concatenate(
        [grad_key[:, halo_len : halo_len + rest_len], grad_key[:, halo_len + rest_len :] + next_k],
        axis=1,
    ).reshape(group_rows, HD)
    own_v = jnp.concatenate(
        [
            grad_value[:, halo_len : halo_len + rest_len],
            grad_value[:, halo_len + rest_len :] + next_v,
        ],
        axis=1,
    ).reshape(group_rows, HD)
    all_results = jnp.concatenate(results, axis=1).reshape(group_rows, HD)
    all_query_grads = jnp.concatenate(query_grads, axis=1).reshape(group_rows, HD)
    outputs, query_grad = (
        lax.all_to_all(all_results, "head", split_axis=0, concat_axis=1, tiled=True),
        lax.all_to_all(all_query_grads, "head", split_axis=0, concat_axis=1, tiled=True),
    )
    wide_gk, wide_gv = (
        lax.all_to_all(own_k, "head", split_axis=0, concat_axis=1, tiled=True),
        lax.all_to_all(own_v, "head", split_axis=0, concat_axis=1, tiled=True),
    )
    group_total = wide_gk.shape[1] // (GROUP * HD)
    key_grad = (
        wide_gk.reshape(tok_count, group_total, GROUP, HD)
        .sum(axis=2)
        .reshape(tok_count, group_total * HD)
        .astype(jnp.bfloat16)
    )
    value_grad = (
        wide_gv.reshape(tok_count, group_total, GROUP, HD)
        .sum(axis=2)
        .reshape(tok_count, group_total * HD)
        .astype(jnp.bfloat16)
    )
    return (outputs, query_grad, key_grad, value_grad)


ROWS_BY_ROWS = (((1,), (1,)), ((), ()))
COLS_BY_COLS = (((0,), (0,)), ((), ()))
PLAIN = (((1,), (0,)), ((), ()))


def dot(left, right, dims):
    return lax.dot_general(left, right, dims, preferred_element_type=jnp.float32)


def head_cols(head):
    return slice(head * HD, (head + 1) * HD)


def own_kernel(span, halo, doc_ref, q_ref, g_ref, k_ref, v_ref, exp_ref, gw_ref, stat_ref, mask_ref):
    device = lax.axis_index("seq") * lax.axis_size("head") + lax.axis_index("head")
    start = doc_ref[device]
    before = doc_ref[jnp.maximum(device - 1, 0)]
    key_pos = lax.broadcasted_iota(jnp.int32, (span, span), 0)
    row_pos = lax.broadcasted_iota(jnp.int32, (span, span), 1)
    allowed = (key_pos <= row_pos) & ((key_pos >= start) | (start > row_pos))
    halo_pos = lax.broadcasted_iota(jnp.int32, (halo, span), 0) - halo
    halo_row = lax.broadcasted_iota(jnp.int32, (halo, span), 1)
    first = jnp.where(device > 0, before - span, span)
    halo_ok = ((halo_pos >= start) | (start > halo_row)) & (halo_pos >= first)
    mask_ref[...] = jnp.where(halo_ok, 0.0, masked_fill)
    keys = k_ref[...]
    values = v_ref[...]
    for head in range(GROUP):
        scores = dot(keys, q_ref[:, head_cols(head)], ROWS_BY_ROWS) * LOG2_SCALE
        scores = jnp.where(allowed, scores, masked_fill)
        top = jnp.max(scores, axis=0, keepdims=True)
        weights = jnp.exp2(scores - top)
        grad_weights = dot(values, g_ref[:, head_cols(head)], ROWS_BY_ROWS)
        exp_ref[head * span : (head + 1) * span] = weights
        gw_ref[head * span : (head + 1) * span] = grad_weights
        stat_ref[head : head + 1] = top
        stat_ref[GROUP + head : GROUP + head + 1] = jnp.sum(weights, axis=0, keepdims=True)
        stat_ref[2 * GROUP + head : 2 * GROUP + head + 1] = jnp.sum(
            weights * grad_weights, axis=0, keepdims=True
        )


def halo_kernel(halo, mask_ref, edge_ref, q_ref, g_ref, stat_ref, p_ref, ds_ref, row_ref, back_ref):
    keys = edge_ref[:, :HD]
    values = edge_ref[:, HD:]
    mask = mask_ref[...]
    grad_key = jnp.zeros((halo, HD), jnp.float32)
    grad_value = jnp.zeros((halo, HD), jnp.float32)
    for head in range(GROUP):
        queries = q_ref[:, head_cols(head)]
        grads = g_ref[:, head_cols(head)]
        scores = dot(keys, queries, ROWS_BY_ROWS) * LOG2_SCALE + mask
        grad_weights = dot(values, grads, ROWS_BY_ROWS)
        own_top = stat_ref[head : head + 1]
        top = jnp.maximum(jnp.max(scores, axis=0, keepdims=True), own_top)
        weights = jnp.exp2(scores - top)
        shift = jnp.exp2(own_top - top)
        total = stat_ref[GROUP + head : GROUP + head + 1] * shift + jnp.sum(weights, axis=0, keepdims=True)
        inner = stat_ref[2 * GROUP + head : 2 * GROUP + head + 1] * shift + jnp.sum(
            weights * grad_weights, axis=0, keepdims=True
        )
        delta = inner / total
        p = weights / total
        p_low = p.astype(jnp.bfloat16)
        ds_low = (p * (grad_weights - delta) * SCALE).astype(jnp.bfloat16)
        grad_key += dot(ds_low, queries, PLAIN)
        grad_value += dot(p_low, grads, PLAIN)
        p_ref[head * halo : (head + 1) * halo] = p_low
        ds_ref[head * halo : (head + 1) * halo] = ds_low
        row_ref[head : head + 1] = shift / total
        row_ref[GROUP + head : GROUP + head + 1] = delta
    back_ref[:, :HD] = grad_key.astype(back_ref.dtype)
    back_ref[:, HD:] = grad_value.astype(back_ref.dtype)


def rest_kernel(
    span, halo, q_ref, g_ref, k_ref, v_ref, edge_ref, exp_ref, gw_ref, p_ref, ds_ref, row_ref,
    out_ref, dq_ref, dk_ref, dv_ref, tail_ref,
):
    keys = k_ref[...]
    values = v_ref[...]
    edge_keys = edge_ref[:, :HD]
    edge_values = edge_ref[:, HD:]
    grad_key = jnp.zeros((span, HD), jnp.float32)
    grad_value = jnp.zeros((span, HD), jnp.float32)
    for head in range(GROUP):
        queries = q_ref[:, head_cols(head)]
        grads = g_ref[:, head_cols(head)]
        p = exp_ref[head * span : (head + 1) * span] * row_ref[head : head + 1]
        p_low = p.astype(jnp.bfloat16)
        inner = gw_ref[head * span : (head + 1) * span] - row_ref[GROUP + head : GROUP + head + 1]
        ds_low = (p * inner * SCALE).astype(jnp.bfloat16)
        p_edge = p_ref[head * halo : (head + 1) * halo]
        ds_edge = ds_ref[head * halo : (head + 1) * halo]
        out = dot(p_low, values, COLS_BY_COLS) + dot(p_edge, edge_values, COLS_BY_COLS)
        out_ref[:, head_cols(head)] = out.astype(jnp.bfloat16)
        dq = dot(ds_low, keys, COLS_BY_COLS) + dot(ds_edge, edge_keys, COLS_BY_COLS)
        dq_ref[:, head_cols(head)] = dq.astype(jnp.bfloat16)
        grad_key += dot(ds_low, queries, PLAIN)
        grad_value += dot(p_low, grads, PLAIN)
    dk_ref[...] = grad_key.astype(jnp.bfloat16)
    dv_ref[...] = grad_value.astype(jnp.bfloat16)
    tail_ref[:, :HD] = grad_key[span - halo :]
    tail_ref[:, HD:] = grad_value[span - halo :]


def tail_kernel(span, halo, tail_ref, back_ref, dk_in, dv_in, dk_ref, dv_ref, sum_ref, sems):
    del dk_in, dv_in
    total = tail_ref[...] + back_ref[...].astype(jnp.float32)
    sum_ref[0] = total[:, :HD].astype(jnp.bfloat16)
    sum_ref[1] = total[:, HD:].astype(jnp.bfloat16)
    copies = [
        pltpu.make_async_copy(sum_ref.at[at], ref.at[pl.ds(span - halo, halo)], sems.at[at])
        for at, ref in enumerate((dk_ref, dv_ref))
    ]
    for copy in copies:
        copy.start()
    for copy in copies:
        copy.wait()


def passed_on(value, steps):
    axes = ("seq", "head")
    count = lax.axis_size("seq") * lax.axis_size("head")
    first, last = (max(0, -steps), min(count, count - steps))
    return lax.ppermute(value, axes, [(source, source + steps) for source in range(first, last)])


def span_on_device(queries, key_rows, value_rows, out_grad, doc_start):
    span = queries.shape[0]
    halo = span // 4
    vmem = pl.BlockSpec(memory_space=pltpu.VMEM)
    smem = pl.BlockSpec(memory_space=pltpu.SMEM)
    hbm = pl.BlockSpec(memory_space=pl.ANY)
    f32, bf16 = (jnp.float32, jnp.bfloat16)
    near = lambda value: pltpu.with_memory_space_constraint(value, pltpu.VMEM)
    edge = passed_on(
        jnp.concatenate([key_rows[span - halo :], value_rows[span - halo :]], axis=1), 1
    )
    exp_own, gw_own, stats, mask = pl.pallas_call(
        lambda *refs: own_kernel(span, halo, *refs),
        in_specs=[smem, vmem, vmem, vmem, vmem],
        out_specs=[vmem] * 4,
        out_shape=[
            pltpu.VMEM((GROUP * span, span), f32),
            pltpu.VMEM((GROUP * span, span), f32),
            pltpu.VMEM((4 * GROUP, span), f32),
            pltpu.VMEM((halo, span), f32),
        ],
        name="own_scores",
    )(doc_start, near(queries), near(out_grad), near(key_rows), near(value_rows))
    p_edge, ds_edge, rows, back = pl.pallas_call(
        lambda *refs: halo_kernel(halo, *refs),
        in_specs=[vmem] * 5,
        out_specs=[vmem] * 4,
        out_shape=[
            pltpu.VMEM((GROUP * halo, span), bf16),
            pltpu.VMEM((GROUP * halo, span), bf16),
            pltpu.VMEM((2 * GROUP, span), f32),
            pltpu.VMEM((halo, 2 * HD), f32),
        ],
        name="halo_grads",
    )(near(mask), near(edge), near(queries), near(out_grad), near(stats))
    returned = passed_on(back, -1)
    outputs, query_grad, key_grad, value_grad, tail = pl.pallas_call(
        lambda *refs: rest_kernel(span, halo, *refs),
        in_specs=[vmem] * 10,
        out_specs=[vmem] * 5,
        out_shape=[
            jax.ShapeDtypeStruct(queries.shape, bf16),
            jax.ShapeDtypeStruct(queries.shape, bf16),
            jax.ShapeDtypeStruct(key_rows.shape, bf16),
            jax.ShapeDtypeStruct(key_rows.shape, bf16),
            pltpu.VMEM((halo, 2 * HD), f32),
        ],
        name="own_grads",
    )(*[near(x) for x in (queries, out_grad, key_rows, value_rows, edge, exp_own, gw_own, p_edge, ds_edge, rows)])
    key_grad, value_grad = pl.pallas_call(
        lambda *refs: tail_kernel(span, halo, *refs),
        in_specs=[vmem, vmem, hbm, hbm],
        out_specs=[hbm, hbm],
        out_shape=[
            jax.ShapeDtypeStruct(key_rows.shape, bf16),
            jax.ShapeDtypeStruct(key_rows.shape, bf16),
        ],
        scratch_shapes=[pltpu.VMEM((2, halo, HD), bf16), pltpu.SemaphoreType.DMA((2,))],
        input_output_aliases={2: 0, 3: 1},
        name="tail_grads",
    )(near(tail), near(returned), key_grad, value_grad)
    return (outputs, query_grad, key_grad, value_grad)


def per_device(queries, key_rows, value_rows, out_grad, doc_start):
    span = queries.shape[0] * lax.axis_size("head") // SPANS_DEV
    whole_span = span == queries.shape[0] and key_rows.shape[1] == HD and queries.shape[1] == GROUP * HD
    plan = span_on_device if whole_span else spans_over_devices
    return plan(queries, key_rows, value_rows, out_grad, doc_start)


def solution(mesh):
    placed = (
        P(("seq", "head"), None),
        P(("seq", "head"), None),
        P(("seq", "head"), None),
        P(("seq", "head"), None),
        P(),
    )
    return jax.shard_map(
        per_device,
        mesh=mesh,
        in_specs=placed,
        out_specs=(
            P(("seq", "head"), None),
            P(("seq", "head"), None),
            P(("seq", "head"), None),
            P(("seq", "head"), None),
        ),
        check_vma=False,
    )
```

```python
import math

import jax
import jax.numpy as jnp
from jax import lax
from jax.experimental import pallas as pl
from jax.experimental.pallas import tpu as pltpu
from jax.sharding import PartitionSpec as P

HD = 128
GROUP = 4
SPANS_DEV = 4
SCALE = 1.0 / math.sqrt(HD)
LOG2_SCALE = SCALE * math.log2(math.e)
VMEM_GRANT = 16 * 1024 * 1024


masked_fill = -1e30


def passed_along(value, axis, steps):
    count = lax.axis_size(axis)
    first, last = (max(0, -steps), min(count, count - steps))
    return lax.ppermute(value, axis, [(source, source + steps) for source in range(first, last)])


def allowed_mask(
    first_row, row_count, key_count, halo_len, span_len, span_start, prev_begin, span_index
):
    row_pos = first_row + lax.broadcasted_iota(jnp.int32, (row_count, key_count), 0)
    col_pos = lax.broadcasted_iota(jnp.int32, (row_count, key_count), 1) - halo_len
    return (
        (col_pos <= row_pos)
        & ((col_pos >= span_start) | (span_start > row_pos))
        & (col_pos >= prev_begin - span_len)
        & ((col_pos >= 0) | (span_index > 0))
    )


def attend(query_rows, grad_rows, key_block, value_block, allowed, head_dim):
    score_scale = 1.0 / math.sqrt(head_dim)
    contract = (((2,), (2,)), ((0,), (0,)))
    forward = (((2,), (1,)), ((0,), (0,)))
    backward = (((1,), (1,)), ((0,), (0,)))
    scores = (
        lax.dot_general(query_rows, key_block, contract, preferred_element_type=jnp.float32)
        * score_scale
    )
    masked = jnp.where(allowed, scores, masked_fill)
    row_max = jnp.max(masked, axis=2, keepdims=True)
    exp_scores = jnp.where(allowed, jnp.exp(masked - row_max), 0.0)
    weights = exp_scores / jnp.sum(exp_scores, axis=2, keepdims=True)
    weights_low = weights.astype(jnp.bfloat16)
    result = lax.dot_general(
        weights_low, value_block, forward, preferred_element_type=jnp.float32
    ).astype(jnp.bfloat16)
    grad_weights = lax.dot_general(
        grad_rows, value_block, contract, preferred_element_type=jnp.float32
    )
    row_delta = jnp.sum(weights * grad_weights, axis=2, keepdims=True)
    grad_scores = (weights * (grad_weights - row_delta) * score_scale).astype(jnp.bfloat16)
    grad_query = lax.dot_general(
        grad_scores, key_block, forward, preferred_element_type=jnp.float32
    )
    grad_key = lax.dot_general(
        grad_scores, query_rows, backward, preferred_element_type=jnp.float32
    )
    grad_value = lax.dot_general(
        weights_low, grad_rows, backward, preferred_element_type=jnp.float32
    )
    return (result, grad_query, grad_key, grad_value)


def spans_over_devices(queries, key_rows, value_rows, out_grad, doc_start):
    tok_count = queries.shape[0]
    head_count = lax.axis_size("head")
    group_rows = tok_count * head_count
    span_len = group_rows // SPANS_DEV
    halo_len = span_len // 4
    half_len = span_len // 2
    rest_len = span_len - halo_len
    head_q, head_grad = (
        lax.all_to_all(queries, "head", split_axis=1, concat_axis=0, tiled=True),
        lax.all_to_all(out_grad, "head", split_axis=1, concat_axis=0, tiled=True),
    )
    full_k, full_v = (
        lax.all_gather(key_rows, "head", axis=0, tiled=True),
        lax.all_gather(value_rows, "head", axis=0, tiled=True),
    )
    column = lax.axis_index("head") // GROUP * HD
    head_k = lax.dynamic_slice_in_dim(full_k, column, HD, 1)
    head_v = lax.dynamic_slice_in_dim(full_v, column, HD, 1)
    query_3 = head_q.reshape(SPANS_DEV, span_len, HD)
    grad_3 = head_grad.reshape(SPANS_DEV, span_len, HD)
    keys_3 = head_k.reshape(SPANS_DEV, span_len, HD)
    values_3 = head_v.reshape(SPANS_DEV, span_len, HD)
    tail_k = keys_3[:, rest_len:]
    tail_v = values_3[:, rest_len:]
    edge_last_k, edge_last_v = passed_along(
        (tail_k[SPANS_DEV - 1], tail_v[SPANS_DEV - 1]), "seq", 1
    )
    edge_k = jnp.concatenate([edge_last_k[None], tail_k[: SPANS_DEV - 1]], axis=0)
    edge_v = jnp.concatenate([edge_last_v[None], tail_v[: SPANS_DEV - 1]], axis=0)
    key_block = jnp.concatenate([edge_k, keys_3], axis=1)
    value_block = jnp.concatenate([edge_v, values_3], axis=1)
    first_span = lax.axis_index("seq") * SPANS_DEV
    span_starts = lax.dynamic_slice_in_dim(doc_start, first_span, SPANS_DEV)
    before_start = lax.dynamic_slice_in_dim(doc_start, jnp.maximum(first_span - 1, 0), 1)
    prev_starts = jnp.concatenate([before_start, span_starts[: SPANS_DEV - 1]], axis=0)
    span_ids = first_span + jnp.arange(SPANS_DEV, dtype=jnp.int32)
    span_starts = span_starts.reshape(SPANS_DEV, 1, 1)
    prev_starts = prev_starts.reshape(SPANS_DEV, 1, 1)
    span_ids = span_ids.reshape(SPANS_DEV, 1, 1)
    grad_key = jnp.zeros((SPANS_DEV, halo_len + span_len, HD), jnp.float32)
    grad_value = jnp.zeros((SPANS_DEV, halo_len + span_len, HD), jnp.float32)
    results = []
    query_grads = []
    for block_index in range(2):
        first_row = block_index * half_len
        key_count = halo_len + first_row + half_len
        allowed = allowed_mask(
            first_row, half_len, key_count, halo_len, span_len, span_starts, prev_starts, span_ids
        )
        result, grad_query, part_key, part_value = attend(
            query_3[:, first_row : first_row + half_len],
            grad_3[:, first_row : first_row + half_len],
            key_block[:, :key_count],
            value_block[:, :key_count],
            allowed,
            HD,
        )
        results.append(result)
        query_grads.append(grad_query.astype(jnp.bfloat16))
        grad_key = grad_key.at[:, :key_count].add(part_key)
        grad_value = grad_value.at[:, :key_count].add(part_value)
    next_last_k, next_last_v = passed_along(
        (grad_key[0, :halo_len], grad_value[0, :halo_len]), "seq", -1
    )
    next_k = jnp.concatenate([grad_key[1:, :halo_len], next_last_k[None]], axis=0)
    next_v = jnp.concatenate([grad_value[1:, :halo_len], next_last_v[None]], axis=0)
    own_k = jnp.concatenate(
        [grad_key[:, halo_len : halo_len + rest_len], grad_key[:, halo_len + rest_len :] + next_k],
        axis=1,
    ).reshape(group_rows, HD)
    own_v = jnp.concatenate(
        [
            grad_value[:, halo_len : halo_len + rest_len],
            grad_value[:, halo_len + rest_len :] + next_v,
        ],
        axis=1,
    ).reshape(group_rows, HD)
    all_results = jnp.concatenate(results, axis=1).reshape(group_rows, HD)
    all_query_grads = jnp.concatenate(query_grads, axis=1).reshape(group_rows, HD)
    outputs, query_grad = (
        lax.all_to_all(all_results, "head", split_axis=0, concat_axis=1, tiled=True),
        lax.all_to_all(all_query_grads, "head", split_axis=0, concat_axis=1, tiled=True),
    )
    wide_gk, wide_gv = (
        lax.all_to_all(own_k, "head", split_axis=0, concat_axis=1, tiled=True),
        lax.all_to_all(own_v, "head", split_axis=0, concat_axis=1, tiled=True),
    )
    group_total = wide_gk.shape[1] // (GROUP * HD)
    key_grad = (
        wide_gk.reshape(tok_count, group_total, GROUP, HD)
        .sum(axis=2)
        .reshape(tok_count, group_total * HD)
        .astype(jnp.bfloat16)
    )
    value_grad = (
        wide_gv.reshape(tok_count, group_total, GROUP, HD)
        .sum(axis=2)
        .reshape(tok_count, group_total * HD)
        .astype(jnp.bfloat16)
    )
    return (outputs, query_grad, key_grad, value_grad)


ROWS_BY_ROWS = (((1,), (1,)), ((), ()))
COLS_BY_COLS = (((0,), (0,)), ((), ()))
PLAIN = (((1,), (0,)), ((), ()))


def dot(left, right, dims):
    return lax.dot_general(left, right, dims, preferred_element_type=jnp.float32)


def head_cols(head):
    return slice(head * HD, (head + 1) * HD)


def own_kernel(
    span, halo, doc_ref, q_far, g_far, k_far, v_far,
    q_ref, g_ref, k_ref, v_ref, exp_ref, gw_ref, stat_ref, mask_ref, sems,
):
    pairs = ((k_far, k_ref), (q_far, q_ref), (v_far, v_ref), (g_far, g_ref))
    copies = [
        pltpu.make_async_copy(far, near, sems.at[at]) for at, (far, near) in enumerate(pairs)
    ]
    for copy in copies:
        copy.start()
    device = lax.axis_index("seq") * lax.axis_size("head") + lax.axis_index("head")
    start = doc_ref[device]
    before = doc_ref[jnp.maximum(device - 1, 0)]
    key_pos = lax.broadcasted_iota(jnp.int32, (span, span), 0)
    row_pos = lax.broadcasted_iota(jnp.int32, (span, span), 1)
    allowed = (key_pos <= row_pos) & ((key_pos >= start) | (start > row_pos))
    halo_pos = lax.broadcasted_iota(jnp.int32, (halo, span), 0) - halo
    halo_row = lax.broadcasted_iota(jnp.int32, (halo, span), 1)
    first = jnp.where(device > 0, before - span, span)
    halo_ok = ((halo_pos >= start) | (start > halo_row)) & (halo_pos >= first)
    mask_ref[...] = jnp.where(halo_ok, 0.0, masked_fill)
    for copy in copies:
        copy.wait()
    keys = k_ref[...]
    values = v_ref[...]
    for head in range(GROUP):
        scores = dot(keys, q_ref[:, head_cols(head)], ROWS_BY_ROWS) * LOG2_SCALE
        scores = jnp.where(allowed, scores, masked_fill)
        top = jnp.max(scores, axis=0, keepdims=True)
        weights = jnp.exp2(scores - top)
        grad_weights = dot(values, g_ref[:, head_cols(head)], ROWS_BY_ROWS)
        exp_ref[head * span : (head + 1) * span] = weights
        gw_ref[head * span : (head + 1) * span] = grad_weights
        stat_ref[head : head + 1] = top
        stat_ref[GROUP + head : GROUP + head + 1] = jnp.sum(weights, axis=0, keepdims=True)
        stat_ref[2 * GROUP + head : 2 * GROUP + head + 1] = jnp.sum(
            weights * grad_weights, axis=0, keepdims=True
        )


def halo_kernel(halo, mask_ref, edge_ref, q_ref, g_ref, stat_ref, p_ref, ds_ref, row_ref, back_ref):
    keys = edge_ref[:, :HD]
    values = edge_ref[:, HD:]
    mask = mask_ref[...]
    grad_key = jnp.zeros((halo, HD), jnp.float32)
    grad_value = jnp.zeros((halo, HD), jnp.float32)
    for head in range(GROUP):
        queries = q_ref[:, head_cols(head)]
        grads = g_ref[:, head_cols(head)]
        scores = dot(keys, queries, ROWS_BY_ROWS) * LOG2_SCALE + mask
        grad_weights = dot(values, grads, ROWS_BY_ROWS)
        own_top = stat_ref[head : head + 1]
        top = jnp.maximum(jnp.max(scores, axis=0, keepdims=True), own_top)
        weights = jnp.exp2(scores - top)
        shift = jnp.exp2(own_top - top)
        total = stat_ref[GROUP + head : GROUP + head + 1] * shift + jnp.sum(weights, axis=0, keepdims=True)
        inner = stat_ref[2 * GROUP + head : 2 * GROUP + head + 1] * shift + jnp.sum(
            weights * grad_weights, axis=0, keepdims=True
        )
        delta = inner / total
        p = weights / total
        p_low = p.astype(jnp.bfloat16)
        ds_low = (p * (grad_weights - delta) * SCALE).astype(jnp.bfloat16)
        grad_key += dot(ds_low, queries, PLAIN)
        grad_value += dot(p_low, grads, PLAIN)
        p_ref[head * halo : (head + 1) * halo] = p_low
        ds_ref[head * halo : (head + 1) * halo] = ds_low
        row_ref[head : head + 1] = shift / total
        row_ref[GROUP + head : GROUP + head + 1] = delta
    back_ref[:, :HD] = grad_key.astype(back_ref.dtype)
    back_ref[:, HD:] = grad_value.astype(back_ref.dtype)


def rest_kernel(
    span, halo, q_ref, g_ref, k_ref, v_ref, edge_ref, exp_ref, gw_ref, p_ref, ds_ref, row_ref,
    out_ref, dq_ref, dk_ref, dv_ref, tail_ref,
):
    keys = k_ref[...]
    values = v_ref[...]
    edge_keys = edge_ref[:, :HD]
    edge_values = edge_ref[:, HD:]
    grad_key = jnp.zeros((span, HD), jnp.float32)
    grad_value = jnp.zeros((span, HD), jnp.float32)
    for head in range(GROUP):
        queries = q_ref[:, head_cols(head)]
        grads = g_ref[:, head_cols(head)]
        p = exp_ref[head * span : (head + 1) * span] * row_ref[head : head + 1]
        p_low = p.astype(jnp.bfloat16)
        inner = gw_ref[head * span : (head + 1) * span] - row_ref[GROUP + head : GROUP + head + 1]
        ds_low = (p * inner * SCALE).astype(jnp.bfloat16)
        p_edge = p_ref[head * halo : (head + 1) * halo]
        ds_edge = ds_ref[head * halo : (head + 1) * halo]
        out = dot(p_low, values, COLS_BY_COLS) + dot(p_edge, edge_values, COLS_BY_COLS)
        out_ref[:, head_cols(head)] = out.astype(jnp.bfloat16)
        dq = dot(ds_low, keys, COLS_BY_COLS) + dot(ds_edge, edge_keys, COLS_BY_COLS)
        dq_ref[:, head_cols(head)] = dq.astype(jnp.bfloat16)
        grad_key += dot(ds_low, queries, PLAIN)
        grad_value += dot(p_low, grads, PLAIN)
    dk_ref[...] = grad_key.astype(jnp.bfloat16)
    dv_ref[...] = grad_value.astype(jnp.bfloat16)
    tail_ref[:, :HD] = grad_key[span - halo :]
    tail_ref[:, HD:] = grad_value[span - halo :]


def tail_kernel(span, halo, tail_ref, back_ref, dk_in, dv_in, dk_ref, dv_ref, sum_ref, sems):
    del dk_in, dv_in
    total = tail_ref[...] + back_ref[...].astype(jnp.float32)
    sum_ref[0] = total[:, :HD].astype(jnp.bfloat16)
    sum_ref[1] = total[:, HD:].astype(jnp.bfloat16)
    copies = [
        pltpu.make_async_copy(sum_ref.at[at], ref.at[pl.ds(span - halo, halo)], sems.at[at])
        for at, ref in enumerate((dk_ref, dv_ref))
    ]
    for copy in copies:
        copy.start()
    for copy in copies:
        copy.wait()


def passed_on(value, steps):
    count = lax.axis_size("seq") * lax.axis_size("head")
    ring = [(source, (source + steps) % count) for source in range(count)]
    return lax.ppermute(value, ("seq", "head"), ring)


def span_on_device(queries, key_rows, value_rows, out_grad, doc_start):
    span = queries.shape[0]
    halo = span // 4
    vmem = pl.BlockSpec(memory_space=pltpu.VMEM)
    smem = pl.BlockSpec(memory_space=pltpu.SMEM)
    hbm = pl.BlockSpec(memory_space=pltpu.HBM)
    f32, bf16 = (jnp.float32, jnp.bfloat16)
    near = lambda value: pltpu.with_memory_space_constraint(value, pltpu.VMEM)
    far = lambda value: pltpu.with_memory_space_constraint(value, pltpu.HBM)
    params = pltpu.CompilerParams(vmem_limit_bytes=VMEM_GRANT)
    edge = passed_on(
        jnp.concatenate([key_rows[span - halo :], value_rows[span - halo :]], axis=1), 1
    )
    near_q, near_g, near_k, near_v, exp_own, gw_own, stats, mask = pl.pallas_call(
        lambda *refs: own_kernel(span, halo, *refs),
        in_specs=[smem, hbm, hbm, hbm, hbm],
        out_specs=[vmem] * 8,
        out_shape=[
            pltpu.VMEM(queries.shape, bf16),
            pltpu.VMEM(queries.shape, bf16),
            pltpu.VMEM(key_rows.shape, bf16),
            pltpu.VMEM(key_rows.shape, bf16),
            pltpu.VMEM((GROUP * span, span), f32),
            pltpu.VMEM((GROUP * span, span), f32),
            pltpu.VMEM((4 * GROUP, span), f32),
            pltpu.VMEM((halo, span), f32),
        ],
        scratch_shapes=[pltpu.SemaphoreType.DMA((4,))],
        compiler_params=params,
        name="own_scores",
    )(doc_start, *[far(x) for x in (queries, out_grad, key_rows, value_rows)])
    near_q, near_g, near_k, near_v = [near(x) for x in (near_q, near_g, near_k, near_v)]
    p_edge, ds_edge, rows, back = pl.pallas_call(
        lambda *refs: halo_kernel(halo, *refs),
        in_specs=[vmem] * 5,
        out_specs=[vmem] * 4,
        out_shape=[
            pltpu.VMEM((GROUP * halo, span), bf16),
            pltpu.VMEM((GROUP * halo, span), bf16),
            pltpu.VMEM((2 * GROUP, span), f32),
            pltpu.VMEM((halo, 2 * HD), f32),
        ],
        compiler_params=params,
        name="halo_grads",
    )(near(mask), near(edge), near_q, near_g, near(stats))
    returned = passed_on(back, -1)
    outputs, query_grad, key_grad, value_grad, tail = pl.pallas_call(
        lambda *refs: rest_kernel(span, halo, *refs),
        in_specs=[vmem] * 10,
        out_specs=[vmem] * 5,
        out_shape=[
            jax.ShapeDtypeStruct(queries.shape, bf16),
            jax.ShapeDtypeStruct(queries.shape, bf16),
            jax.ShapeDtypeStruct(key_rows.shape, bf16),
            jax.ShapeDtypeStruct(key_rows.shape, bf16),
            pltpu.VMEM((halo, 2 * HD), f32),
        ],
        compiler_params=params,
        name="own_grads",
    )(near_q, near_g, near_k, near_v, *[near(x) for x in (edge, exp_own, gw_own, p_edge, ds_edge, rows)])
    key_grad, value_grad = pl.pallas_call(
        lambda *refs: tail_kernel(span, halo, *refs),
        in_specs=[vmem, vmem, hbm, hbm],
        out_specs=[hbm, hbm],
        out_shape=[
            jax.ShapeDtypeStruct(key_rows.shape, bf16),
            jax.ShapeDtypeStruct(key_rows.shape, bf16),
        ],
        scratch_shapes=[pltpu.VMEM((2, halo, HD), bf16), pltpu.SemaphoreType.DMA((2,))],
        input_output_aliases={2: 0, 3: 1},
        compiler_params=params,
        name="tail_grads",
    )(near(tail), near(returned), key_grad, value_grad)
    return (outputs, query_grad, key_grad, value_grad)


def per_device(queries, key_rows, value_rows, out_grad, doc_start):
    span = queries.shape[0] * lax.axis_size("head") // SPANS_DEV
    whole_span = span == queries.shape[0] and key_rows.shape[1] == HD and queries.shape[1] == GROUP * HD
    plan = span_on_device if whole_span else spans_over_devices
    return plan(queries, key_rows, value_rows, out_grad, doc_start)


def solution(mesh):
    placed = (
        P(("seq", "head"), None),
        P(("seq", "head"), None),
        P(("seq", "head"), None),
        P(("seq", "head"), None),
        P(),
    )
    return jax.shard_map(
        per_device,
        mesh=mesh,
        in_specs=placed,
        out_specs=(
            P(("seq", "head"), None),
            P(("seq", "head"), None),
            P(("seq", "head"), None),
            P(("seq", "head"), None),
        ),
        check_vma=False,
    )
```

```python
import math

import jax
import jax.numpy as jnp
from jax import lax
from jax.experimental import pallas as pl
from jax.experimental.pallas import tpu as pltpu
from jax.sharding import PartitionSpec as P

HD = 128
GROUP = 4
SPANS_DEV = 4
SCALE = 1.0 / math.sqrt(HD)
LOG2_SCALE = SCALE * math.log2(math.e)
VMEM_GRANT = 16 * 1024 * 1024


masked_fill = -1e30


def passed_along(value, axis, steps):
    count = lax.axis_size(axis)
    first, last = (max(0, -steps), min(count, count - steps))
    return lax.ppermute(value, axis, [(source, source + steps) for source in range(first, last)])


def allowed_mask(
    first_row, row_count, key_count, halo_len, span_len, span_start, prev_begin, span_index
):
    row_pos = first_row + lax.broadcasted_iota(jnp.int32, (row_count, key_count), 0)
    col_pos = lax.broadcasted_iota(jnp.int32, (row_count, key_count), 1) - halo_len
    return (
        (col_pos <= row_pos)
        & ((col_pos >= span_start) | (span_start > row_pos))
        & (col_pos >= prev_begin - span_len)
        & ((col_pos >= 0) | (span_index > 0))
    )


def attend(query_rows, grad_rows, key_block, value_block, allowed, head_dim):
    score_scale = 1.0 / math.sqrt(head_dim)
    contract = (((2,), (2,)), ((0,), (0,)))
    forward = (((2,), (1,)), ((0,), (0,)))
    backward = (((1,), (1,)), ((0,), (0,)))
    scores = (
        lax.dot_general(query_rows, key_block, contract, preferred_element_type=jnp.float32)
        * score_scale
    )
    masked = jnp.where(allowed, scores, masked_fill)
    row_max = jnp.max(masked, axis=2, keepdims=True)
    exp_scores = jnp.where(allowed, jnp.exp(masked - row_max), 0.0)
    weights = exp_scores / jnp.sum(exp_scores, axis=2, keepdims=True)
    weights_low = weights.astype(jnp.bfloat16)
    result = lax.dot_general(
        weights_low, value_block, forward, preferred_element_type=jnp.float32
    ).astype(jnp.bfloat16)
    grad_weights = lax.dot_general(
        grad_rows, value_block, contract, preferred_element_type=jnp.float32
    )
    row_delta = jnp.sum(weights * grad_weights, axis=2, keepdims=True)
    grad_scores = (weights * (grad_weights - row_delta) * score_scale).astype(jnp.bfloat16)
    grad_query = lax.dot_general(
        grad_scores, key_block, forward, preferred_element_type=jnp.float32
    )
    grad_key = lax.dot_general(
        grad_scores, query_rows, backward, preferred_element_type=jnp.float32
    )
    grad_value = lax.dot_general(
        weights_low, grad_rows, backward, preferred_element_type=jnp.float32
    )
    return (result, grad_query, grad_key, grad_value)


def spans_over_devices(queries, key_rows, value_rows, out_grad, doc_start):
    tok_count = queries.shape[0]
    head_count = lax.axis_size("head")
    group_rows = tok_count * head_count
    span_len = group_rows // SPANS_DEV
    halo_len = span_len // 4
    half_len = span_len // 2
    rest_len = span_len - halo_len
    head_q, head_grad = (
        lax.all_to_all(queries, "head", split_axis=1, concat_axis=0, tiled=True),
        lax.all_to_all(out_grad, "head", split_axis=1, concat_axis=0, tiled=True),
    )
    full_k, full_v = (
        lax.all_gather(key_rows, "head", axis=0, tiled=True),
        lax.all_gather(value_rows, "head", axis=0, tiled=True),
    )
    column = lax.axis_index("head") // GROUP * HD
    head_k = lax.dynamic_slice_in_dim(full_k, column, HD, 1)
    head_v = lax.dynamic_slice_in_dim(full_v, column, HD, 1)
    query_3 = head_q.reshape(SPANS_DEV, span_len, HD)
    grad_3 = head_grad.reshape(SPANS_DEV, span_len, HD)
    keys_3 = head_k.reshape(SPANS_DEV, span_len, HD)
    values_3 = head_v.reshape(SPANS_DEV, span_len, HD)
    tail_k = keys_3[:, rest_len:]
    tail_v = values_3[:, rest_len:]
    edge_last_k, edge_last_v = passed_along(
        (tail_k[SPANS_DEV - 1], tail_v[SPANS_DEV - 1]), "seq", 1
    )
    edge_k = jnp.concatenate([edge_last_k[None], tail_k[: SPANS_DEV - 1]], axis=0)
    edge_v = jnp.concatenate([edge_last_v[None], tail_v[: SPANS_DEV - 1]], axis=0)
    key_block = jnp.concatenate([edge_k, keys_3], axis=1)
    value_block = jnp.concatenate([edge_v, values_3], axis=1)
    first_span = lax.axis_index("seq") * SPANS_DEV
    span_starts = lax.dynamic_slice_in_dim(doc_start, first_span, SPANS_DEV)
    before_start = lax.dynamic_slice_in_dim(doc_start, jnp.maximum(first_span - 1, 0), 1)
    prev_starts = jnp.concatenate([before_start, span_starts[: SPANS_DEV - 1]], axis=0)
    span_ids = first_span + jnp.arange(SPANS_DEV, dtype=jnp.int32)
    span_starts = span_starts.reshape(SPANS_DEV, 1, 1)
    prev_starts = prev_starts.reshape(SPANS_DEV, 1, 1)
    span_ids = span_ids.reshape(SPANS_DEV, 1, 1)
    grad_key = jnp.zeros((SPANS_DEV, halo_len + span_len, HD), jnp.float32)
    grad_value = jnp.zeros((SPANS_DEV, halo_len + span_len, HD), jnp.float32)
    results = []
    query_grads = []
    for block_index in range(2):
        first_row = block_index * half_len
        key_count = halo_len + first_row + half_len
        allowed = allowed_mask(
            first_row, half_len, key_count, halo_len, span_len, span_starts, prev_starts, span_ids
        )
        result, grad_query, part_key, part_value = attend(
            query_3[:, first_row : first_row + half_len],
            grad_3[:, first_row : first_row + half_len],
            key_block[:, :key_count],
            value_block[:, :key_count],
            allowed,
            HD,
        )
        results.append(result)
        query_grads.append(grad_query.astype(jnp.bfloat16))
        grad_key = grad_key.at[:, :key_count].add(part_key)
        grad_value = grad_value.at[:, :key_count].add(part_value)
    next_last_k, next_last_v = passed_along(
        (grad_key[0, :halo_len], grad_value[0, :halo_len]), "seq", -1
    )
    next_k = jnp.concatenate([grad_key[1:, :halo_len], next_last_k[None]], axis=0)
    next_v = jnp.concatenate([grad_value[1:, :halo_len], next_last_v[None]], axis=0)
    own_k = jnp.concatenate(
        [grad_key[:, halo_len : halo_len + rest_len], grad_key[:, halo_len + rest_len :] + next_k],
        axis=1,
    ).reshape(group_rows, HD)
    own_v = jnp.concatenate(
        [
            grad_value[:, halo_len : halo_len + rest_len],
            grad_value[:, halo_len + rest_len :] + next_v,
        ],
        axis=1,
    ).reshape(group_rows, HD)
    all_results = jnp.concatenate(results, axis=1).reshape(group_rows, HD)
    all_query_grads = jnp.concatenate(query_grads, axis=1).reshape(group_rows, HD)
    outputs, query_grad = (
        lax.all_to_all(all_results, "head", split_axis=0, concat_axis=1, tiled=True),
        lax.all_to_all(all_query_grads, "head", split_axis=0, concat_axis=1, tiled=True),
    )
    wide_gk, wide_gv = (
        lax.all_to_all(own_k, "head", split_axis=0, concat_axis=1, tiled=True),
        lax.all_to_all(own_v, "head", split_axis=0, concat_axis=1, tiled=True),
    )
    group_total = wide_gk.shape[1] // (GROUP * HD)
    key_grad = (
        wide_gk.reshape(tok_count, group_total, GROUP, HD)
        .sum(axis=2)
        .reshape(tok_count, group_total * HD)
        .astype(jnp.bfloat16)
    )
    value_grad = (
        wide_gv.reshape(tok_count, group_total, GROUP, HD)
        .sum(axis=2)
        .reshape(tok_count, group_total * HD)
        .astype(jnp.bfloat16)
    )
    return (outputs, query_grad, key_grad, value_grad)


ROWS_BY_ROWS = (((1,), (1,)), ((), ()))
COLS_BY_COLS = (((0,), (0,)), ((), ()))
PLAIN = (((1,), (0,)), ((), ()))


def dot(left, right, dims):
    return lax.dot_general(left, right, dims, preferred_element_type=jnp.float32)


def head_cols(head):
    return slice(head * HD, (head + 1) * HD)


def device_index():
    return lax.axis_index("seq") * lax.axis_size("head") + lax.axis_index("head")


def start_all(pairs, sems):
    copies = [pltpu.make_async_copy(source, target, sems.at[at]) for at, (source, target) in enumerate(pairs)]
    for copy in copies:
        copy.start()
    return copies


def own_kernel(
    span, halo, doc_far, q_far, g_far, k_far, v_far,
    q_ref, g_ref, k_ref, v_ref, exp_ref, gw_ref, stat_ref, mask_ref, tail_ref, out_far, dq_far, dk_far, dv_far,
    doc_ref, row_ref, out_ref, dq_ref, dk_ref, dv_ref, in_sems, sems,
):
    copies = start_all(
        ((k_far, k_ref), (q_far, q_ref), (doc_far, doc_ref), (v_far, v_ref), (g_far, g_ref)), in_sems
    )
    for copy in copies:
        copy.wait()
    device = device_index()
    start = doc_ref[device]
    first = jnp.where(device > 0, doc_ref[jnp.maximum(device - 1, 0)] - span, span)
    half = span // 2
    key_pos = lax.broadcasted_iota(jnp.int32, (half, span), 0)
    row_pos = lax.broadcasted_iota(jnp.int32, (half, span), 1)
    allowed_low = (key_pos <= row_pos) & ((key_pos >= start) | (start > row_pos))
    key_high = lax.broadcasted_iota(jnp.int32, (half, half), 0)
    row_high = lax.broadcasted_iota(jnp.int32, (half, half), 1)
    start_high = start - half
    allowed_high = (key_high <= row_high) & ((key_high >= start_high) | (start_high > row_high))
    halo_pos = lax.broadcasted_iota(jnp.int32, (halo, span), 0) - halo
    halo_row = lax.broadcasted_iota(jnp.int32, (halo, span), 1)
    halo_ok = ((halo_pos >= start) | (start > halo_row)) & (halo_pos >= first)
    mask_ref[...] = jnp.where(halo_ok, 0.0, masked_fill)
    fill_low = jnp.where(allowed_low, 0.0, masked_fill)
    fill_high = jnp.where(allowed_high, 0.0, masked_fill)
    keys_low, keys_high = (k_ref[:half], k_ref[half:])
    values_low, values_high = (v_ref[:half], v_ref[half:])
    nothing = jnp.zeros((half, half), jnp.float32)
    for head in range(GROUP):
        at = head * span
        queries = q_ref[:, head_cols(head)]
        grads = g_ref[:, head_cols(head)]
        low = dot(keys_low, queries, ROWS_BY_ROWS) * LOG2_SCALE + fill_low
        high = dot(keys_high, queries[half:], ROWS_BY_ROWS) * LOG2_SCALE + fill_high
        gw_low = dot(values_low, grads, ROWS_BY_ROWS)
        gw_high = dot(values_high, grads[half:], ROWS_BY_ROWS)
        top_low = jnp.max(low, axis=0, keepdims=True)
        top_high = jnp.maximum(top_low[:, half:], jnp.max(high, axis=0, keepdims=True))
        top = jnp.concatenate([top_low[:, :half], top_high], axis=1)
        low = jnp.exp2(low - top)
        high = jnp.exp2(high - top_high)
        total = jnp.sum(low, axis=0, keepdims=True)
        inner = jnp.sum(low * gw_low, axis=0, keepdims=True)
        total_high = total[:, half:] + jnp.sum(high, axis=0, keepdims=True)
        inner_high = inner[:, half:] + jnp.sum(high * gw_high, axis=0, keepdims=True)
        exp_ref[at : at + half] = low
        gw_ref[at : at + half] = gw_low
        exp_ref[at + half : at + span, half:] = high
        gw_ref[at + half : at + span, half:] = gw_high
        exp_ref[at + half : at + span, :half] = nothing
        gw_ref[at + half : at + span, :half] = nothing
        stat_ref[head : head + 1] = top
        stat_ref[GROUP + head : GROUP + head + 1] = jnp.concatenate([total[:, :half], total_high], axis=1)
        stat_ref[2 * GROUP + head : 2 * GROUP + head + 1] = jnp.concatenate([inner[:, :half], inner_high], axis=1)

    @pl.when(device == 0)
    def _():
        share = 1.0 / stat_ref[GROUP : 2 * GROUP]
        row_ref[:GROUP] = share
        row_ref[GROUP:] = stat_ref[2 * GROUP : 3 * GROUP] * share
        finish(
            span, halo, q_ref, g_ref, k_ref, v_ref, exp_ref, gw_ref, row_ref, None,
            (out_ref, dq_ref, dk_ref, dv_ref, tail_ref), (out_far, dq_far, dk_far, dv_far), sems,
        )


def halo_kernel(halo, mask_ref, edge_ref, q_ref, g_ref, stat_ref, p_ref, ds_ref, row_ref, back_ref):
    first = device_index() == 0

    @pl.when(first)
    def _():
        back_ref[...] = jnp.zeros_like(back_ref)

    @pl.when(jnp.logical_not(first))
    def _():
        keys = edge_ref[:, :HD]
        values = edge_ref[:, HD:]
        mask = mask_ref[...]
        grad_key = jnp.zeros((halo, HD), jnp.float32)
        grad_value = jnp.zeros((halo, HD), jnp.float32)
        for head in range(GROUP):
            queries = q_ref[:, head_cols(head)]
            grads = g_ref[:, head_cols(head)]
            scores = dot(keys, queries, ROWS_BY_ROWS) * LOG2_SCALE + mask
            grad_weights = dot(values, grads, ROWS_BY_ROWS)
            own_top = stat_ref[head : head + 1]
            top = jnp.maximum(jnp.max(scores, axis=0, keepdims=True), own_top)
            weights = jnp.exp2(scores - top)
            shift = jnp.exp2(own_top - top)
            total = stat_ref[GROUP + head : GROUP + head + 1] * shift + jnp.sum(weights, axis=0, keepdims=True)
            inner = stat_ref[2 * GROUP + head : 2 * GROUP + head + 1] * shift + jnp.sum(
                weights * grad_weights, axis=0, keepdims=True
            )
            share = 1.0 / total
            delta = inner * share
            p = weights * share
            p_low = p.astype(jnp.bfloat16)
            ds_low = (p * (grad_weights - delta) * SCALE).astype(jnp.bfloat16)
            grad_key += dot(ds_low, queries, PLAIN)
            grad_value += dot(p_low, grads, PLAIN)
            p_ref[head * halo : (head + 1) * halo] = p_low
            ds_ref[head * halo : (head + 1) * halo] = ds_low
            row_ref[head : head + 1] = shift * share
            row_ref[GROUP + head : GROUP + head + 1] = delta
        back_ref[:, :HD] = grad_key.astype(back_ref.dtype)
        back_ref[:, HD:] = grad_value.astype(back_ref.dtype)


def finish(span, halo, q_ref, g_ref, k_ref, v_ref, exp_ref, gw_ref, row_ref, edge, near, far, sems):
    out_ref, dq_ref, dk_ref, dv_ref, tail_ref = near
    keys = k_ref[...]
    values = v_ref[...]
    grad_key = jnp.zeros((span, HD), jnp.float32)
    grad_value = jnp.zeros((span, HD), jnp.float32)
    for head in range(GROUP):
        queries = q_ref[:, head_cols(head)]
        grads = g_ref[:, head_cols(head)]
        p = exp_ref[head * span : (head + 1) * span] * row_ref[head : head + 1]
        p_low = p.astype(jnp.bfloat16)
        inner = gw_ref[head * span : (head + 1) * span] - row_ref[GROUP + head : GROUP + head + 1]
        ds_low = (p * inner * SCALE).astype(jnp.bfloat16)
        out = dot(p_low, values, COLS_BY_COLS)
        dq = dot(ds_low, keys, COLS_BY_COLS)
        if edge is not None:
            edge_ref, p_ref, ds_ref = edge
            out += dot(p_ref[head * halo : (head + 1) * halo], edge_ref[:, HD:], COLS_BY_COLS)
            dq += dot(ds_ref[head * halo : (head + 1) * halo], edge_ref[:, :HD], COLS_BY_COLS)
        out_ref[:, head_cols(head)] = out.astype(jnp.bfloat16)
        dq_ref[:, head_cols(head)] = dq.astype(jnp.bfloat16)
        grad_key += dot(ds_low, queries, PLAIN)
        grad_value += dot(p_low, grads, PLAIN)
    dk_ref[...] = grad_key.astype(jnp.bfloat16)
    dv_ref[...] = grad_value.astype(jnp.bfloat16)
    tail_ref[:, :HD] = grad_key[span - halo :]
    tail_ref[:, HD:] = grad_value[span - halo :]
    for copy in start_all(zip(near[:4], far), sems):
        copy.wait()


def rest_kernel(
    span, halo, q_ref, g_ref, k_ref, v_ref, edge_ref, exp_ref, gw_ref, p_ref, ds_ref, stat_ref,
    out_in, dq_in, dk_in, dv_in, tail_in, out_far, dq_far, dk_far, dv_far, tail_ref,
    out_ref, dq_ref, dk_ref, dv_ref, sems,
):
    del out_in, dq_in, dk_in, dv_in, tail_in

    @pl.when(device_index() > 0)
    def _():
        finish(
            span, halo, q_ref, g_ref, k_ref, v_ref, exp_ref, gw_ref, stat_ref, (edge_ref, p_ref, ds_ref),
            (out_ref, dq_ref, dk_ref, dv_ref, tail_ref), (out_far, dq_far, dk_far, dv_far), sems,
        )


def tail_kernel(span, halo, tail_ref, back_ref, dk_in, dv_in, dk_far, dv_far, dk_ref, dv_ref, sems):
    del dk_in, dv_in
    total = tail_ref[...] + back_ref[...].astype(jnp.float32)
    dk_ref[...] = total[:, :HD].astype(jnp.bfloat16)
    dv_ref[...] = total[:, HD:].astype(jnp.bfloat16)
    last = pl.ds(span - halo, halo)
    for copy in start_all(((dk_ref, dk_far.at[last]), (dv_ref, dv_far.at[last])), sems):
        copy.wait()


def passed_on(value, steps):
    count = lax.axis_size("seq") * lax.axis_size("head")
    ring = [(source, (source + steps) % count) for source in range(count)]
    return lax.ppermute(value, ("seq", "head"), ring)


def span_on_device(queries, key_rows, value_rows, out_grad, doc_start):
    span = queries.shape[0]
    halo = span // 4
    wide, slim = (queries.shape, key_rows.shape)
    f32, bf16 = (jnp.float32, jnp.bfloat16)
    vmem = pl.BlockSpec(memory_space=pltpu.VMEM)
    hbm = pl.BlockSpec(memory_space=pltpu.HBM)
    near = lambda *values: [pltpu.with_memory_space_constraint(value, pltpu.VMEM) for value in values]
    far = lambda *values: [pltpu.with_memory_space_constraint(value, pltpu.HBM) for value in values]
    params = pltpu.CompilerParams(vmem_limit_bytes=VMEM_GRANT)
    results = [pltpu.VMEM(shape, bf16) for shape in (wide, wide, slim, slim)]
    results_far = [pltpu.HBM(shape, bf16) for shape in (wide, wide, slim, slim)]

    edge = passed_on(
        jnp.concatenate([key_rows[span - halo :], value_rows[span - halo :]], axis=1), 1
    )
    own = pl.pallas_call(
        lambda *refs: own_kernel(span, halo, *refs),
        in_specs=[hbm] * 5,
        out_specs=[vmem] * 9 + [hbm] * 4,
        out_shape=results
        + [
            pltpu.VMEM((GROUP * span, span), f32),
            pltpu.VMEM((GROUP * span, span), f32),
            pltpu.VMEM((4 * GROUP, span), f32),
            pltpu.VMEM((halo, span), f32),
            pltpu.VMEM((halo, 2 * HD), f32),
        ]
        + results_far,
        scratch_shapes=[pltpu.SMEM(doc_start.shape, jnp.int32), pltpu.VMEM((2 * GROUP, span), f32)]
        + results
        + [pltpu.SemaphoreType.DMA((5,)), pltpu.SemaphoreType.DMA((4,))],
        compiler_params=params,
        name="own_scores",
    )(*far(doc_start, queries, out_grad, key_rows, value_rows))
    inputs = near(*own[:4])
    exp_own, gw_own, stats, mask, tail, outputs, query_grad, key_grad, value_grad = own[4:]
    p_edge, ds_edge, rows, back = pl.pallas_call(
        lambda *refs: halo_kernel(halo, *refs),
        in_specs=[vmem] * 5,
        out_specs=[vmem] * 4,
        out_shape=[
            pltpu.VMEM((GROUP * halo, span), bf16),
            pltpu.VMEM((GROUP * halo, span), bf16),
            pltpu.VMEM((2 * GROUP, span), f32),
            pltpu.VMEM((halo, 2 * HD), bf16),
        ],
        compiler_params=params,
        name="halo_grads",
    )(*near(mask, edge), *inputs[:2], *near(stats))
    returned = passed_on(back, -1)
    outputs, query_grad, key_grad, value_grad, tail = pl.pallas_call(
        lambda *refs: rest_kernel(span, halo, *refs),
        in_specs=[vmem] * 10 + [hbm] * 4 + [vmem],
        out_specs=[hbm] * 4 + [vmem],
        out_shape=results_far + [pltpu.VMEM((halo, 2 * HD), f32)],
        scratch_shapes=results + [pltpu.SemaphoreType.DMA((4,))],
        input_output_aliases={10: 0, 11: 1, 12: 2, 13: 3, 14: 4},
        compiler_params=params,
        name="own_grads",
    )(
        *inputs,
        *near(edge, exp_own, gw_own, p_edge, ds_edge, rows),
        *far(outputs, query_grad, key_grad, value_grad),
        *near(tail),
    )
    key_grad, value_grad = pl.pallas_call(
        lambda *refs: tail_kernel(span, halo, *refs),
        in_specs=[vmem, vmem, hbm, hbm],
        out_specs=[hbm, hbm],
        out_shape=results_far[2:],
        scratch_shapes=[pltpu.VMEM((halo, HD), bf16)] * 2 + [pltpu.SemaphoreType.DMA((2,))],
        input_output_aliases={2: 0, 3: 1},
        compiler_params=params,
        name="tail_grads",
    )(*near(tail, returned), *far(key_grad, value_grad))
    return (outputs, query_grad, key_grad, value_grad)


def per_device(queries, key_rows, value_rows, out_grad, doc_start):
    span = queries.shape[0] * lax.axis_size("head") // SPANS_DEV
    whole_span = span == queries.shape[0] and key_rows.shape[1] == HD and queries.shape[1] == GROUP * HD
    plan = span_on_device if whole_span else spans_over_devices
    return plan(queries, key_rows, value_rows, out_grad, doc_start)


def solution(mesh):
    placed = (
        P(("seq", "head"), None),
        P(("seq", "head"), None),
        P(("seq", "head"), None),
        P(("seq", "head"), None),
        P(),
    )
    return jax.shard_map(
        per_device,
        mesh=mesh,
        in_specs=placed,
        out_specs=(
            P(("seq", "head"), None),
            P(("seq", "head"), None),
            P(("seq", "head"), None),
            P(("seq", "head"), None),
        ),
        check_vma=False,
    )
```

```python
import math

import jax
import jax.numpy as jnp
from jax import lax
from jax.experimental import pallas as pl
from jax.experimental.pallas import tpu as pltpu
from jax.sharding import PartitionSpec as P

HD = 128
GROUP = 4
SPANS_DEV = 4
SCALE = 1.0 / math.sqrt(HD)
LOG2_SCALE = SCALE * math.log2(math.e)
VMEM_GRANT = 16 * 1024 * 1024
CUTS = 2


masked_fill = -1e30


def passed_along(value, axis, steps):
    count = lax.axis_size(axis)
    first, last = (max(0, -steps), min(count, count - steps))
    return lax.ppermute(value, axis, [(source, source + steps) for source in range(first, last)])


def allowed_mask(
    first_row, row_count, key_count, halo_len, span_len, span_start, prev_begin, span_index
):
    row_pos = first_row + lax.broadcasted_iota(jnp.int32, (row_count, key_count), 0)
    col_pos = lax.broadcasted_iota(jnp.int32, (row_count, key_count), 1) - halo_len
    return (
        (col_pos <= row_pos)
        & ((col_pos >= span_start) | (span_start > row_pos))
        & (col_pos >= prev_begin - span_len)
        & ((col_pos >= 0) | (span_index > 0))
    )


def attend(query_rows, grad_rows, key_block, value_block, allowed, head_dim):
    score_scale = 1.0 / math.sqrt(head_dim)
    contract = (((2,), (2,)), ((0,), (0,)))
    forward = (((2,), (1,)), ((0,), (0,)))
    backward = (((1,), (1,)), ((0,), (0,)))
    scores = (
        lax.dot_general(query_rows, key_block, contract, preferred_element_type=jnp.float32)
        * score_scale
    )
    masked = jnp.where(allowed, scores, masked_fill)
    row_max = jnp.max(masked, axis=2, keepdims=True)
    exp_scores = jnp.where(allowed, jnp.exp(masked - row_max), 0.0)
    weights = exp_scores / jnp.sum(exp_scores, axis=2, keepdims=True)
    weights_low = weights.astype(jnp.bfloat16)
    result = lax.dot_general(
        weights_low, value_block, forward, preferred_element_type=jnp.float32
    ).astype(jnp.bfloat16)
    grad_weights = lax.dot_general(
        grad_rows, value_block, contract, preferred_element_type=jnp.float32
    )
    row_delta = jnp.sum(weights * grad_weights, axis=2, keepdims=True)
    grad_scores = (weights * (grad_weights - row_delta) * score_scale).astype(jnp.bfloat16)
    grad_query = lax.dot_general(
        grad_scores, key_block, forward, preferred_element_type=jnp.float32
    )
    grad_key = lax.dot_general(
        grad_scores, query_rows, backward, preferred_element_type=jnp.float32
    )
    grad_value = lax.dot_general(
        weights_low, grad_rows, backward, preferred_element_type=jnp.float32
    )
    return (result, grad_query, grad_key, grad_value)


def spans_over_devices(queries, key_rows, value_rows, out_grad, doc_start):
    tok_count = queries.shape[0]
    head_count = lax.axis_size("head")
    group_rows = tok_count * head_count
    span_len = group_rows // SPANS_DEV
    halo_len = span_len // 4
    half_len = span_len // 2
    rest_len = span_len - halo_len
    head_q, head_grad = (
        lax.all_to_all(queries, "head", split_axis=1, concat_axis=0, tiled=True),
        lax.all_to_all(out_grad, "head", split_axis=1, concat_axis=0, tiled=True),
    )
    full_k, full_v = (
        lax.all_gather(key_rows, "head", axis=0, tiled=True),
        lax.all_gather(value_rows, "head", axis=0, tiled=True),
    )
    column = lax.axis_index("head") // GROUP * HD
    head_k = lax.dynamic_slice_in_dim(full_k, column, HD, 1)
    head_v = lax.dynamic_slice_in_dim(full_v, column, HD, 1)
    query_3 = head_q.reshape(SPANS_DEV, span_len, HD)
    grad_3 = head_grad.reshape(SPANS_DEV, span_len, HD)
    keys_3 = head_k.reshape(SPANS_DEV, span_len, HD)
    values_3 = head_v.reshape(SPANS_DEV, span_len, HD)
    tail_k = keys_3[:, rest_len:]
    tail_v = values_3[:, rest_len:]
    edge_last_k, edge_last_v = passed_along(
        (tail_k[SPANS_DEV - 1], tail_v[SPANS_DEV - 1]), "seq", 1
    )
    edge_k = jnp.concatenate([edge_last_k[None], tail_k[: SPANS_DEV - 1]], axis=0)
    edge_v = jnp.concatenate([edge_last_v[None], tail_v[: SPANS_DEV - 1]], axis=0)
    key_block = jnp.concatenate([edge_k, keys_3], axis=1)
    value_block = jnp.concatenate([edge_v, values_3], axis=1)
    first_span = lax.axis_index("seq") * SPANS_DEV
    span_starts = lax.dynamic_slice_in_dim(doc_start, first_span, SPANS_DEV)
    before_start = lax.dynamic_slice_in_dim(doc_start, jnp.maximum(first_span - 1, 0), 1)
    prev_starts = jnp.concatenate([before_start, span_starts[: SPANS_DEV - 1]], axis=0)
    span_ids = first_span + jnp.arange(SPANS_DEV, dtype=jnp.int32)
    span_starts = span_starts.reshape(SPANS_DEV, 1, 1)
    prev_starts = prev_starts.reshape(SPANS_DEV, 1, 1)
    span_ids = span_ids.reshape(SPANS_DEV, 1, 1)
    grad_key = jnp.zeros((SPANS_DEV, halo_len + span_len, HD), jnp.float32)
    grad_value = jnp.zeros((SPANS_DEV, halo_len + span_len, HD), jnp.float32)
    results = []
    query_grads = []
    for block_index in range(2):
        first_row = block_index * half_len
        key_count = halo_len + first_row + half_len
        allowed = allowed_mask(
            first_row, half_len, key_count, halo_len, span_len, span_starts, prev_starts, span_ids
        )
        result, grad_query, part_key, part_value = attend(
            query_3[:, first_row : first_row + half_len],
            grad_3[:, first_row : first_row + half_len],
            key_block[:, :key_count],
            value_block[:, :key_count],
            allowed,
            HD,
        )
        results.append(result)
        query_grads.append(grad_query.astype(jnp.bfloat16))
        grad_key = grad_key.at[:, :key_count].add(part_key)
        grad_value = grad_value.at[:, :key_count].add(part_value)
    next_last_k, next_last_v = passed_along(
        (grad_key[0, :halo_len], grad_value[0, :halo_len]), "seq", -1
    )
    next_k = jnp.concatenate([grad_key[1:, :halo_len], next_last_k[None]], axis=0)
    next_v = jnp.concatenate([grad_value[1:, :halo_len], next_last_v[None]], axis=0)
    own_k = jnp.concatenate(
        [grad_key[:, halo_len : halo_len + rest_len], grad_key[:, halo_len + rest_len :] + next_k],
        axis=1,
    ).reshape(group_rows, HD)
    own_v = jnp.concatenate(
        [
            grad_value[:, halo_len : halo_len + rest_len],
            grad_value[:, halo_len + rest_len :] + next_v,
        ],
        axis=1,
    ).reshape(group_rows, HD)
    all_results = jnp.concatenate(results, axis=1).reshape(group_rows, HD)
    all_query_grads = jnp.concatenate(query_grads, axis=1).reshape(group_rows, HD)
    outputs, query_grad = (
        lax.all_to_all(all_results, "head", split_axis=0, concat_axis=1, tiled=True),
        lax.all_to_all(all_query_grads, "head", split_axis=0, concat_axis=1, tiled=True),
    )
    wide_gk, wide_gv = (
        lax.all_to_all(own_k, "head", split_axis=0, concat_axis=1, tiled=True),
        lax.all_to_all(own_v, "head", split_axis=0, concat_axis=1, tiled=True),
    )
    group_total = wide_gk.shape[1] // (GROUP * HD)
    key_grad = (
        wide_gk.reshape(tok_count, group_total, GROUP, HD)
        .sum(axis=2)
        .reshape(tok_count, group_total * HD)
        .astype(jnp.bfloat16)
    )
    value_grad = (
        wide_gv.reshape(tok_count, group_total, GROUP, HD)
        .sum(axis=2)
        .reshape(tok_count, group_total * HD)
        .astype(jnp.bfloat16)
    )
    return (outputs, query_grad, key_grad, value_grad)


ROWS_BY_ROWS = (((1,), (1,)), ((), ()))
COLS_BY_COLS = (((0,), (0,)), ((), ()))
PLAIN = (((1,), (0,)), ((), ()))


def dot(left, right, dims):
    return lax.dot_general(left, right, dims, preferred_element_type=jnp.float32)


def head_cols(head):
    return slice(head * HD, (head + 1) * HD)


def device_index():
    return lax.axis_index("seq") * lax.axis_size("head") + lax.axis_index("head")


def start_all(pairs, sems):
    copies = [pltpu.make_async_copy(source, target, sems.at[at]) for at, (source, target) in enumerate(pairs)]
    for copy in copies:
        copy.start()
    return copies


def pack_kernel(span, halo, doc_far, k_far, v_far, edge_ref, info_ref, doc_ref, sems):
    last = pl.ds(span - halo, halo)
    copies = start_all(
        (
            (k_far.at[last], edge_ref.at[:, :HD]),
            (v_far.at[last], edge_ref.at[:, HD:]),
            (doc_far, doc_ref),
        ),
        sems,
    )
    for copy in copies:
        copy.wait()
    device = device_index()
    before = doc_ref[jnp.maximum(device - 1, 0)]
    row = lax.broadcasted_iota(jnp.int32, info_ref.shape, 0)
    first = jnp.where(device > 0, before - span, span)
    info_ref[...] = jnp.where(row == 0, doc_ref[device], first)


def own_kernel(
    span, halo, info_ref, q_ref, g_ref, k_ref, v_ref, exp_ref, gw_ref, stat_ref, mask_ref, tail_ref, out_far, dq_far, dk_far, dv_far,
    row_ref, out_ref, dq_ref, dk_ref, dv_ref, sems,
):
    half = span // 2
    start = info_ref[0:1]
    key_pos = lax.broadcasted_iota(jnp.int32, (half, span), 0)
    row_pos = lax.broadcasted_iota(jnp.int32, (half, span), 1)
    allowed_low = (key_pos <= row_pos) & ((key_pos >= start) | (start > row_pos))
    key_high = lax.broadcasted_iota(jnp.int32, (half, half), 0)
    row_high = lax.broadcasted_iota(jnp.int32, (half, half), 1)
    start_high = start[:, half:] - half
    allowed_high = (key_high <= row_high) & ((key_high >= start_high) | (start_high > row_high))
    halo_pos = lax.broadcasted_iota(jnp.int32, (halo, span), 0) - halo
    halo_row = lax.broadcasted_iota(jnp.int32, (halo, span), 1)
    halo_ok = ((halo_pos >= start) | (start > halo_row)) & (halo_pos >= info_ref[1:2])
    mask_ref[...] = jnp.where(halo_ok, 0.0, masked_fill)
    fill_low = jnp.where(allowed_low, 0.0, masked_fill)
    fill_high = jnp.where(allowed_high, 0.0, masked_fill)
    keys_low, keys_high = (k_ref[:half], k_ref[half:])
    values_low, values_high = (v_ref[:half], v_ref[half:])
    nothing = jnp.zeros((half, half), jnp.float32)
    for head in range(GROUP):
        at = head * span
        queries = q_ref[:, head_cols(head)]
        grads = g_ref[:, head_cols(head)]
        low = dot(keys_low, queries, ROWS_BY_ROWS) * LOG2_SCALE + fill_low
        high = dot(keys_high, queries[half:], ROWS_BY_ROWS) * LOG2_SCALE + fill_high
        gw_low = dot(values_low, grads, ROWS_BY_ROWS)
        gw_high = dot(values_high, grads[half:], ROWS_BY_ROWS)
        top_low = jnp.max(low, axis=0, keepdims=True)
        top_high = jnp.maximum(top_low[:, half:], jnp.max(high, axis=0, keepdims=True))
        top = jnp.concatenate([top_low[:, :half], top_high], axis=1)
        low = jnp.exp2(low - top)
        high = jnp.exp2(high - top_high)
        total = jnp.sum(low, axis=0, keepdims=True)
        inner = jnp.sum(low * gw_low, axis=0, keepdims=True)
        total_high = total[:, half:] + jnp.sum(high, axis=0, keepdims=True)
        inner_high = inner[:, half:] + jnp.sum(high * gw_high, axis=0, keepdims=True)
        exp_ref[at : at + half] = low
        gw_ref[at : at + half] = gw_low
        exp_ref[at + half : at + span, half:] = high
        gw_ref[at + half : at + span, half:] = gw_high
        exp_ref[at + half : at + span, :half] = nothing
        gw_ref[at + half : at + span, :half] = nothing
        stat_ref[head : head + 1] = top
        stat_ref[GROUP + head : GROUP + head + 1] = jnp.concatenate([total[:, :half], total_high], axis=1)
        stat_ref[2 * GROUP + head : 2 * GROUP + head + 1] = jnp.concatenate([inner[:, :half], inner_high], axis=1)

    @pl.when(device_index() == 0)
    def _():
        share = 1.0 / stat_ref[GROUP : 2 * GROUP]
        row_ref[:GROUP] = share
        row_ref[GROUP:] = stat_ref[2 * GROUP : 3 * GROUP] * share
        finish(
            span, halo, q_ref, g_ref, k_ref, v_ref, exp_ref, gw_ref, row_ref, None,
            (out_ref, dq_ref, dk_ref, dv_ref, tail_ref), (out_far, dq_far, dk_far, dv_far), sems,
        )


def halo_kernel(halo, mask_ref, edge_ref, q_ref, g_ref, stat_ref, p_ref, ds_ref, row_ref, back_ref):
    first = device_index() == 0

    @pl.when(first)
    def _():
        back_ref[...] = jnp.zeros_like(back_ref)

    @pl.when(jnp.logical_not(first))
    def _():
        keys = edge_ref[:, :HD]
        values = edge_ref[:, HD:]
        mask = mask_ref[...]
        grad_key = jnp.zeros((halo, HD), jnp.float32)
        grad_value = jnp.zeros((halo, HD), jnp.float32)
        for head in range(GROUP):
            queries = q_ref[:, head_cols(head)]
            grads = g_ref[:, head_cols(head)]
            scores = dot(keys, queries, ROWS_BY_ROWS) * LOG2_SCALE + mask
            grad_weights = dot(values, grads, ROWS_BY_ROWS)
            own_top = stat_ref[head : head + 1]
            top = jnp.maximum(jnp.max(scores, axis=0, keepdims=True), own_top)
            weights = jnp.exp2(scores - top)
            shift = jnp.exp2(own_top - top)
            total = stat_ref[GROUP + head : GROUP + head + 1] * shift + jnp.sum(weights, axis=0, keepdims=True)
            inner = stat_ref[2 * GROUP + head : 2 * GROUP + head + 1] * shift + jnp.sum(
                weights * grad_weights, axis=0, keepdims=True
            )
            share = 1.0 / total
            delta = inner * share
            p = weights * share
            p_low = p.astype(jnp.bfloat16)
            ds_low = (p * (grad_weights - delta) * SCALE).astype(jnp.bfloat16)
            grad_key += dot(ds_low, queries, PLAIN)
            grad_value += dot(p_low, grads, PLAIN)
            p_ref[head * halo : (head + 1) * halo] = p_low
            ds_ref[head * halo : (head + 1) * halo] = ds_low
            row_ref[head : head + 1] = shift * share
            row_ref[GROUP + head : GROUP + head + 1] = delta
        back_ref[:, :HD] = grad_key.astype(back_ref.dtype)
        back_ref[:, HD:] = grad_value.astype(back_ref.dtype)


def finish(span, halo, q_ref, g_ref, k_ref, v_ref, exp_ref, gw_ref, row_ref, edge, near, far, sems):
    out_ref, dq_ref, dk_ref, dv_ref, tail_ref = near
    keys = k_ref[...]
    values = v_ref[...]
    grad_key = jnp.zeros((span, HD), jnp.float32)
    grad_value = jnp.zeros((span, HD), jnp.float32)
    for head in range(GROUP):
        queries = q_ref[:, head_cols(head)]
        grads = g_ref[:, head_cols(head)]
        p = exp_ref[head * span : (head + 1) * span] * row_ref[head : head + 1]
        p_low = p.astype(jnp.bfloat16)
        inner = gw_ref[head * span : (head + 1) * span] - row_ref[GROUP + head : GROUP + head + 1]
        ds_low = (p * inner * SCALE).astype(jnp.bfloat16)
        out = dot(p_low, values, COLS_BY_COLS)
        dq = dot(ds_low, keys, COLS_BY_COLS)
        if edge is not None:
            edge_ref, p_ref, ds_ref = edge
            out += dot(p_ref[head * halo : (head + 1) * halo], edge_ref[:, HD:], COLS_BY_COLS)
            dq += dot(ds_ref[head * halo : (head + 1) * halo], edge_ref[:, :HD], COLS_BY_COLS)
        out_ref[:, head_cols(head)] = out.astype(jnp.bfloat16)
        dq_ref[:, head_cols(head)] = dq.astype(jnp.bfloat16)
        grad_key += dot(ds_low, queries, PLAIN)
        grad_value += dot(p_low, grads, PLAIN)
    dk_ref[...] = grad_key.astype(jnp.bfloat16)
    dv_ref[...] = grad_value.astype(jnp.bfloat16)
    tail_ref[:, :HD] = grad_key[span - halo :]
    tail_ref[:, HD:] = grad_value[span - halo :]
    for copy in start_all(zip(near[:4], far), sems):
        copy.wait()


def rest_kernel(
    span, halo, q_ref, g_ref, k_ref, v_ref, edge_ref, exp_ref, gw_ref, p_ref, ds_ref, stat_ref,
    out_in, dq_in, dk_in, dv_in, tail_in, out_far, dq_far, dk_far, dv_far, tail_ref,
    out_ref, dq_ref, dk_ref, dv_ref, sems,
):
    del out_in, dq_in, dk_in, dv_in, tail_in

    @pl.when(device_index() > 0)
    def _():
        finish(
            span, halo, q_ref, g_ref, k_ref, v_ref, exp_ref, gw_ref, stat_ref, (edge_ref, p_ref, ds_ref),
            (out_ref, dq_ref, dk_ref, dv_ref, tail_ref), (out_far, dq_far, dk_far, dv_far), sems,
        )


def tail_kernel(span, halo, tail_ref, back_ref, dk_in, dv_in, dk_far, dv_far, dk_ref, dv_ref, sems):
    del dk_in, dv_in
    total = tail_ref[...] + back_ref[...].astype(jnp.float32)
    dk_ref[...] = total[:, :HD].astype(jnp.bfloat16)
    dv_ref[...] = total[:, HD:].astype(jnp.bfloat16)
    last = pl.ds(span - halo, halo)
    for copy in start_all(((dk_ref, dk_far.at[last]), (dv_ref, dv_far.at[last])), sems):
        copy.wait()


def passed_on(value, steps):
    count = lax.axis_size("seq") * lax.axis_size("head")
    ring = [(source, (source + steps) % count) for source in range(count)]
    return lax.ppermute(value, ("seq", "head"), ring)


def span_on_device(queries, key_rows, value_rows, out_grad, doc_start):
    span = queries.shape[0]
    halo = span // 4
    wide, slim = (queries.shape, key_rows.shape)
    f32, bf16 = (jnp.float32, jnp.bfloat16)
    vmem = pl.BlockSpec(memory_space=pltpu.VMEM)
    hbm = pl.BlockSpec(memory_space=pltpu.HBM)
    near = lambda *values: [pltpu.with_memory_space_constraint(value, pltpu.VMEM) for value in values]
    far = lambda *values: [pltpu.with_memory_space_constraint(value, pltpu.HBM) for value in values]
    params = pltpu.CompilerParams(vmem_limit_bytes=VMEM_GRANT)
    results = [pltpu.VMEM(shape, bf16) for shape in (wide, wide, slim, slim)]
    results_far = [pltpu.HBM(shape, bf16) for shape in (wide, wide, slim, slim)]

    last_rows, info = pl.pallas_call(
        lambda *refs: pack_kernel(span, halo, *refs),
        in_specs=[hbm] * 3,
        out_specs=[vmem] * 2,
        out_shape=[pltpu.VMEM((halo, 2 * HD), bf16), pltpu.VMEM((8, span), jnp.int32)],
        scratch_shapes=[pltpu.SMEM(doc_start.shape, jnp.int32), pltpu.SemaphoreType.DMA((3,))],
        compiler_params=params,
        cost_estimate=pl.CostEstimate(flops=4000000000, bytes_accessed=4 * 1024 * 1024, transcendentals=0),
        name="pack",
    )(*far(doc_start, key_rows, value_rows))
    edge = passed_on(last_rows, 1)
    own = pl.pallas_call(
        lambda *refs: own_kernel(span, halo, *refs),
        in_specs=[vmem] * 5,
        out_specs=[vmem] * 5 + [hbm] * 4,
        out_shape=[
            pltpu.VMEM((GROUP * span, span), f32),
            pltpu.VMEM((GROUP * span, span), f32),
            pltpu.VMEM((4 * GROUP, span), f32),
            pltpu.VMEM((halo, span), f32),
            pltpu.VMEM((halo, 2 * HD), f32),
        ]
        + results_far,
        scratch_shapes=[pltpu.VMEM((2 * GROUP, span), f32)]
        + results
        + [pltpu.SemaphoreType.DMA((4,))],
        compiler_params=params,
        name="own_scores",
    )(*near(info), queries, out_grad, key_rows, value_rows)
    inputs = (queries, out_grad, key_rows, value_rows)
    exp_own, gw_own, stats, mask, tail, outputs, query_grad, key_grad, value_grad = own
    p_edge, ds_edge, rows, back = pl.pallas_call(
        lambda *refs: halo_kernel(halo, *refs),
        in_specs=[vmem] * 5,
        out_specs=[vmem] * 4,
        out_shape=[
            pltpu.VMEM((GROUP * halo, span), bf16),
            pltpu.VMEM((GROUP * halo, span), bf16),
            pltpu.VMEM((2 * GROUP, span), f32),
            pltpu.VMEM((halo, 2 * HD), bf16),
        ],
        compiler_params=params,
        name="halo_grads",
    )(*near(mask, edge), *inputs[:2], *near(stats))
    returned = passed_on(back, -1)
    outputs, query_grad, key_grad, value_grad, tail = pl.pallas_call(
        lambda *refs: rest_kernel(span, halo, *refs),
        in_specs=[vmem] * 10 + [hbm] * 4 + [vmem],
        out_specs=[hbm] * 4 + [vmem],
        out_shape=results_far + [pltpu.VMEM((halo, 2 * HD), f32)],
        scratch_shapes=results + [pltpu.SemaphoreType.DMA((4,))],
        input_output_aliases={10: 0, 11: 1, 12: 2, 13: 3, 14: 4},
        compiler_params=params,
        name="own_grads",
    )(
        *inputs,
        *near(edge, exp_own, gw_own, p_edge, ds_edge, rows),
        *far(outputs, query_grad, key_grad, value_grad),
        *near(tail),
    )
    key_grad, value_grad = pl.pallas_call(
        lambda *refs: tail_kernel(span, halo, *refs),
        in_specs=[vmem, vmem, hbm, hbm],
        out_specs=[hbm, hbm],
        out_shape=results_far[2:],
        scratch_shapes=[pltpu.VMEM((halo, HD), bf16)] * 2 + [pltpu.SemaphoreType.DMA((2,))],
        input_output_aliases={2: 0, 3: 1},
        compiler_params=params,
        name="tail_grads",
    )(*near(tail, returned), *far(key_grad, value_grad))
    return (outputs, query_grad, key_grad, value_grad)


def per_device(queries, key_rows, value_rows, out_grad, doc_start):
    span = queries.shape[0] * lax.axis_size("head") // SPANS_DEV
    whole_span = span == queries.shape[0] and key_rows.shape[1] == HD and queries.shape[1] == GROUP * HD
    plan = span_on_device if whole_span else spans_over_devices
    return plan(queries, key_rows, value_rows, out_grad, doc_start)


def solution(mesh):
    placed = (
        P(("seq", "head"), None),
        P(("seq", "head"), None),
        P(("seq", "head"), None),
        P(("seq", "head"), None),
        P(),
    )
    return jax.shard_map(
        per_device,
        mesh=mesh,
        in_specs=placed,
        out_specs=(
            P(("seq", "head"), None),
            P(("seq", "head"), None),
            P(("seq", "head"), None),
            P(("seq", "head"), None),
        ),
        check_vma=False,
    )
```

```python
import math

import jax
import jax.numpy as jnp
from jax import lax
from jax.experimental import pallas as pl
from jax.experimental.pallas import tpu as pltpu
from jax.sharding import PartitionSpec as P

HD = 128
GROUP = 4
SPANS_DEV = 4
SCALE = 1.0 / math.sqrt(HD)
LOG2_SCALE = SCALE * math.log2(math.e)
VMEM_GRANT = 16 * 1024 * 1024


masked_fill = -1e30


def passed_along(value, axis, steps):
    count = lax.axis_size(axis)
    first, last = (max(0, -steps), min(count, count - steps))
    return lax.ppermute(value, axis, [(source, source + steps) for source in range(first, last)])


def allowed_mask(
    first_row, row_count, key_count, halo_len, span_len, span_start, prev_begin, span_index
):
    row_pos = first_row + lax.broadcasted_iota(jnp.int32, (row_count, key_count), 0)
    col_pos = lax.broadcasted_iota(jnp.int32, (row_count, key_count), 1) - halo_len
    return (
        (col_pos <= row_pos)
        & ((col_pos >= span_start) | (span_start > row_pos))
        & (col_pos >= prev_begin - span_len)
        & ((col_pos >= 0) | (span_index > 0))
    )


def attend(query_rows, grad_rows, key_block, value_block, allowed, head_dim):
    score_scale = 1.0 / math.sqrt(head_dim)
    contract = (((2,), (2,)), ((0,), (0,)))
    forward = (((2,), (1,)), ((0,), (0,)))
    backward = (((1,), (1,)), ((0,), (0,)))
    scores = (
        lax.dot_general(query_rows, key_block, contract, preferred_element_type=jnp.float32)
        * score_scale
    )
    masked = jnp.where(allowed, scores, masked_fill)
    row_max = jnp.max(masked, axis=2, keepdims=True)
    exp_scores = jnp.where(allowed, jnp.exp(masked - row_max), 0.0)
    weights = exp_scores / jnp.sum(exp_scores, axis=2, keepdims=True)
    weights_low = weights.astype(jnp.bfloat16)
    result = lax.dot_general(
        weights_low, value_block, forward, preferred_element_type=jnp.float32
    ).astype(jnp.bfloat16)
    grad_weights = lax.dot_general(
        grad_rows, value_block, contract, preferred_element_type=jnp.float32
    )
    row_delta = jnp.sum(weights * grad_weights, axis=2, keepdims=True)
    grad_scores = (weights * (grad_weights - row_delta) * score_scale).astype(jnp.bfloat16)
    grad_query = lax.dot_general(
        grad_scores, key_block, forward, preferred_element_type=jnp.float32
    )
    grad_key = lax.dot_general(
        grad_scores, query_rows, backward, preferred_element_type=jnp.float32
    )
    grad_value = lax.dot_general(
        weights_low, grad_rows, backward, preferred_element_type=jnp.float32
    )
    return (result, grad_query, grad_key, grad_value)


def spans_over_devices(queries, key_rows, value_rows, out_grad, doc_start):
    tok_count = queries.shape[0]
    head_count = lax.axis_size("head")
    group_rows = tok_count * head_count
    span_len = group_rows // SPANS_DEV
    halo_len = span_len // 4
    half_len = span_len // 2
    rest_len = span_len - halo_len
    head_q, head_grad = (
        lax.all_to_all(queries, "head", split_axis=1, concat_axis=0, tiled=True),
        lax.all_to_all(out_grad, "head", split_axis=1, concat_axis=0, tiled=True),
    )
    full_k, full_v = (
        lax.all_gather(key_rows, "head", axis=0, tiled=True),
        lax.all_gather(value_rows, "head", axis=0, tiled=True),
    )
    column = lax.axis_index("head") // GROUP * HD
    head_k = lax.dynamic_slice_in_dim(full_k, column, HD, 1)
    head_v = lax.dynamic_slice_in_dim(full_v, column, HD, 1)
    query_3 = head_q.reshape(SPANS_DEV, span_len, HD)
    grad_3 = head_grad.reshape(SPANS_DEV, span_len, HD)
    keys_3 = head_k.reshape(SPANS_DEV, span_len, HD)
    values_3 = head_v.reshape(SPANS_DEV, span_len, HD)
    tail_k = keys_3[:, rest_len:]
    tail_v = values_3[:, rest_len:]
    edge_last_k, edge_last_v = passed_along(
        (tail_k[SPANS_DEV - 1], tail_v[SPANS_DEV - 1]), "seq", 1
    )
    edge_k = jnp.concatenate([edge_last_k[None], tail_k[: SPANS_DEV - 1]], axis=0)
    edge_v = jnp.concatenate([edge_last_v[None], tail_v[: SPANS_DEV - 1]], axis=0)
    key_block = jnp.concatenate([edge_k, keys_3], axis=1)
    value_block = jnp.concatenate([edge_v, values_3], axis=1)
    first_span = lax.axis_index("seq") * SPANS_DEV
    span_starts = lax.dynamic_slice_in_dim(doc_start, first_span, SPANS_DEV)
    before_start = lax.dynamic_slice_in_dim(doc_start, jnp.maximum(first_span - 1, 0), 1)
    prev_starts = jnp.concatenate([before_start, span_starts[: SPANS_DEV - 1]], axis=0)
    span_ids = first_span + jnp.arange(SPANS_DEV, dtype=jnp.int32)
    span_starts = span_starts.reshape(SPANS_DEV, 1, 1)
    prev_starts = prev_starts.reshape(SPANS_DEV, 1, 1)
    span_ids = span_ids.reshape(SPANS_DEV, 1, 1)
    grad_key = jnp.zeros((SPANS_DEV, halo_len + span_len, HD), jnp.float32)
    grad_value = jnp.zeros((SPANS_DEV, halo_len + span_len, HD), jnp.float32)
    results = []
    query_grads = []
    for block_index in range(2):
        first_row = block_index * half_len
        key_count = halo_len + first_row + half_len
        allowed = allowed_mask(
            first_row, half_len, key_count, halo_len, span_len, span_starts, prev_starts, span_ids
        )
        result, grad_query, part_key, part_value = attend(
            query_3[:, first_row : first_row + half_len],
            grad_3[:, first_row : first_row + half_len],
            key_block[:, :key_count],
            value_block[:, :key_count],
            allowed,
            HD,
        )
        results.append(result)
        query_grads.append(grad_query.astype(jnp.bfloat16))
        grad_key = grad_key.at[:, :key_count].add(part_key)
        grad_value = grad_value.at[:, :key_count].add(part_value)
    next_last_k, next_last_v = passed_along(
        (grad_key[0, :halo_len], grad_value[0, :halo_len]), "seq", -1
    )
    next_k = jnp.concatenate([grad_key[1:, :halo_len], next_last_k[None]], axis=0)
    next_v = jnp.concatenate([grad_value[1:, :halo_len], next_last_v[None]], axis=0)
    own_k = jnp.concatenate(
        [grad_key[:, halo_len : halo_len + rest_len], grad_key[:, halo_len + rest_len :] + next_k],
        axis=1,
    ).reshape(group_rows, HD)
    own_v = jnp.concatenate(
        [
            grad_value[:, halo_len : halo_len + rest_len],
            grad_value[:, halo_len + rest_len :] + next_v,
        ],
        axis=1,
    ).reshape(group_rows, HD)
    all_results = jnp.concatenate(results, axis=1).reshape(group_rows, HD)
    all_query_grads = jnp.concatenate(query_grads, axis=1).reshape(group_rows, HD)
    outputs, query_grad = (
        lax.all_to_all(all_results, "head", split_axis=0, concat_axis=1, tiled=True),
        lax.all_to_all(all_query_grads, "head", split_axis=0, concat_axis=1, tiled=True),
    )
    wide_gk, wide_gv = (
        lax.all_to_all(own_k, "head", split_axis=0, concat_axis=1, tiled=True),
        lax.all_to_all(own_v, "head", split_axis=0, concat_axis=1, tiled=True),
    )
    group_total = wide_gk.shape[1] // (GROUP * HD)
    key_grad = (
        wide_gk.reshape(tok_count, group_total, GROUP, HD)
        .sum(axis=2)
        .reshape(tok_count, group_total * HD)
        .astype(jnp.bfloat16)
    )
    value_grad = (
        wide_gv.reshape(tok_count, group_total, GROUP, HD)
        .sum(axis=2)
        .reshape(tok_count, group_total * HD)
        .astype(jnp.bfloat16)
    )
    return (outputs, query_grad, key_grad, value_grad)


ROWS_BY_ROWS = (((1,), (1,)), ((), ()))
COLS_BY_COLS = (((0,), (0,)), ((), ()))
PLAIN = (((1,), (0,)), ((), ()))


def dot(left, right, dims):
    return lax.dot_general(left, right, dims, preferred_element_type=jnp.float32)


def head_cols(head):
    return slice(head * HD, (head + 1) * HD)


def device_index():
    return lax.axis_index("seq") * lax.axis_size("head") + lax.axis_index("head")


def start_all(pairs, sems):
    copies = [pltpu.make_async_copy(source, target, sems.at[at]) for at, (source, target) in enumerate(pairs)]
    for copy in copies:
        copy.start()
    return copies


def side_by_side(ref, rows=slice(None)):
    return jnp.concatenate([ref[rows, head_cols(head)] for head in range(GROUP)], axis=0)


def pack_kernel(span, halo, k_far, v_far, edge_ref, sems):
    last = device_index() == lax.axis_size("seq") * lax.axis_size("head") - 1

    @pl.when(last)
    def _():
        edge_ref[...] = jnp.zeros_like(edge_ref)

    @pl.when(jnp.logical_not(last))
    def _():
        tail = pl.ds(span - halo, halo)
        pairs = ((k_far.at[tail], edge_ref.at[:, :HD]), (v_far.at[tail], edge_ref.at[:, HD:]))
        for copy in start_all(pairs, sems):
            copy.wait()


def own_kernel(
    span, halo, doc_far, q_ref, g_ref, k_ref, v_ref,
    low_ref, high_ref, gw_low_ref, gw_high_ref, stat_ref, mask_ref, tail_ref, out_far, dq_far, dk_far, dv_far,
    doc_ref, row_ref, out_ref, dq_ref, dk_ref, dv_ref, doc_sem, sems,
):
    half = span // 2
    doc_copy = pltpu.make_async_copy(doc_far, doc_ref, doc_sem)
    doc_copy.start()
    gw_low = dot(v_ref[:half], side_by_side(g_ref), ROWS_BY_ROWS)
    gw_high = dot(v_ref[half:], side_by_side(g_ref, slice(half, span)), ROWS_BY_ROWS)
    low = dot(k_ref[:half], side_by_side(q_ref), ROWS_BY_ROWS)
    high = dot(k_ref[half:], side_by_side(q_ref, slice(half, span)), ROWS_BY_ROWS)
    doc_copy.wait()
    device = device_index()
    start = doc_ref[device]
    first = jnp.where(device > 0, doc_ref[jnp.maximum(device - 1, 0)] - span, span)
    key_pos = lax.broadcasted_iota(jnp.int32, (half, span), 0)
    row_pos = lax.broadcasted_iota(jnp.int32, (half, span), 1)
    fill_low = jnp.where((key_pos <= row_pos) & ((key_pos >= start) | (start > row_pos)), 0.0, masked_fill)
    key_pos = half + lax.broadcasted_iota(jnp.int32, (half, half), 0)
    row_pos = half + lax.broadcasted_iota(jnp.int32, (half, half), 1)
    fill_high = jnp.where((key_pos <= row_pos) & ((key_pos >= start) | (start > row_pos)), 0.0, masked_fill)
    key_pos = lax.broadcasted_iota(jnp.int32, (halo, span), 0) - halo
    row_pos = lax.broadcasted_iota(jnp.int32, (halo, span), 1)
    halo_ok = ((key_pos >= start) | (start > row_pos)) & (key_pos >= first)
    mask_ref[...] = jnp.where(halo_ok, 0.0, masked_fill)
    for head in range(GROUP):
        wide = slice(head * span, (head + 1) * span)
        slim = slice(head * half, (head + 1) * half)
        part = low[:, wide] * LOG2_SCALE + fill_low
        part_high = high[:, slim] * LOG2_SCALE + fill_high
        top = jnp.max(part, axis=0, keepdims=True)
        top_high = jnp.maximum(top[:, half:], jnp.max(part_high, axis=0, keepdims=True))
        top = jnp.concatenate([top[:, :half], top_high], axis=1)
        part = jnp.exp2(part - top)
        part_high = jnp.exp2(part_high - top_high)
        total = jnp.sum(part, axis=0, keepdims=True)
        inner = jnp.sum(part * gw_low[:, wide], axis=0, keepdims=True)
        total_high = total[:, half:] + jnp.sum(part_high, axis=0, keepdims=True)
        inner_high = inner[:, half:] + jnp.sum(part_high * gw_high[:, slim], axis=0, keepdims=True)
        low_ref[:, wide] = part
        high_ref[:, slim] = part_high
        stat_ref[0:1, wide] = top
        stat_ref[1:2, wide] = jnp.concatenate([total[:, :half], total_high], axis=1)
        stat_ref[2:3, wide] = jnp.concatenate([inner[:, :half], inner_high], axis=1)
    gw_low_ref[...] = gw_low
    gw_high_ref[...] = gw_high

    @pl.when(device == 0)
    def _():
        share = 1.0 / stat_ref[1:2]
        row_ref[0:1] = share
        row_ref[1:2] = stat_ref[2:3] * share
        finish(
            span, halo, q_ref, g_ref, k_ref, v_ref, low_ref, high_ref, gw_low_ref, gw_high_ref, row_ref, None,
            (out_ref, dq_ref, dk_ref, dv_ref, tail_ref), (out_far, dq_far, dk_far, dv_far), sems,
        )


def halo_kernel(span, mask_ref, edge_ref, q_ref, g_ref, stat_ref, p_ref, ds_ref, row_ref, back_ref):
    first = device_index() == 0

    @pl.when(first)
    def _():
        back_ref[...] = jnp.zeros_like(back_ref)

    @pl.when(jnp.logical_not(first))
    def _():
        queries = side_by_side(q_ref)
        grads = side_by_side(g_ref)
        mask = jnp.concatenate([mask_ref[...]] * GROUP, axis=1)
        scores = dot(edge_ref[:, :HD], queries, ROWS_BY_ROWS) * LOG2_SCALE + mask
        grad_weights = dot(edge_ref[:, HD:], grads, ROWS_BY_ROWS)
        own_top = stat_ref[0:1]
        top = jnp.maximum(jnp.max(scores, axis=0, keepdims=True), own_top)
        weights = jnp.exp2(scores - top)
        shift = jnp.exp2(own_top - top)
        total = stat_ref[1:2] * shift + jnp.sum(weights, axis=0, keepdims=True)
        inner = stat_ref[2:3] * shift + jnp.sum(weights * grad_weights, axis=0, keepdims=True)
        share = 1.0 / total
        delta = inner * share
        p = weights * share
        p_low = p.astype(jnp.bfloat16)
        ds_low = (p * (grad_weights - delta) * SCALE).astype(jnp.bfloat16)
        back_ref[:, :HD] = dot(ds_low, queries, PLAIN).astype(back_ref.dtype)
        back_ref[:, HD:] = dot(p_low, grads, PLAIN).astype(back_ref.dtype)
        p_ref[...] = p_low
        ds_ref[...] = ds_low
        row_ref[0:1] = shift * share
        row_ref[1:2] = delta


def finish(
    span, halo, q_ref, g_ref, k_ref, v_ref, low_ref, high_ref, gw_low_ref, gw_high_ref, row_ref, edge, near, far, sems
):
    out_ref, dq_ref, dk_ref, dv_ref, tail_ref = near
    half = span // 2
    nothing = jnp.zeros((half, half), jnp.bfloat16)
    share = row_ref[0:1]
    delta = row_ref[1:2]
    later = lambda row: jnp.concatenate(
        [row[:, head * span + half : (head + 1) * span] for head in range(GROUP)], axis=1
    )
    whole = lambda low, high: jnp.concatenate(
        [
            low,
            jnp.concatenate(
                [piece for head in range(GROUP) for piece in (nothing, high[:, head * half : (head + 1) * half])],
                axis=1,
            ),
        ],
        axis=0,
    )
    low = low_ref[...] * share
    high = high_ref[...] * later(share)
    p = whole(low.astype(jnp.bfloat16), high.astype(jnp.bfloat16))
    ds = whole(
        (low * (gw_low_ref[...] - delta) * SCALE).astype(jnp.bfloat16),
        (high * (gw_high_ref[...] - later(delta)) * SCALE).astype(jnp.bfloat16),
    )
    grad_key = dot(ds, side_by_side(q_ref), PLAIN)
    grad_value = dot(p, side_by_side(g_ref), PLAIN)
    keys = k_ref[...]
    values = v_ref[...]
    if edge is not None:
        edge_ref, p_ref, ds_ref = edge
        keys = jnp.concatenate([edge_ref[:, :HD], keys], axis=0)
        values = jnp.concatenate([edge_ref[:, HD:], values], axis=0)
        p = jnp.concatenate([p_ref[...], p], axis=0)
        ds = jnp.concatenate([ds_ref[...], ds], axis=0)
    out = dot(p, values, COLS_BY_COLS).astype(jnp.bfloat16)
    dq = dot(ds, keys, COLS_BY_COLS).astype(jnp.bfloat16)
    for head in range(GROUP):
        out_ref[:, head_cols(head)] = out[head * span : (head + 1) * span]
        dq_ref[:, head_cols(head)] = dq[head * span : (head + 1) * span]
    dk_ref[...] = grad_key.astype(jnp.bfloat16)
    dv_ref[...] = grad_value.astype(jnp.bfloat16)
    tail_ref[:, :HD] = grad_key[span - halo :]
    tail_ref[:, HD:] = grad_value[span - halo :]
    for copy in start_all(zip(near[:4], far), sems):
        copy.wait()


def rest_kernel(
    span, halo, q_ref, g_ref, k_ref, v_ref, edge_ref, low_ref, high_ref, gw_low_ref, gw_high_ref, p_ref, ds_ref,
    row_ref, out_in, dq_in, dk_in, dv_in, tail_in, out_far, dq_far, dk_far, dv_far, tail_ref,
    out_ref, dq_ref, dk_ref, dv_ref, sems,
):
    del out_in, dq_in, dk_in, dv_in, tail_in

    @pl.when(device_index() > 0)
    def _():
        finish(
            span, halo, q_ref, g_ref, k_ref, v_ref, low_ref, high_ref, gw_low_ref, gw_high_ref, row_ref,
            (edge_ref, p_ref, ds_ref), (out_ref, dq_ref, dk_ref, dv_ref, tail_ref),
            (out_far, dq_far, dk_far, dv_far), sems,
        )


def tail_kernel(span, halo, tail_ref, back_ref, dk_in, dv_in, dk_far, dv_far, dk_ref, dv_ref, sems):
    del dk_in, dv_in
    total = tail_ref[...] + back_ref[...].astype(jnp.float32)
    dk_ref[...] = total[:, :HD].astype(jnp.bfloat16)
    dv_ref[...] = total[:, HD:].astype(jnp.bfloat16)
    last = pl.ds(span - halo, halo)
    for copy in start_all(((dk_ref, dk_far.at[last]), (dv_ref, dv_far.at[last])), sems):
        copy.wait()


def passed_on(value, steps):
    count = lax.axis_size("seq") * lax.axis_size("head")
    ring = [(source, (source + steps) % count) for source in range(count)]
    return lax.ppermute(value, ("seq", "head"), ring)


def span_on_device(queries, key_rows, value_rows, out_grad, doc_start):
    span = queries.shape[0]
    halo = span // 4
    wide, slim = (queries.shape, key_rows.shape)
    f32, bf16 = (jnp.float32, jnp.bfloat16)
    vmem = pl.BlockSpec(memory_space=pltpu.VMEM)
    hbm = pl.BlockSpec(memory_space=pltpu.HBM)
    near = lambda *values: [pltpu.with_memory_space_constraint(value, pltpu.VMEM) for value in values]
    far = lambda *values: [pltpu.with_memory_space_constraint(value, pltpu.HBM) for value in values]
    params = pltpu.CompilerParams(vmem_limit_bytes=VMEM_GRANT)
    results = [pltpu.VMEM(shape, bf16) for shape in (wide, wide, slim, slim)]
    results_far = [pltpu.HBM(shape, bf16) for shape in (wide, wide, slim, slim)]

    last_rows = pl.pallas_call(
        lambda *refs: pack_kernel(span, halo, *refs),
        in_specs=[hbm] * 2,
        out_specs=vmem,
        out_shape=pltpu.VMEM((halo, 2 * HD), bf16),
        scratch_shapes=[pltpu.SemaphoreType.DMA((2,))],
        compiler_params=params,
        cost_estimate=pl.CostEstimate(flops=4000000000, bytes_accessed=4 * 1024 * 1024, transcendentals=0),
        name="pack",
    )(*far(key_rows, value_rows))
    edge = passed_on(last_rows, 1)
    inputs = (queries, out_grad, key_rows, value_rows)
    low, high, gw_low, gw_high, stats, mask, tail, outputs, query_grad, key_grad, value_grad = pl.pallas_call(
        lambda *refs: own_kernel(span, halo, *refs),
        in_specs=[hbm] + [vmem] * 4,
        out_specs=[vmem] * 7 + [hbm] * 4,
        out_shape=[
            pltpu.VMEM((span // 2, GROUP * span), f32),
            pltpu.VMEM((span // 2, GROUP * span // 2), f32),
            pltpu.VMEM((span // 2, GROUP * span), f32),
            pltpu.VMEM((span // 2, GROUP * span // 2), f32),
            pltpu.VMEM((8, GROUP * span), f32),
            pltpu.VMEM((halo, span), f32),
            pltpu.VMEM((halo, 2 * HD), f32),
        ]
        + results_far,
        scratch_shapes=[pltpu.SMEM(doc_start.shape, jnp.int32), pltpu.VMEM((8, GROUP * span), f32)]
        + results
        + [pltpu.SemaphoreType.DMA(()), pltpu.SemaphoreType.DMA((4,))],
        compiler_params=params,
        name="own_scores",
    )(*far(doc_start), *inputs)
    p_edge, ds_edge, rows, back = pl.pallas_call(
        lambda *refs: halo_kernel(span, *refs),
        in_specs=[vmem] * 5,
        out_specs=[vmem] * 4,
        out_shape=[
            pltpu.VMEM((halo, GROUP * span), bf16),
            pltpu.VMEM((halo, GROUP * span), bf16),
            pltpu.VMEM((8, GROUP * span), f32),
            pltpu.VMEM((halo, 2 * HD), bf16),
        ],
        compiler_params=params,
        name="halo_grads",
    )(*near(mask, edge), *inputs[:2], *near(stats))
    returned = passed_on(back, -1)
    outputs, query_grad, key_grad, value_grad, tail = pl.pallas_call(
        lambda *refs: rest_kernel(span, halo, *refs),
        in_specs=[vmem] * 12 + [hbm] * 4 + [vmem],
        out_specs=[hbm] * 4 + [vmem],
        out_shape=results_far + [pltpu.VMEM((halo, 2 * HD), f32)],
        scratch_shapes=results + [pltpu.SemaphoreType.DMA((4,))],
        input_output_aliases={12: 0, 13: 1, 14: 2, 15: 3, 16: 4},
        compiler_params=params,
        name="own_grads",
    )(
        *inputs,
        *near(edge, low, high, gw_low, gw_high, p_edge, ds_edge, rows),
        *far(outputs, query_grad, key_grad, value_grad),
        *near(tail),
    )
    key_grad, value_grad = pl.pallas_call(
        lambda *refs: tail_kernel(span, halo, *refs),
        in_specs=[vmem, vmem, hbm, hbm],
        out_specs=[hbm, hbm],
        out_shape=results_far[2:],
        scratch_shapes=[pltpu.VMEM((halo, HD), bf16)] * 2 + [pltpu.SemaphoreType.DMA((2,))],
        input_output_aliases={2: 0, 3: 1},
        compiler_params=params,
        name="tail_grads",
    )(*near(tail, returned), *far(key_grad, value_grad))
    return (outputs, query_grad, key_grad, value_grad)


def per_device(queries, key_rows, value_rows, out_grad, doc_start):
    span = queries.shape[0] * lax.axis_size("head") // SPANS_DEV
    whole_span = span == queries.shape[0] and key_rows.shape[1] == HD and queries.shape[1] == GROUP * HD
    plan = span_on_device if whole_span else spans_over_devices
    return plan(queries, key_rows, value_rows, out_grad, doc_start)


def solution(mesh):
    placed = (
        P(("seq", "head"), None),
        P(("seq", "head"), None),
        P(("seq", "head"), None),
        P(("seq", "head"), None),
        P(),
    )
    return jax.shard_map(
        per_device,
        mesh=mesh,
        in_specs=placed,
        out_specs=(
            P(("seq", "head"), None),
            P(("seq", "head"), None),
            P(("seq", "head"), None),
            P(("seq", "head"), None),
        ),
        check_vma=False,
    )
```

```python
import math

import jax
import jax.numpy as jnp
from jax import lax
from jax.experimental import pallas as pl
from jax.experimental.pallas import tpu as pltpu
from jax.sharding import PartitionSpec as P

HD = 128
GROUP = 4
SPANS_DEV = 4
SCALE = 1.0 / math.sqrt(HD)
LOG2_SCALE = SCALE * math.log2(math.e)
VMEM_GRANT = 16 * 1024 * 1024


masked_fill = -1e30


def passed_along(value, axis, steps):
    count = lax.axis_size(axis)
    first, last = (max(0, -steps), min(count, count - steps))
    return lax.ppermute(value, axis, [(source, source + steps) for source in range(first, last)])


def allowed_mask(
    first_row, row_count, key_count, halo_len, span_len, span_start, prev_begin, span_index
):
    row_pos = first_row + lax.broadcasted_iota(jnp.int32, (row_count, key_count), 0)
    col_pos = lax.broadcasted_iota(jnp.int32, (row_count, key_count), 1) - halo_len
    return (
        (col_pos <= row_pos)
        & ((col_pos >= span_start) | (span_start > row_pos))
        & (col_pos >= prev_begin - span_len)
        & ((col_pos >= 0) | (span_index > 0))
    )


def attend(query_rows, grad_rows, key_block, value_block, allowed, head_dim):
    score_scale = 1.0 / math.sqrt(head_dim)
    contract = (((2,), (2,)), ((0,), (0,)))
    forward = (((2,), (1,)), ((0,), (0,)))
    backward = (((1,), (1,)), ((0,), (0,)))
    scores = (
        lax.dot_general(query_rows, key_block, contract, preferred_element_type=jnp.float32)
        * score_scale
    )
    masked = jnp.where(allowed, scores, masked_fill)
    row_max = jnp.max(masked, axis=2, keepdims=True)
    exp_scores = jnp.where(allowed, jnp.exp(masked - row_max), 0.0)
    weights = exp_scores / jnp.sum(exp_scores, axis=2, keepdims=True)
    weights_low = weights.astype(jnp.bfloat16)
    result = lax.dot_general(
        weights_low, value_block, forward, preferred_element_type=jnp.float32
    ).astype(jnp.bfloat16)
    grad_weights = lax.dot_general(
        grad_rows, value_block, contract, preferred_element_type=jnp.float32
    )
    row_delta = jnp.sum(weights * grad_weights, axis=2, keepdims=True)
    grad_scores = (weights * (grad_weights - row_delta) * score_scale).astype(jnp.bfloat16)
    grad_query = lax.dot_general(
        grad_scores, key_block, forward, preferred_element_type=jnp.float32
    )
    grad_key = lax.dot_general(
        grad_scores, query_rows, backward, preferred_element_type=jnp.float32
    )
    grad_value = lax.dot_general(
        weights_low, grad_rows, backward, preferred_element_type=jnp.float32
    )
    return (result, grad_query, grad_key, grad_value)


def spans_over_devices(queries, key_rows, value_rows, out_grad, doc_start):
    tok_count = queries.shape[0]
    head_count = lax.axis_size("head")
    group_rows = tok_count * head_count
    span_len = group_rows // SPANS_DEV
    halo_len = span_len // 4
    half_len = span_len // 2
    rest_len = span_len - halo_len
    head_q, head_grad = (
        lax.all_to_all(queries, "head", split_axis=1, concat_axis=0, tiled=True),
        lax.all_to_all(out_grad, "head", split_axis=1, concat_axis=0, tiled=True),
    )
    full_k, full_v = (
        lax.all_gather(key_rows, "head", axis=0, tiled=True),
        lax.all_gather(value_rows, "head", axis=0, tiled=True),
    )
    column = lax.axis_index("head") // GROUP * HD
    head_k = lax.dynamic_slice_in_dim(full_k, column, HD, 1)
    head_v = lax.dynamic_slice_in_dim(full_v, column, HD, 1)
    query_3 = head_q.reshape(SPANS_DEV, span_len, HD)
    grad_3 = head_grad.reshape(SPANS_DEV, span_len, HD)
    keys_3 = head_k.reshape(SPANS_DEV, span_len, HD)
    values_3 = head_v.reshape(SPANS_DEV, span_len, HD)
    tail_k = keys_3[:, rest_len:]
    tail_v = values_3[:, rest_len:]
    edge_last_k, edge_last_v = passed_along(
        (tail_k[SPANS_DEV - 1], tail_v[SPANS_DEV - 1]), "seq", 1
    )
    edge_k = jnp.concatenate([edge_last_k[None], tail_k[: SPANS_DEV - 1]], axis=0)
    edge_v = jnp.concatenate([edge_last_v[None], tail_v[: SPANS_DEV - 1]], axis=0)
    key_block = jnp.concatenate([edge_k, keys_3], axis=1)
    value_block = jnp.concatenate([edge_v, values_3], axis=1)
    first_span = lax.axis_index("seq") * SPANS_DEV
    span_starts = lax.dynamic_slice_in_dim(doc_start, first_span, SPANS_DEV)
    before_start = lax.dynamic_slice_in_dim(doc_start, jnp.maximum(first_span - 1, 0), 1)
    prev_starts = jnp.concatenate([before_start, span_starts[: SPANS_DEV - 1]], axis=0)
    span_ids = first_span + jnp.arange(SPANS_DEV, dtype=jnp.int32)
    span_starts = span_starts.reshape(SPANS_DEV, 1, 1)
    prev_starts = prev_starts.reshape(SPANS_DEV, 1, 1)
    span_ids = span_ids.reshape(SPANS_DEV, 1, 1)
    grad_key = jnp.zeros((SPANS_DEV, halo_len + span_len, HD), jnp.float32)
    grad_value = jnp.zeros((SPANS_DEV, halo_len + span_len, HD), jnp.float32)
    results = []
    query_grads = []
    for block_index in range(2):
        first_row = block_index * half_len
        key_count = halo_len + first_row + half_len
        allowed = allowed_mask(
            first_row, half_len, key_count, halo_len, span_len, span_starts, prev_starts, span_ids
        )
        result, grad_query, part_key, part_value = attend(
            query_3[:, first_row : first_row + half_len],
            grad_3[:, first_row : first_row + half_len],
            key_block[:, :key_count],
            value_block[:, :key_count],
            allowed,
            HD,
        )
        results.append(result)
        query_grads.append(grad_query.astype(jnp.bfloat16))
        grad_key = grad_key.at[:, :key_count].add(part_key)
        grad_value = grad_value.at[:, :key_count].add(part_value)
    next_last_k, next_last_v = passed_along(
        (grad_key[0, :halo_len], grad_value[0, :halo_len]), "seq", -1
    )
    next_k = jnp.concatenate([grad_key[1:, :halo_len], next_last_k[None]], axis=0)
    next_v = jnp.concatenate([grad_value[1:, :halo_len], next_last_v[None]], axis=0)
    own_k = jnp.concatenate(
        [grad_key[:, halo_len : halo_len + rest_len], grad_key[:, halo_len + rest_len :] + next_k],
        axis=1,
    ).reshape(group_rows, HD)
    own_v = jnp.concatenate(
        [
            grad_value[:, halo_len : halo_len + rest_len],
            grad_value[:, halo_len + rest_len :] + next_v,
        ],
        axis=1,
    ).reshape(group_rows, HD)
    all_results = jnp.concatenate(results, axis=1).reshape(group_rows, HD)
    all_query_grads = jnp.concatenate(query_grads, axis=1).reshape(group_rows, HD)
    outputs, query_grad = (
        lax.all_to_all(all_results, "head", split_axis=0, concat_axis=1, tiled=True),
        lax.all_to_all(all_query_grads, "head", split_axis=0, concat_axis=1, tiled=True),
    )
    wide_gk, wide_gv = (
        lax.all_to_all(own_k, "head", split_axis=0, concat_axis=1, tiled=True),
        lax.all_to_all(own_v, "head", split_axis=0, concat_axis=1, tiled=True),
    )
    group_total = wide_gk.shape[1] // (GROUP * HD)
    key_grad = (
        wide_gk.reshape(tok_count, group_total, GROUP, HD)
        .sum(axis=2)
        .reshape(tok_count, group_total * HD)
        .astype(jnp.bfloat16)
    )
    value_grad = (
        wide_gv.reshape(tok_count, group_total, GROUP, HD)
        .sum(axis=2)
        .reshape(tok_count, group_total * HD)
        .astype(jnp.bfloat16)
    )
    return (outputs, query_grad, key_grad, value_grad)


ROWS_BY_ROWS = (((1,), (1,)), ((), ()))
COLS_BY_COLS = (((0,), (0,)), ((), ()))
PLAIN = (((1,), (0,)), ((), ()))


def dot(left, right, dims):
    return lax.dot_general(left, right, dims, preferred_element_type=jnp.float32)


def head_cols(head):
    return slice(head * HD, (head + 1) * HD)


def device_index():
    return lax.axis_index("seq") * lax.axis_size("head") + lax.axis_index("head")


def start_all(pairs, sems):
    copies = [pltpu.make_async_copy(source, target, sems.at[at]) for at, (source, target) in enumerate(pairs)]
    for copy in copies:
        copy.start()
    return copies


def side_by_side(ref, rows=slice(None)):
    return jnp.concatenate([ref[rows, head_cols(head)] for head in range(GROUP)], axis=0)


def pack_kernel(span, halo, k_far, v_far, edge_ref, sems):
    last = device_index() == device_count() - 1

    @pl.when(last)
    def _():
        edge_ref[...] = jnp.zeros_like(edge_ref)

    @pl.when(jnp.logical_not(last))
    def _():
        tail = pl.ds(span - halo, halo)
        pairs = ((k_far.at[tail], edge_ref.at[:, :HD]), (v_far.at[tail], edge_ref.at[:, HD:]))
        for copy in start_all(pairs, sems):
            copy.wait()


def own_kernel(
    span, halo, doc_far, q_ref, g_ref, k_ref, v_ref,
    low_ref, high_ref, gw_low_ref, gw_high_ref, stat_ref, mask_ref, tail_ref, out_far, dq_far, dk_far, dv_far,
    doc_ref, row_ref, out_ref, dq_ref, dk_ref, dv_ref, doc_sem, sems,
):
    half = span // 2
    doc_copy = pltpu.make_async_copy(doc_far, doc_ref, doc_sem)
    doc_copy.start()
    gw_low = dot(v_ref[:half], side_by_side(g_ref), ROWS_BY_ROWS)
    gw_high = dot(v_ref[half:], side_by_side(g_ref, slice(half, span)), ROWS_BY_ROWS)
    low = dot(k_ref[:half], side_by_side(q_ref), ROWS_BY_ROWS)
    high = dot(k_ref[half:], side_by_side(q_ref, slice(half, span)), ROWS_BY_ROWS)
    doc_copy.wait()
    device = device_index()
    start = doc_ref[device]
    first = jnp.where(device > 0, doc_ref[jnp.maximum(device - 1, 0)] - span, span)
    key_pos = lax.broadcasted_iota(jnp.int32, (half, span), 0)
    row_pos = lax.broadcasted_iota(jnp.int32, (half, span), 1)
    fill_low = jnp.where((key_pos <= row_pos) & ((key_pos >= start) | (start > row_pos)), 0.0, masked_fill)
    key_pos = half + lax.broadcasted_iota(jnp.int32, (half, half), 0)
    row_pos = half + lax.broadcasted_iota(jnp.int32, (half, half), 1)
    fill_high = jnp.where((key_pos <= row_pos) & ((key_pos >= start) | (start > row_pos)), 0.0, masked_fill)
    key_pos = lax.broadcasted_iota(jnp.int32, (halo, span), 0) - halo
    row_pos = lax.broadcasted_iota(jnp.int32, (halo, span), 1)
    halo_ok = ((key_pos >= start) | (start > row_pos)) & (key_pos >= first)
    mask_ref[...] = jnp.where(halo_ok, 0.0, masked_fill)
    for head in range(GROUP):
        wide = slice(head * span, (head + 1) * span)
        slim = slice(head * half, (head + 1) * half)
        part = low[:, wide] * LOG2_SCALE + fill_low
        part_high = high[:, slim] * LOG2_SCALE + fill_high
        top = jnp.max(part, axis=0, keepdims=True)
        top_high = jnp.maximum(top[:, half:], jnp.max(part_high, axis=0, keepdims=True))
        top = jnp.concatenate([top[:, :half], top_high], axis=1)
        part = jnp.exp2(part - top)
        part_high = jnp.exp2(part_high - top_high)
        total = jnp.sum(part, axis=0, keepdims=True)
        inner = jnp.sum(part * gw_low[:, wide], axis=0, keepdims=True)
        total_high = total[:, half:] + jnp.sum(part_high, axis=0, keepdims=True)
        inner_high = inner[:, half:] + jnp.sum(part_high * gw_high[:, slim], axis=0, keepdims=True)
        low_ref[:, wide] = part
        high_ref[:, slim] = part_high
        stat_ref[0:1, wide] = top
        stat_ref[1:2, wide] = jnp.concatenate([total[:, :half], total_high], axis=1)
        stat_ref[2:3, wide] = jnp.concatenate([inner[:, :half], inner_high], axis=1)
    gw_low_ref[...] = gw_low
    gw_high_ref[...] = gw_high

    @pl.when(device == 0)
    def _():
        share = 1.0 / stat_ref[1:2]
        row_ref[0:1] = share
        row_ref[1:2] = stat_ref[2:3] * share
        finish(
            span, halo, q_ref, g_ref, k_ref, v_ref, low_ref, high_ref, gw_low_ref, gw_high_ref, row_ref, None,
            (out_ref, dq_ref, dk_ref, dv_ref, tail_ref), (out_far, dq_far, dk_far, dv_far), sems,
        )


def halo_kernel(
    span, mask_ref, pair_ref, ring_ref, q_ref, g_ref, stat_ref, edge_ref, p_ref, ds_ref, row_ref, back_ref
):
    first = device_index() == 0

    @pl.when(first)
    def _():
        back_ref[...] = jnp.zeros_like(back_ref)

    @pl.when(jnp.logical_not(first))
    def _():
        queries = side_by_side(q_ref)
        grads = side_by_side(g_ref)
        mask = jnp.concatenate([mask_ref[...]] * GROUP, axis=1)
        edge = jnp.where(device_index() == ring_cut(), pair_ref[...], ring_ref[...])
        edge_ref[...] = edge
        scores = dot(edge[:, :HD], queries, ROWS_BY_ROWS) * LOG2_SCALE + mask
        grad_weights = dot(edge[:, HD:], grads, ROWS_BY_ROWS)
        own_top = stat_ref[0:1]
        top = jnp.maximum(jnp.max(scores, axis=0, keepdims=True), own_top)
        weights = jnp.exp2(scores - top)
        shift = jnp.exp2(own_top - top)
        total = stat_ref[1:2] * shift + jnp.sum(weights, axis=0, keepdims=True)
        inner = stat_ref[2:3] * shift + jnp.sum(weights * grad_weights, axis=0, keepdims=True)
        share = 1.0 / total
        delta = inner * share
        p = weights * share
        p_low = p.astype(jnp.bfloat16)
        ds_low = (p * (grad_weights - delta) * SCALE).astype(jnp.bfloat16)
        back_ref[:, :HD] = dot(ds_low, queries, PLAIN).astype(back_ref.dtype)
        back_ref[:, HD:] = dot(p_low, grads, PLAIN).astype(back_ref.dtype)
        p_ref[...] = p_low
        ds_ref[...] = ds_low
        row_ref[0:1] = shift * share
        row_ref[1:2] = delta


def finish(
    span, halo, q_ref, g_ref, k_ref, v_ref, low_ref, high_ref, gw_low_ref, gw_high_ref, row_ref, edge, near, far, sems
):
    out_ref, dq_ref, dk_ref, dv_ref, tail_ref = near
    half = span // 2
    nothing = jnp.zeros((half, half), jnp.bfloat16)
    share = row_ref[0:1]
    delta = row_ref[1:2]
    later = lambda row: jnp.concatenate(
        [row[:, head * span + half : (head + 1) * span] for head in range(GROUP)], axis=1
    )
    whole = lambda low, high: jnp.concatenate(
        [
            low,
            jnp.concatenate(
                [piece for head in range(GROUP) for piece in (nothing, high[:, head * half : (head + 1) * half])],
                axis=1,
            ),
        ],
        axis=0,
    )
    low = low_ref[...] * share
    high = high_ref[...] * later(share)
    p = whole(low.astype(jnp.bfloat16), high.astype(jnp.bfloat16))
    ds = whole(
        (low * (gw_low_ref[...] - delta) * SCALE).astype(jnp.bfloat16),
        (high * (gw_high_ref[...] - later(delta)) * SCALE).astype(jnp.bfloat16),
    )
    grad_key = dot(ds, side_by_side(q_ref), PLAIN)
    grad_value = dot(p, side_by_side(g_ref), PLAIN)
    keys = k_ref[...]
    values = v_ref[...]
    if edge is not None:
        edge_ref, p_ref, ds_ref = edge
        keys = jnp.concatenate([edge_ref[:, :HD], keys], axis=0)
        values = jnp.concatenate([edge_ref[:, HD:], values], axis=0)
        p = jnp.concatenate([p_ref[...], p], axis=0)
        ds = jnp.concatenate([ds_ref[...], ds], axis=0)
    out = dot(p, values, COLS_BY_COLS).astype(jnp.bfloat16)
    dq = dot(ds, keys, COLS_BY_COLS).astype(jnp.bfloat16)
    for head in range(GROUP):
        out_ref[:, head_cols(head)] = out[head * span : (head + 1) * span]
        dq_ref[:, head_cols(head)] = dq[head * span : (head + 1) * span]
    dk_ref[...] = grad_key.astype(jnp.bfloat16)
    dv_ref[...] = grad_value.astype(jnp.bfloat16)
    tail_ref[:, :HD] = grad_key[span - halo :]
    tail_ref[:, HD:] = grad_value[span - halo :]
    for copy in start_all(zip(near[:4], far), sems):
        copy.wait()


def rest_kernel(
    span, halo, q_ref, g_ref, k_ref, v_ref, edge_ref, low_ref, high_ref, gw_low_ref, gw_high_ref, p_ref, ds_ref,
    row_ref, out_in, dq_in, dk_in, dv_in, tail_in, out_far, dq_far, dk_far, dv_far, tail_ref,
    out_ref, dq_ref, dk_ref, dv_ref, sems,
):
    del out_in, dq_in, dk_in, dv_in, tail_in

    @pl.when(device_index() > 0)
    def _():
        finish(
            span, halo, q_ref, g_ref, k_ref, v_ref, low_ref, high_ref, gw_low_ref, gw_high_ref, row_ref,
            (edge_ref, p_ref, ds_ref), (out_ref, dq_ref, dk_ref, dv_ref, tail_ref),
            (out_far, dq_far, dk_far, dv_far), sems,
        )


def tail_kernel(span, halo, tail_ref, pair_ref, ring_ref, dk_in, dv_in, dk_far, dv_far, dk_ref, dv_ref, sems):
    del dk_in, dv_in
    device = device_index()
    back = jnp.where(device == ring_cut() - 1, pair_ref[...], ring_ref[...]).astype(jnp.float32)
    total = tail_ref[...] + jnp.where(device == device_count() - 1, 0.0, back)
    dk_ref[...] = total[:, :HD].astype(jnp.bfloat16)
    dv_ref[...] = total[:, HD:].astype(jnp.bfloat16)
    last = pl.ds(span - halo, halo)
    for copy in start_all(((dk_ref, dk_far.at[last]), (dv_ref, dv_far.at[last])), sems):
        copy.wait()


def device_count():
    return lax.axis_size("seq") * lax.axis_size("head")


def ring_cut():
    return device_count() // 2 - 2


def passed_on(value, steps):
    count = device_count()
    cut = ring_cut()
    rings = [(source, source + 1) for source in range(count)]
    rings[cut - 1] = (cut - 1, 0)
    rings[count - 1] = (count - 1, cut)
    pairs = [(source, source ^ 1) for source in range(count)]
    pairs[cut - 2 : cut + 2] = [(cut - 2, cut - 1), (cut - 1, cut), (cut, cut + 1), (cut + 1, cut - 2)]
    if steps < 0:
        rings, pairs = [[(target, source) for source, target in way] for way in (rings, pairs)]
    by_pair = lax.ppermute(value, ("seq", "head"), pairs)
    return by_pair, lax.ppermute(value, ("seq", "head"), rings)


def span_on_device(queries, key_rows, value_rows, out_grad, doc_start):
    span = queries.shape[0]
    halo = span // 4
    wide, slim = (queries.shape, key_rows.shape)
    f32, bf16 = (jnp.float32, jnp.bfloat16)
    vmem = pl.BlockSpec(memory_space=pltpu.VMEM)
    hbm = pl.BlockSpec(memory_space=pltpu.HBM)
    near = lambda *values: [pltpu.with_memory_space_constraint(value, pltpu.VMEM) for value in values]
    far = lambda *values: [pltpu.with_memory_space_constraint(value, pltpu.HBM) for value in values]
    params = pltpu.CompilerParams(vmem_limit_bytes=VMEM_GRANT)
    results = [pltpu.VMEM(shape, bf16) for shape in (wide, wide, slim, slim)]
    results_far = [pltpu.HBM(shape, bf16) for shape in (wide, wide, slim, slim)]

    last_rows = pl.pallas_call(
        lambda *refs: pack_kernel(span, halo, *refs),
        in_specs=[hbm] * 2,
        out_specs=vmem,
        out_shape=pltpu.VMEM((halo, 2 * HD), bf16),
        scratch_shapes=[pltpu.SemaphoreType.DMA((2,))],
        compiler_params=params,
        cost_estimate=pl.CostEstimate(flops=4000000000, bytes_accessed=4 * 1024 * 1024, transcendentals=0),
        name="pack",
    )(*far(key_rows, value_rows))
    edges = passed_on(last_rows, 1)
    inputs = (queries, out_grad, key_rows, value_rows)
    low, high, gw_low, gw_high, stats, mask, tail, outputs, query_grad, key_grad, value_grad = pl.pallas_call(
        lambda *refs: own_kernel(span, halo, *refs),
        in_specs=[hbm] + [vmem] * 4,
        out_specs=[vmem] * 7 + [hbm] * 4,
        out_shape=[
            pltpu.VMEM((span // 2, GROUP * span), f32),
            pltpu.VMEM((span // 2, GROUP * span // 2), f32),
            pltpu.VMEM((span // 2, GROUP * span), f32),
            pltpu.VMEM((span // 2, GROUP * span // 2), f32),
            pltpu.VMEM((8, GROUP * span), f32),
            pltpu.VMEM((halo, span), f32),
            pltpu.VMEM((halo, 2 * HD), f32),
        ]
        + results_far,
        scratch_shapes=[pltpu.SMEM(doc_start.shape, jnp.int32), pltpu.VMEM((8, GROUP * span), f32)]
        + results
        + [pltpu.SemaphoreType.DMA(()), pltpu.SemaphoreType.DMA((4,))],
        compiler_params=params,
        name="own_scores",
    )(*far(doc_start), *inputs)
    edge, p_edge, ds_edge, rows, back = pl.pallas_call(
        lambda *refs: halo_kernel(span, *refs),
        in_specs=[vmem] * 6,
        out_specs=[vmem] * 5,
        out_shape=[
            pltpu.VMEM((halo, 2 * HD), bf16),
            pltpu.VMEM((halo, GROUP * span), bf16),
            pltpu.VMEM((halo, GROUP * span), bf16),
            pltpu.VMEM((8, GROUP * span), f32),
            pltpu.VMEM((halo, 2 * HD), bf16),
        ],
        compiler_params=params,
        name="halo_grads",
    )(*near(mask, *edges), *inputs[:2], *near(stats))
    returned = passed_on(back, -1)
    outputs, query_grad, key_grad, value_grad, tail = pl.pallas_call(
        lambda *refs: rest_kernel(span, halo, *refs),
        in_specs=[vmem] * 12 + [hbm] * 4 + [vmem],
        out_specs=[hbm] * 4 + [vmem],
        out_shape=results_far + [pltpu.VMEM((halo, 2 * HD), f32)],
        scratch_shapes=results + [pltpu.SemaphoreType.DMA((4,))],
        input_output_aliases={12: 0, 13: 1, 14: 2, 15: 3, 16: 4},
        compiler_params=params,
        name="own_grads",
    )(
        *inputs,
        *near(edge, low, high, gw_low, gw_high, p_edge, ds_edge, rows),
        *far(outputs, query_grad, key_grad, value_grad),
        *near(tail),
    )
    key_grad, value_grad = pl.pallas_call(
        lambda *refs: tail_kernel(span, halo, *refs),
        in_specs=[vmem, vmem, vmem, hbm, hbm],
        out_specs=[hbm, hbm],
        out_shape=results_far[2:],
        scratch_shapes=[pltpu.VMEM((halo, HD), bf16)] * 2 + [pltpu.SemaphoreType.DMA((2,))],
        input_output_aliases={3: 0, 4: 1},
        compiler_params=params,
        name="tail_grads",
    )(*near(tail, *returned), *far(key_grad, value_grad))
    return (outputs, query_grad, key_grad, value_grad)


def per_device(queries, key_rows, value_rows, out_grad, doc_start):
    span = queries.shape[0] * lax.axis_size("head") // SPANS_DEV
    whole_span = span == queries.shape[0] and key_rows.shape[1] == HD and queries.shape[1] == GROUP * HD
    whole_span = whole_span and device_count() % 4 == 0 and device_count() >= 8
    plan = span_on_device if whole_span else spans_over_devices
    return plan(queries, key_rows, value_rows, out_grad, doc_start)


def solution(mesh):
    placed = (
        P(("seq", "head"), None),
        P(("seq", "head"), None),
        P(("seq", "head"), None),
        P(("seq", "head"), None),
        P(),
    )
    return jax.shard_map(
        per_device,
        mesh=mesh,
        in_specs=placed,
        out_specs=(
            P(("seq", "head"), None),
            P(("seq", "head"), None),
            P(("seq", "head"), None),
            P(("seq", "head"), None),
        ),
        check_vma=False,
    )
```

```python
import math

import jax
import jax.numpy as jnp
from jax import lax
from jax.experimental import pallas as pl
from jax.experimental.pallas import tpu as pltpu
from jax.sharding import PartitionSpec as P

HD = 128
GROUP = 4
SPANS_DEV = 4
SCALE = 1.0 / math.sqrt(HD)
LOG2_SCALE = SCALE * math.log2(math.e)
VMEM_GRANT = 16 * 1024 * 1024


masked_fill = -1e30


def passed_along(value, axis, steps):
    count = lax.axis_size(axis)
    first, last = (max(0, -steps), min(count, count - steps))
    return lax.ppermute(value, axis, [(source, source + steps) for source in range(first, last)])


def allowed_mask(
    first_row, row_count, key_count, halo_len, span_len, span_start, prev_begin, span_index
):
    row_pos = first_row + lax.broadcasted_iota(jnp.int32, (row_count, key_count), 0)
    col_pos = lax.broadcasted_iota(jnp.int32, (row_count, key_count), 1) - halo_len
    return (
        (col_pos <= row_pos)
        & ((col_pos >= span_start) | (span_start > row_pos))
        & (col_pos >= prev_begin - span_len)
        & ((col_pos >= 0) | (span_index > 0))
    )


def attend(query_rows, grad_rows, key_block, value_block, allowed, head_dim):
    score_scale = 1.0 / math.sqrt(head_dim)
    contract = (((2,), (2,)), ((0,), (0,)))
    forward = (((2,), (1,)), ((0,), (0,)))
    backward = (((1,), (1,)), ((0,), (0,)))
    scores = (
        lax.dot_general(query_rows, key_block, contract, preferred_element_type=jnp.float32)
        * score_scale
    )
    masked = jnp.where(allowed, scores, masked_fill)
    row_max = jnp.max(masked, axis=2, keepdims=True)
    exp_scores = jnp.where(allowed, jnp.exp(masked - row_max), 0.0)
    weights = exp_scores / jnp.sum(exp_scores, axis=2, keepdims=True)
    weights_low = weights.astype(jnp.bfloat16)
    result = lax.dot_general(
        weights_low, value_block, forward, preferred_element_type=jnp.float32
    ).astype(jnp.bfloat16)
    grad_weights = lax.dot_general(
        grad_rows, value_block, contract, preferred_element_type=jnp.float32
    )
    row_delta = jnp.sum(weights * grad_weights, axis=2, keepdims=True)
    grad_scores = (weights * (grad_weights - row_delta) * score_scale).astype(jnp.bfloat16)
    grad_query = lax.dot_general(
        grad_scores, key_block, forward, preferred_element_type=jnp.float32
    )
    grad_key = lax.dot_general(
        grad_scores, query_rows, backward, preferred_element_type=jnp.float32
    )
    grad_value = lax.dot_general(
        weights_low, grad_rows, backward, preferred_element_type=jnp.float32
    )
    return (result, grad_query, grad_key, grad_value)


def spans_over_devices(queries, key_rows, value_rows, out_grad, doc_start):
    tok_count = queries.shape[0]
    head_count = lax.axis_size("head")
    group_rows = tok_count * head_count
    span_len = group_rows // SPANS_DEV
    halo_len = span_len // 4
    half_len = span_len // 2
    rest_len = span_len - halo_len
    head_q, head_grad = (
        lax.all_to_all(queries, "head", split_axis=1, concat_axis=0, tiled=True),
        lax.all_to_all(out_grad, "head", split_axis=1, concat_axis=0, tiled=True),
    )
    full_k, full_v = (
        lax.all_gather(key_rows, "head", axis=0, tiled=True),
        lax.all_gather(value_rows, "head", axis=0, tiled=True),
    )
    column = lax.axis_index("head") // GROUP * HD
    head_k = lax.dynamic_slice_in_dim(full_k, column, HD, 1)
    head_v = lax.dynamic_slice_in_dim(full_v, column, HD, 1)
    query_3 = head_q.reshape(SPANS_DEV, span_len, HD)
    grad_3 = head_grad.reshape(SPANS_DEV, span_len, HD)
    keys_3 = head_k.reshape(SPANS_DEV, span_len, HD)
    values_3 = head_v.reshape(SPANS_DEV, span_len, HD)
    tail_k = keys_3[:, rest_len:]
    tail_v = values_3[:, rest_len:]
    edge_last_k, edge_last_v = passed_along(
        (tail_k[SPANS_DEV - 1], tail_v[SPANS_DEV - 1]), "seq", 1
    )
    edge_k = jnp.concatenate([edge_last_k[None], tail_k[: SPANS_DEV - 1]], axis=0)
    edge_v = jnp.concatenate([edge_last_v[None], tail_v[: SPANS_DEV - 1]], axis=0)
    key_block = jnp.concatenate([edge_k, keys_3], axis=1)
    value_block = jnp.concatenate([edge_v, values_3], axis=1)
    first_span = lax.axis_index("seq") * SPANS_DEV
    span_starts = lax.dynamic_slice_in_dim(doc_start, first_span, SPANS_DEV)
    before_start = lax.dynamic_slice_in_dim(doc_start, jnp.maximum(first_span - 1, 0), 1)
    prev_starts = jnp.concatenate([before_start, span_starts[: SPANS_DEV - 1]], axis=0)
    span_ids = first_span + jnp.arange(SPANS_DEV, dtype=jnp.int32)
    span_starts = span_starts.reshape(SPANS_DEV, 1, 1)
    prev_starts = prev_starts.reshape(SPANS_DEV, 1, 1)
    span_ids = span_ids.reshape(SPANS_DEV, 1, 1)
    grad_key = jnp.zeros((SPANS_DEV, halo_len + span_len, HD), jnp.float32)
    grad_value = jnp.zeros((SPANS_DEV, halo_len + span_len, HD), jnp.float32)
    results = []
    query_grads = []
    for block_index in range(2):
        first_row = block_index * half_len
        key_count = halo_len + first_row + half_len
        allowed = allowed_mask(
            first_row, half_len, key_count, halo_len, span_len, span_starts, prev_starts, span_ids
        )
        result, grad_query, part_key, part_value = attend(
            query_3[:, first_row : first_row + half_len],
            grad_3[:, first_row : first_row + half_len],
            key_block[:, :key_count],
            value_block[:, :key_count],
            allowed,
            HD,
        )
        results.append(result)
        query_grads.append(grad_query.astype(jnp.bfloat16))
        grad_key = grad_key.at[:, :key_count].add(part_key)
        grad_value = grad_value.at[:, :key_count].add(part_value)
    next_last_k, next_last_v = passed_along(
        (grad_key[0, :halo_len], grad_value[0, :halo_len]), "seq", -1
    )
    next_k = jnp.concatenate([grad_key[1:, :halo_len], next_last_k[None]], axis=0)
    next_v = jnp.concatenate([grad_value[1:, :halo_len], next_last_v[None]], axis=0)
    own_k = jnp.concatenate(
        [grad_key[:, halo_len : halo_len + rest_len], grad_key[:, halo_len + rest_len :] + next_k],
        axis=1,
    ).reshape(group_rows, HD)
    own_v = jnp.concatenate(
        [
            grad_value[:, halo_len : halo_len + rest_len],
            grad_value[:, halo_len + rest_len :] + next_v,
        ],
        axis=1,
    ).reshape(group_rows, HD)
    all_results = jnp.concatenate(results, axis=1).reshape(group_rows, HD)
    all_query_grads = jnp.concatenate(query_grads, axis=1).reshape(group_rows, HD)
    outputs, query_grad = (
        lax.all_to_all(all_results, "head", split_axis=0, concat_axis=1, tiled=True),
        lax.all_to_all(all_query_grads, "head", split_axis=0, concat_axis=1, tiled=True),
    )
    wide_gk, wide_gv = (
        lax.all_to_all(own_k, "head", split_axis=0, concat_axis=1, tiled=True),
        lax.all_to_all(own_v, "head", split_axis=0, concat_axis=1, tiled=True),
    )
    group_total = wide_gk.shape[1] // (GROUP * HD)
    key_grad = (
        wide_gk.reshape(tok_count, group_total, GROUP, HD)
        .sum(axis=2)
        .reshape(tok_count, group_total * HD)
        .astype(jnp.bfloat16)
    )
    value_grad = (
        wide_gv.reshape(tok_count, group_total, GROUP, HD)
        .sum(axis=2)
        .reshape(tok_count, group_total * HD)
        .astype(jnp.bfloat16)
    )
    return (outputs, query_grad, key_grad, value_grad)


ROWS_BY_ROWS = (((1,), (1,)), ((), ()))
COLS_BY_COLS = (((0,), (0,)), ((), ()))
PLAIN = (((1,), (0,)), ((), ()))


def dot(left, right, dims):
    return lax.dot_general(left, right, dims, preferred_element_type=jnp.float32)


def head_cols(head):
    return slice(head * HD, (head + 1) * HD)


def device_index():
    return lax.axis_index("seq") * lax.axis_size("head") + lax.axis_index("head")


def start_all(pairs, sems):
    copies = [pltpu.make_async_copy(source, target, sems.at[at]) for at, (source, target) in enumerate(pairs)]
    for copy in copies:
        copy.start()
    return copies


def side_by_side(ref, rows=slice(None)):
    return jnp.concatenate([ref[rows, head_cols(head)] for head in range(GROUP)], axis=0)


def sends_far(device):
    return (device % 2 == 1) & (device < device_count() - 1)


def write_info(span, doc_ref, info_ref):
    device = device_index()
    before = doc_ref[jnp.maximum(device - 1, 0)]
    row = lax.broadcasted_iota(jnp.int32, info_ref.shape, 0)
    first = jnp.where(device > 0, before - span, span)
    info_ref[...] = jnp.where(row == 0, doc_ref[device], first)


def pack_kernel(span, halo, doc_far, k_far, v_far, edge_ref, info_ref, doc_ref, sems):
    sends = sends_far(device_index())

    @pl.when(jnp.logical_not(sends))
    def _():
        edge_ref[...] = jnp.zeros_like(edge_ref)
        info_ref[...] = jnp.zeros_like(info_ref)

    @pl.when(sends)
    def _():
        tail = pl.ds(span - halo, halo)
        pairs = (
            (k_far.at[tail], edge_ref.at[:, :HD]),
            (v_far.at[tail], edge_ref.at[:, HD:]),
            (doc_far, doc_ref),
        )
        for copy in start_all(pairs, sems):
            copy.wait()
        write_info(span, doc_ref, info_ref)


def pair_pack_kernel(span, halo, k_ref, v_ref, edge_ref):
    edge_ref[:, :HD] = k_ref[span - halo :]
    edge_ref[:, HD:] = v_ref[span - halo :]


def own_kernel(
    span, halo, doc_far, far_info_ref, q_ref, g_ref, k_ref, v_ref,
    low_ref, high_ref, gw_low_ref, gw_high_ref, stat_ref, mask_ref, tail_ref, out_far, dq_far, dk_far, dv_far,
    doc_ref, info_ref, row_ref, out_ref, dq_ref, dk_ref, dv_ref, doc_sem, sems,
):
    half = span // 2
    device = device_index()

    @pl.when(sends_far(device))
    def _():
        info_ref[...] = far_info_ref[...]

    @pl.when(jnp.logical_not(sends_far(device)))
    def _():
        copy = pltpu.make_async_copy(doc_far, doc_ref, doc_sem)
        copy.start()
        copy.wait()
        write_info(span, doc_ref, info_ref)

    gw_low = dot(v_ref[:half], side_by_side(g_ref), ROWS_BY_ROWS)
    gw_high = dot(v_ref[half:], side_by_side(g_ref, slice(half, span)), ROWS_BY_ROWS)
    low = dot(k_ref[:half], side_by_side(q_ref), ROWS_BY_ROWS)
    high = dot(k_ref[half:], side_by_side(q_ref, slice(half, span)), ROWS_BY_ROWS)
    start = info_ref[0:1, :1]
    first = info_ref[1:2, :1]
    key_pos = lax.broadcasted_iota(jnp.int32, (half, span), 0)
    row_pos = lax.broadcasted_iota(jnp.int32, (half, span), 1)
    fill_low = jnp.where((key_pos <= row_pos) & ((key_pos >= start) | (start > row_pos)), 0.0, masked_fill)
    key_pos = half + lax.broadcasted_iota(jnp.int32, (half, half), 0)
    row_pos = half + lax.broadcasted_iota(jnp.int32, (half, half), 1)
    fill_high = jnp.where((key_pos <= row_pos) & ((key_pos >= start) | (start > row_pos)), 0.0, masked_fill)
    key_pos = lax.broadcasted_iota(jnp.int32, (halo, span), 0) - halo
    row_pos = lax.broadcasted_iota(jnp.int32, (halo, span), 1)
    halo_ok = ((key_pos >= start) | (start > row_pos)) & (key_pos >= first)
    mask_ref[...] = jnp.where(halo_ok, 0.0, masked_fill)
    for head in range(GROUP):
        wide = slice(head * span, (head + 1) * span)
        slim = slice(head * half, (head + 1) * half)
        part = low[:, wide] * LOG2_SCALE + fill_low
        part_high = high[:, slim] * LOG2_SCALE + fill_high
        top = jnp.max(part, axis=0, keepdims=True)
        top_high = jnp.maximum(top[:, half:], jnp.max(part_high, axis=0, keepdims=True))
        top = jnp.concatenate([top[:, :half], top_high], axis=1)
        part = jnp.exp2(part - top)
        part_high = jnp.exp2(part_high - top_high)
        total = jnp.sum(part, axis=0, keepdims=True)
        inner = jnp.sum(part * gw_low[:, wide], axis=0, keepdims=True)
        total_high = total[:, half:] + jnp.sum(part_high, axis=0, keepdims=True)
        inner_high = inner[:, half:] + jnp.sum(part_high * gw_high[:, slim], axis=0, keepdims=True)
        low_ref[:, wide] = part
        high_ref[:, slim] = part_high
        stat_ref[0:1, wide] = top
        stat_ref[1:2, wide] = jnp.concatenate([total[:, :half], total_high], axis=1)
        stat_ref[2:3, wide] = jnp.concatenate([inner[:, :half], inner_high], axis=1)
    gw_low_ref[...] = gw_low
    gw_high_ref[...] = gw_high

    @pl.when(device == 0)
    def _():
        share = 1.0 / stat_ref[1:2]
        row_ref[0:1] = share
        row_ref[1:2] = stat_ref[2:3] * share
        finish(
            span, halo, q_ref, g_ref, k_ref, v_ref, low_ref, high_ref, gw_low_ref, gw_high_ref, row_ref, None,
            (out_ref, dq_ref, dk_ref, dv_ref, tail_ref), (out_far, dq_far, dk_far, dv_far), sems,
        )


def halo_kernel(
    span, mask_ref, pair_ref, ring_ref, q_ref, g_ref, stat_ref, edge_ref, p_ref, ds_ref, row_ref, back_ref
):
    first = device_index() == 0

    @pl.when(first)
    def _():
        back_ref[...] = jnp.zeros_like(back_ref)

    @pl.when(jnp.logical_not(first))
    def _():
        queries = side_by_side(q_ref)
        grads = side_by_side(g_ref)
        mask = jnp.concatenate([mask_ref[...]] * GROUP, axis=1)
        device = device_index()
        edge = jnp.where((device % 2 == 1) | (device == ring_cut(1)), pair_ref[...], ring_ref[...])
        edge_ref[...] = edge
        scores = dot(edge[:, :HD], queries, ROWS_BY_ROWS) * LOG2_SCALE + mask
        grad_weights = dot(edge[:, HD:], grads, ROWS_BY_ROWS)
        own_top = stat_ref[0:1]
        top = jnp.maximum(jnp.max(scores, axis=0, keepdims=True), own_top)
        weights = jnp.exp2(scores - top)
        shift = jnp.exp2(own_top - top)
        total = stat_ref[1:2] * shift + jnp.sum(weights, axis=0, keepdims=True)
        inner = stat_ref[2:3] * shift + jnp.sum(weights * grad_weights, axis=0, keepdims=True)
        share = 1.0 / total
        delta = inner * share
        p = weights * share
        p_low = p.astype(jnp.bfloat16)
        ds_low = (p * (grad_weights - delta) * SCALE).astype(jnp.bfloat16)
        back_ref[:, :HD] = dot(ds_low, queries, PLAIN).astype(back_ref.dtype)
        back_ref[:, HD:] = dot(p_low, grads, PLAIN).astype(back_ref.dtype)
        p_ref[...] = p_low
        ds_ref[...] = ds_low
        row_ref[0:1] = shift * share
        row_ref[1:2] = delta


def finish(
    span, halo, q_ref, g_ref, k_ref, v_ref, low_ref, high_ref, gw_low_ref, gw_high_ref, row_ref, edge, near, far, sems
):
    out_ref, dq_ref, dk_ref, dv_ref, tail_ref = near
    half = span // 2
    nothing = jnp.zeros((half, half), jnp.bfloat16)
    share = row_ref[0:1]
    delta = row_ref[1:2]
    later = lambda row: jnp.concatenate(
        [row[:, head * span + half : (head + 1) * span] for head in range(GROUP)], axis=1
    )
    whole = lambda low, high: jnp.concatenate(
        [
            low,
            jnp.concatenate(
                [piece for head in range(GROUP) for piece in (nothing, high[:, head * half : (head + 1) * half])],
                axis=1,
            ),
        ],
        axis=0,
    )
    low = low_ref[...] * share
    high = high_ref[...] * later(share)
    p = whole(low.astype(jnp.bfloat16), high.astype(jnp.bfloat16))
    ds = whole(
        (low * (gw_low_ref[...] - delta) * SCALE).astype(jnp.bfloat16),
        (high * (gw_high_ref[...] - later(delta)) * SCALE).astype(jnp.bfloat16),
    )
    grad_key = dot(ds, side_by_side(q_ref), PLAIN)
    grad_value = dot(p, side_by_side(g_ref), PLAIN)
    keys = k_ref[...]
    values = v_ref[...]
    if edge is not None:
        edge_ref, p_ref, ds_ref = edge
        keys = jnp.concatenate([edge_ref[:, :HD], keys], axis=0)
        values = jnp.concatenate([edge_ref[:, HD:], values], axis=0)
        p = jnp.concatenate([p_ref[...], p], axis=0)
        ds = jnp.concatenate([ds_ref[...], ds], axis=0)
    out = dot(p, values, COLS_BY_COLS).astype(jnp.bfloat16)
    dq = dot(ds, keys, COLS_BY_COLS).astype(jnp.bfloat16)
    for head in range(GROUP):
        out_ref[:, head_cols(head)] = out[head * span : (head + 1) * span]
        dq_ref[:, head_cols(head)] = dq[head * span : (head + 1) * span]
    dk_ref[...] = grad_key.astype(jnp.bfloat16)
    dv_ref[...] = grad_value.astype(jnp.bfloat16)
    tail_ref[:, :HD] = grad_key[span - halo :]
    tail_ref[:, HD:] = grad_value[span - halo :]
    for copy in start_all(zip(near[:4], far), sems):
        copy.wait()


def rest_kernel(
    span, halo, q_ref, g_ref, k_ref, v_ref, edge_ref, low_ref, high_ref, gw_low_ref, gw_high_ref, p_ref, ds_ref,
    row_ref, out_in, dq_in, dk_in, dv_in, tail_in, out_far, dq_far, dk_far, dv_far, tail_ref,
    out_ref, dq_ref, dk_ref, dv_ref, sems,
):
    del out_in, dq_in, dk_in, dv_in, tail_in

    @pl.when(device_index() > 0)
    def _():
        finish(
            span, halo, q_ref, g_ref, k_ref, v_ref, low_ref, high_ref, gw_low_ref, gw_high_ref, row_ref,
            (edge_ref, p_ref, ds_ref), (out_ref, dq_ref, dk_ref, dv_ref, tail_ref),
            (out_far, dq_far, dk_far, dv_far), sems,
        )


def tail_kernel(span, halo, tail_ref, pair_ref, ring_ref, dk_in, dv_in, dk_far, dv_far, dk_ref, dv_ref, sems):
    del dk_in, dv_in
    device = device_index()
    back = jnp.where(device == ring_cut(-1) - 1, pair_ref[...], ring_ref[...]).astype(jnp.float32)
    total = tail_ref[...] + jnp.where(device == device_count() - 1, 0.0, back)
    dk_ref[...] = total[:, :HD].astype(jnp.bfloat16)
    dv_ref[...] = total[:, HD:].astype(jnp.bfloat16)
    last = pl.ds(span - halo, halo)
    for copy in start_all(((dk_ref, dk_far.at[last]), (dv_ref, dv_far.at[last])), sems):
        copy.wait()


def device_count():
    return lax.axis_size("seq") * lax.axis_size("head")


def ring_cut(steps):
    return device_count() // 4 - 2 if steps > 0 else device_count() // 2 - 2


def passed_on(value, pair_value, steps):
    count = device_count()
    cut = ring_cut(steps)
    rings = [(source, source + 1) for source in range(count)]
    rings[cut - 1] = (cut - 1, 0)
    rings[count - 1] = (count - 1, cut)
    pairs = [(source, source ^ 1) for source in range(count)]
    pairs[cut - 2 : cut + 2] = [(cut - 2, cut - 1), (cut - 1, cut), (cut, cut + 1), (cut + 1, cut - 2)]
    if steps < 0:
        rings, pairs = [[(target, source) for source, target in way] for way in (rings, pairs)]
    by_pair = lax.ppermute(pair_value, ("seq", "head"), pairs)
    return by_pair, lax.ppermute(value, ("seq", "head"), rings)


def span_on_device(queries, key_rows, value_rows, out_grad, doc_start):
    span = queries.shape[0]
    halo = span // 4
    wide, slim = (queries.shape, key_rows.shape)
    f32, bf16 = (jnp.float32, jnp.bfloat16)
    vmem = pl.BlockSpec(memory_space=pltpu.VMEM)
    hbm = pl.BlockSpec(memory_space=pltpu.HBM)
    near = lambda *values: [pltpu.with_memory_space_constraint(value, pltpu.VMEM) for value in values]
    far = lambda *values: [pltpu.with_memory_space_constraint(value, pltpu.HBM) for value in values]
    params = pltpu.CompilerParams(vmem_limit_bytes=VMEM_GRANT)
    results = [pltpu.VMEM(shape, bf16) for shape in (wide, wide, slim, slim)]
    results_far = [pltpu.HBM(shape, bf16) for shape in (wide, wide, slim, slim)]

    last_rows, info = pl.pallas_call(
        lambda *refs: pack_kernel(span, halo, *refs),
        in_specs=[hbm] * 3,
        out_specs=[vmem] * 2,
        out_shape=[pltpu.VMEM((halo, 2 * HD), bf16), pltpu.VMEM((8, HD), jnp.int32)],
        scratch_shapes=[pltpu.SMEM(doc_start.shape, jnp.int32), pltpu.SemaphoreType.DMA((3,))],
        compiler_params=params,
        cost_estimate=pl.CostEstimate(flops=4000000000, bytes_accessed=4 * 1024 * 1024, transcendentals=0),
        name="pack",
    )(*far(doc_start, key_rows, value_rows))
    pair_rows = pl.pallas_call(
        lambda *refs: pair_pack_kernel(span, halo, *refs),
        in_specs=[vmem] * 2,
        out_specs=vmem,
        out_shape=pltpu.VMEM((halo, 2 * HD), bf16),
        compiler_params=params,
        name="pair_pack",
    )(key_rows, value_rows)
    edges = passed_on(last_rows, pair_rows, 1)
    inputs = (queries, out_grad, key_rows, value_rows)
    low, high, gw_low, gw_high, stats, mask, tail, outputs, query_grad, key_grad, value_grad = pl.pallas_call(
        lambda *refs: own_kernel(span, halo, *refs),
        in_specs=[hbm] + [vmem] * 5,
        out_specs=[vmem] * 7 + [hbm] * 4,
        out_shape=[
            pltpu.VMEM((span // 2, GROUP * span), f32),
            pltpu.VMEM((span // 2, GROUP * span // 2), f32),
            pltpu.VMEM((span // 2, GROUP * span), f32),
            pltpu.VMEM((span // 2, GROUP * span // 2), f32),
            pltpu.VMEM((8, GROUP * span), f32),
            pltpu.VMEM((halo, span), f32),
            pltpu.VMEM((halo, 2 * HD), f32),
        ]
        + results_far,
        scratch_shapes=[
            pltpu.SMEM(doc_start.shape, jnp.int32),
            pltpu.VMEM((8, HD), jnp.int32),
            pltpu.VMEM((8, GROUP * span), f32),
        ]
        + results
        + [pltpu.SemaphoreType.DMA(()), pltpu.SemaphoreType.DMA((4,))],
        compiler_params=params,
        name="own_scores",
    )(*far(doc_start), *near(info), *inputs)
    edge, p_edge, ds_edge, rows, back = pl.pallas_call(
        lambda *refs: halo_kernel(span, *refs),
        in_specs=[vmem] * 6,
        out_specs=[vmem] * 5,
        out_shape=[
            pltpu.VMEM((halo, 2 * HD), bf16),
            pltpu.VMEM((halo, GROUP * span), bf16),
            pltpu.VMEM((halo, GROUP * span), bf16),
            pltpu.VMEM((8, GROUP * span), f32),
            pltpu.VMEM((halo, 2 * HD), bf16),
        ],
        compiler_params=params,
        name="halo_grads",
    )(*near(mask, *edges), *inputs[:2], *near(stats))
    returned = passed_on(back, back, -1)
    outputs, query_grad, key_grad, value_grad, tail = pl.pallas_call(
        lambda *refs: rest_kernel(span, halo, *refs),
        in_specs=[vmem] * 12 + [hbm] * 4 + [vmem],
        out_specs=[hbm] * 4 + [vmem],
        out_shape=results_far + [pltpu.VMEM((halo, 2 * HD), f32)],
        scratch_shapes=results + [pltpu.SemaphoreType.DMA((4,))],
        input_output_aliases={12: 0, 13: 1, 14: 2, 15: 3, 16: 4},
        compiler_params=params,
        name="own_grads",
    )(
        *inputs,
        *near(edge, low, high, gw_low, gw_high, p_edge, ds_edge, rows),
        *far(outputs, query_grad, key_grad, value_grad),
        *near(tail),
    )
    key_grad, value_grad = pl.pallas_call(
        lambda *refs: tail_kernel(span, halo, *refs),
        in_specs=[vmem, vmem, vmem, hbm, hbm],
        out_specs=[hbm, hbm],
        out_shape=results_far[2:],
        scratch_shapes=[pltpu.VMEM((halo, HD), bf16)] * 2 + [pltpu.SemaphoreType.DMA((2,))],
        input_output_aliases={3: 0, 4: 1},
        compiler_params=params,
        name="tail_grads",
    )(*near(tail, *returned), *far(key_grad, value_grad))
    return (outputs, query_grad, key_grad, value_grad)


def per_device(queries, key_rows, value_rows, out_grad, doc_start):
    span = queries.shape[0] * lax.axis_size("head") // SPANS_DEV
    whole_span = span == queries.shape[0] and key_rows.shape[1] == HD and queries.shape[1] == GROUP * HD
    whole_span = whole_span and device_count() % 8 == 0 and device_count() >= 16
    plan = span_on_device if whole_span else spans_over_devices
    return plan(queries, key_rows, value_rows, out_grad, doc_start)


def solution(mesh):
    placed = (
        P(("seq", "head"), None),
        P(("seq", "head"), None),
        P(("seq", "head"), None),
        P(("seq", "head"), None),
        P(),
    )
    return jax.shard_map(
        per_device,
        mesh=mesh,
        in_specs=placed,
        out_specs=(
            P(("seq", "head"), None),
            P(("seq", "head"), None),
            P(("seq", "head"), None),
            P(("seq", "head"), None),
        ),
        check_vma=False,
    )
```

```python
import math

import jax
import jax.numpy as jnp
from jax import lax
from jax.experimental import pallas as pl
from jax.experimental.pallas import tpu as pltpu
from jax.sharding import PartitionSpec as P

HD = 128
GROUP = 4
SPANS_DEV = 4
SCALE = 1.0 / math.sqrt(HD)
LOG2_SCALE = SCALE * math.log2(math.e)
VMEM_GRANT = 16 * 1024 * 1024


masked_fill = -1e30


def passed_along(value, axis, steps):
    count = lax.axis_size(axis)
    first, last = (max(0, -steps), min(count, count - steps))
    return lax.ppermute(value, axis, [(source, source + steps) for source in range(first, last)])


def allowed_mask(
    first_row, row_count, key_count, halo_len, span_len, span_start, prev_begin, span_index
):
    row_pos = first_row + lax.broadcasted_iota(jnp.int32, (row_count, key_count), 0)
    col_pos = lax.broadcasted_iota(jnp.int32, (row_count, key_count), 1) - halo_len
    return (
        (col_pos <= row_pos)
        & ((col_pos >= span_start) | (span_start > row_pos))
        & (col_pos >= prev_begin - span_len)
        & ((col_pos >= 0) | (span_index > 0))
    )


def attend(query_rows, grad_rows, key_block, value_block, allowed, head_dim):
    score_scale = 1.0 / math.sqrt(head_dim)
    contract = (((2,), (2,)), ((0,), (0,)))
    forward = (((2,), (1,)), ((0,), (0,)))
    backward = (((1,), (1,)), ((0,), (0,)))
    scores = (
        lax.dot_general(query_rows, key_block, contract, preferred_element_type=jnp.float32)
        * score_scale
    )
    masked = jnp.where(allowed, scores, masked_fill)
    row_max = jnp.max(masked, axis=2, keepdims=True)
    exp_scores = jnp.where(allowed, jnp.exp(masked - row_max), 0.0)
    weights = exp_scores / jnp.sum(exp_scores, axis=2, keepdims=True)
    weights_low = weights.astype(jnp.bfloat16)
    result = lax.dot_general(
        weights_low, value_block, forward, preferred_element_type=jnp.float32
    ).astype(jnp.bfloat16)
    grad_weights = lax.dot_general(
        grad_rows, value_block, contract, preferred_element_type=jnp.float32
    )
    row_delta = jnp.sum(weights * grad_weights, axis=2, keepdims=True)
    grad_scores = (weights * (grad_weights - row_delta) * score_scale).astype(jnp.bfloat16)
    grad_query = lax.dot_general(
        grad_scores, key_block, forward, preferred_element_type=jnp.float32
    )
    grad_key = lax.dot_general(
        grad_scores, query_rows, backward, preferred_element_type=jnp.float32
    )
    grad_value = lax.dot_general(
        weights_low, grad_rows, backward, preferred_element_type=jnp.float32
    )
    return (result, grad_query, grad_key, grad_value)


def spans_over_devices(queries, key_rows, value_rows, out_grad, doc_start):
    tok_count = queries.shape[0]
    head_count = lax.axis_size("head")
    group_rows = tok_count * head_count
    span_len = group_rows // SPANS_DEV
    halo_len = span_len // 4
    half_len = span_len // 2
    rest_len = span_len - halo_len
    head_q, head_grad = (
        lax.all_to_all(queries, "head", split_axis=1, concat_axis=0, tiled=True),
        lax.all_to_all(out_grad, "head", split_axis=1, concat_axis=0, tiled=True),
    )
    full_k, full_v = (
        lax.all_gather(key_rows, "head", axis=0, tiled=True),
        lax.all_gather(value_rows, "head", axis=0, tiled=True),
    )
    column = lax.axis_index("head") // GROUP * HD
    head_k = lax.dynamic_slice_in_dim(full_k, column, HD, 1)
    head_v = lax.dynamic_slice_in_dim(full_v, column, HD, 1)
    query_3 = head_q.reshape(SPANS_DEV, span_len, HD)
    grad_3 = head_grad.reshape(SPANS_DEV, span_len, HD)
    keys_3 = head_k.reshape(SPANS_DEV, span_len, HD)
    values_3 = head_v.reshape(SPANS_DEV, span_len, HD)
    tail_k = keys_3[:, rest_len:]
    tail_v = values_3[:, rest_len:]
    edge_last_k, edge_last_v = passed_along(
        (tail_k[SPANS_DEV - 1], tail_v[SPANS_DEV - 1]), "seq", 1
    )
    edge_k = jnp.concatenate([edge_last_k[None], tail_k[: SPANS_DEV - 1]], axis=0)
    edge_v = jnp.concatenate([edge_last_v[None], tail_v[: SPANS_DEV - 1]], axis=0)
    key_block = jnp.concatenate([edge_k, keys_3], axis=1)
    value_block = jnp.concatenate([edge_v, values_3], axis=1)
    first_span = lax.axis_index("seq") * SPANS_DEV
    span_starts = lax.dynamic_slice_in_dim(doc_start, first_span, SPANS_DEV)
    before_start = lax.dynamic_slice_in_dim(doc_start, jnp.maximum(first_span - 1, 0), 1)
    prev_starts = jnp.concatenate([before_start, span_starts[: SPANS_DEV - 1]], axis=0)
    span_ids = first_span + jnp.arange(SPANS_DEV, dtype=jnp.int32)
    span_starts = span_starts.reshape(SPANS_DEV, 1, 1)
    prev_starts = prev_starts.reshape(SPANS_DEV, 1, 1)
    span_ids = span_ids.reshape(SPANS_DEV, 1, 1)
    grad_key = jnp.zeros((SPANS_DEV, halo_len + span_len, HD), jnp.float32)
    grad_value = jnp.zeros((SPANS_DEV, halo_len + span_len, HD), jnp.float32)
    results = []
    query_grads = []
    for block_index in range(2):
        first_row = block_index * half_len
        key_count = halo_len + first_row + half_len
        allowed = allowed_mask(
            first_row, half_len, key_count, halo_len, span_len, span_starts, prev_starts, span_ids
        )
        result, grad_query, part_key, part_value = attend(
            query_3[:, first_row : first_row + half_len],
            grad_3[:, first_row : first_row + half_len],
            key_block[:, :key_count],
            value_block[:, :key_count],
            allowed,
            HD,
        )
        results.append(result)
        query_grads.append(grad_query.astype(jnp.bfloat16))
        grad_key = grad_key.at[:, :key_count].add(part_key)
        grad_value = grad_value.at[:, :key_count].add(part_value)
    next_last_k, next_last_v = passed_along(
        (grad_key[0, :halo_len], grad_value[0, :halo_len]), "seq", -1
    )
    next_k = jnp.concatenate([grad_key[1:, :halo_len], next_last_k[None]], axis=0)
    next_v = jnp.concatenate([grad_value[1:, :halo_len], next_last_v[None]], axis=0)
    own_k = jnp.concatenate(
        [grad_key[:, halo_len : halo_len + rest_len], grad_key[:, halo_len + rest_len :] + next_k],
        axis=1,
    ).reshape(group_rows, HD)
    own_v = jnp.concatenate(
        [
            grad_value[:, halo_len : halo_len + rest_len],
            grad_value[:, halo_len + rest_len :] + next_v,
        ],
        axis=1,
    ).reshape(group_rows, HD)
    all_results = jnp.concatenate(results, axis=1).reshape(group_rows, HD)
    all_query_grads = jnp.concatenate(query_grads, axis=1).reshape(group_rows, HD)
    outputs, query_grad = (
        lax.all_to_all(all_results, "head", split_axis=0, concat_axis=1, tiled=True),
        lax.all_to_all(all_query_grads, "head", split_axis=0, concat_axis=1, tiled=True),
    )
    wide_gk, wide_gv = (
        lax.all_to_all(own_k, "head", split_axis=0, concat_axis=1, tiled=True),
        lax.all_to_all(own_v, "head", split_axis=0, concat_axis=1, tiled=True),
    )
    group_total = wide_gk.shape[1] // (GROUP * HD)
    key_grad = (
        wide_gk.reshape(tok_count, group_total, GROUP, HD)
        .sum(axis=2)
        .reshape(tok_count, group_total * HD)
        .astype(jnp.bfloat16)
    )
    value_grad = (
        wide_gv.reshape(tok_count, group_total, GROUP, HD)
        .sum(axis=2)
        .reshape(tok_count, group_total * HD)
        .astype(jnp.bfloat16)
    )
    return (outputs, query_grad, key_grad, value_grad)


ROWS_BY_ROWS = (((1,), (1,)), ((), ()))
COLS_BY_COLS = (((0,), (0,)), ((), ()))
PLAIN = (((1,), (0,)), ((), ()))


def dot(left, right, dims):
    return lax.dot_general(left, right, dims, preferred_element_type=jnp.float32)


def head_cols(head):
    return slice(head * HD, (head + 1) * HD)


def device_index():
    return lax.axis_index("seq") * lax.axis_size("head") + lax.axis_index("head")


def start_all(pairs, sems):
    copies = [pltpu.make_async_copy(source, target, sems.at[at]) for at, (source, target) in enumerate(pairs)]
    for copy in copies:
        copy.start()
    return copies


def side_by_side(ref, rows=slice(None)):
    return jnp.concatenate([ref[rows, head_cols(head)] for head in range(GROUP)], axis=0)


def sends_far(device):
    return (device % 2 == 1) & (device < device_count() - 1)


def write_info(span, doc_ref, info_ref):
    device = device_index()
    before = doc_ref[jnp.maximum(device - 1, 0)]
    row = lax.broadcasted_iota(jnp.int32, info_ref.shape, 0)
    first = jnp.where(device > 0, before - span, span)
    info_ref[...] = jnp.where(row == 0, doc_ref[device], first)


def pack_kernel(span, halo, doc_far, k_far, v_far, edge_ref, info_ref, doc_ref, sems):
    sends = sends_far(device_index())

    @pl.when(jnp.logical_not(sends))
    def _():
        edge_ref[...] = jnp.zeros_like(edge_ref)
        info_ref[...] = jnp.zeros_like(info_ref)

    @pl.when(sends)
    def _():
        tail = pl.ds(span - halo, halo)
        pairs = (
            (k_far.at[tail], edge_ref.at[:, :HD]),
            (v_far.at[tail], edge_ref.at[:, HD:]),
            (doc_far, doc_ref),
        )
        for copy in start_all(pairs, sems):
            copy.wait()
        write_info(span, doc_ref, info_ref)


def pair_pack_kernel(span, halo, k_ref, v_ref, edge_ref):
    edge_ref[:, :HD] = k_ref[span - halo :]
    edge_ref[:, HD:] = v_ref[span - halo :]


def own_kernel(
    span, halo, doc_far, far_info_ref, q_ref, g_ref, k_ref, v_ref,
    low_ref, high_ref, gw_low_ref, gw_high_ref, stat_ref, mask_ref, tail_ref, out_far, dq_far, dk_far, dv_far,
    doc_ref, info_ref, row_ref, out_ref, dq_ref, dk_ref, dv_ref, doc_sem, sems,
):
    half = span // 2
    device = device_index()

    @pl.when(sends_far(device))
    def _():
        info_ref[...] = far_info_ref[...]

    @pl.when(jnp.logical_not(sends_far(device)))
    def _():
        copy = pltpu.make_async_copy(doc_far, doc_ref, doc_sem)
        copy.start()
        copy.wait()
        write_info(span, doc_ref, info_ref)

    gw_low = dot(v_ref[:half], side_by_side(g_ref), ROWS_BY_ROWS)
    gw_high = dot(v_ref[half:], side_by_side(g_ref, slice(half, span)), ROWS_BY_ROWS)
    low = dot(k_ref[:half], side_by_side(q_ref), ROWS_BY_ROWS)
    high = dot(k_ref[half:], side_by_side(q_ref, slice(half, span)), ROWS_BY_ROWS)
    start = info_ref[0:1, :1]
    first = info_ref[1:2, :1]
    key_pos = lax.broadcasted_iota(jnp.int32, (half, span), 0)
    row_pos = lax.broadcasted_iota(jnp.int32, (half, span), 1)
    fill_low = jnp.where((key_pos <= row_pos) & ((key_pos >= start) | (start > row_pos)), 0.0, masked_fill)
    key_pos = half + lax.broadcasted_iota(jnp.int32, (half, half), 0)
    row_pos = half + lax.broadcasted_iota(jnp.int32, (half, half), 1)
    fill_high = jnp.where((key_pos <= row_pos) & ((key_pos >= start) | (start > row_pos)), 0.0, masked_fill)
    key_pos = lax.broadcasted_iota(jnp.int32, (halo, span), 0) - halo
    row_pos = lax.broadcasted_iota(jnp.int32, (halo, span), 1)
    halo_ok = ((key_pos >= start) | (start > row_pos)) & (key_pos >= first)
    mask_ref[...] = jnp.where(halo_ok, 0.0, masked_fill)
    for head in range(GROUP):
        wide = slice(head * span, (head + 1) * span)
        slim = slice(head * half, (head + 1) * half)
        part = low[:, wide] * LOG2_SCALE + fill_low
        part_high = high[:, slim] * LOG2_SCALE + fill_high
        top = jnp.max(part, axis=0, keepdims=True)
        top_high = jnp.maximum(top[:, half:], jnp.max(part_high, axis=0, keepdims=True))
        top = jnp.concatenate([top[:, :half], top_high], axis=1)
        part = jnp.exp2(part - top)
        part_high = jnp.exp2(part_high - top_high)
        total = jnp.sum(part, axis=0, keepdims=True)
        inner = jnp.sum(part * gw_low[:, wide], axis=0, keepdims=True)
        total_high = total[:, half:] + jnp.sum(part_high, axis=0, keepdims=True)
        inner_high = inner[:, half:] + jnp.sum(part_high * gw_high[:, slim], axis=0, keepdims=True)
        low_ref[:, wide] = part
        high_ref[:, slim] = part_high
        stat_ref[0:1, wide] = top
        stat_ref[1:2, wide] = jnp.concatenate([total[:, :half], total_high], axis=1)
        stat_ref[2:3, wide] = jnp.concatenate([inner[:, :half], inner_high], axis=1)
    gw_low_ref[...] = gw_low
    gw_high_ref[...] = gw_high

    @pl.when(device == 0)
    def _():
        share = 1.0 / stat_ref[1:2]
        row_ref[0:1] = share
        row_ref[1:2] = stat_ref[2:3] * share
        finish(
            span, halo, q_ref, g_ref, k_ref, v_ref, low_ref, high_ref, gw_low_ref, gw_high_ref, row_ref, None,
            (out_ref, dq_ref, dk_ref, dv_ref, tail_ref), (out_far, dq_far, dk_far, dv_far), sems,
        )


def halo_kernel(
    span, mask_ref, pair_ref, ring_ref, q_ref, g_ref, stat_ref, edge_ref, p_ref, ds_ref, row_ref, back_ref
):
    queries = side_by_side(q_ref)
    grads = side_by_side(g_ref)
    mask = jnp.concatenate([mask_ref[...]] * GROUP, axis=1)
    device = device_index()
    edge = jnp.where((device % 2 == 1) | (device == ring_cut(1)), pair_ref[...], ring_ref[...])
    edge_ref[...] = edge
    scores = dot(edge[:, :HD], queries, ROWS_BY_ROWS) * LOG2_SCALE + mask
    grad_weights = dot(edge[:, HD:], grads, ROWS_BY_ROWS)
    own_top = stat_ref[0:1]
    top = jnp.maximum(jnp.max(scores, axis=0, keepdims=True), own_top)
    weights = jnp.exp2(scores - top)
    shift = jnp.exp2(own_top - top)
    total = stat_ref[1:2] * shift + jnp.sum(weights, axis=0, keepdims=True)
    inner = stat_ref[2:3] * shift + jnp.sum(weights * grad_weights, axis=0, keepdims=True)
    share = 1.0 / total
    delta = inner * share
    p = weights * share
    p_low = p.astype(jnp.bfloat16)
    ds_low = (p * (grad_weights - delta) * SCALE).astype(jnp.bfloat16)
    back_ref[:, :HD] = dot(ds_low, queries, PLAIN).astype(back_ref.dtype)
    back_ref[:, HD:] = dot(p_low, grads, PLAIN).astype(back_ref.dtype)
    p_ref[...] = p_low
    ds_ref[...] = ds_low
    row_ref[0:1] = shift * share
    row_ref[1:2] = delta


def finish(
    span, halo, q_ref, g_ref, k_ref, v_ref, low_ref, high_ref, gw_low_ref, gw_high_ref, row_ref, edge, near, far, sems
):
    out_ref, dq_ref, dk_ref, dv_ref, tail_ref = near
    half = span // 2
    nothing = jnp.zeros((half, half), jnp.bfloat16)
    share = row_ref[0:1]
    delta = row_ref[1:2]
    later = lambda row: jnp.concatenate(
        [row[:, head * span + half : (head + 1) * span] for head in range(GROUP)], axis=1
    )
    whole = lambda low, high: jnp.concatenate(
        [
            low,
            jnp.concatenate(
                [piece for head in range(GROUP) for piece in (nothing, high[:, head * half : (head + 1) * half])],
                axis=1,
            ),
        ],
        axis=0,
    )
    low = low_ref[...] * share
    high = high_ref[...] * later(share)
    p = whole(low.astype(jnp.bfloat16), high.astype(jnp.bfloat16))
    ds = whole(
        (low * (gw_low_ref[...] - delta) * SCALE).astype(jnp.bfloat16),
        (high * (gw_high_ref[...] - later(delta)) * SCALE).astype(jnp.bfloat16),
    )
    grad_key = dot(ds, side_by_side(q_ref), PLAIN)
    grad_value = dot(p, side_by_side(g_ref), PLAIN)
    keys = k_ref[...]
    values = v_ref[...]
    if edge is not None:
        edge_ref, p_ref, ds_ref = edge
        keys = jnp.concatenate([edge_ref[:, :HD], keys], axis=0)
        values = jnp.concatenate([edge_ref[:, HD:], values], axis=0)
        p = jnp.concatenate([p_ref[...], p], axis=0)
        ds = jnp.concatenate([ds_ref[...], ds], axis=0)
    out = dot(p, values, COLS_BY_COLS).astype(jnp.bfloat16)
    dq = dot(ds, keys, COLS_BY_COLS).astype(jnp.bfloat16)
    for head in range(GROUP):
        out_ref[:, head_cols(head)] = out[head * span : (head + 1) * span]
        dq_ref[:, head_cols(head)] = dq[head * span : (head + 1) * span]
    dk_ref[...] = grad_key.astype(jnp.bfloat16)
    dv_ref[...] = grad_value.astype(jnp.bfloat16)
    tail_ref[:, :HD] = grad_key[span - halo :]
    tail_ref[:, HD:] = grad_value[span - halo :]
    for copy in start_all(zip(near[:4], far), sems):
        copy.wait()


def rest_kernel(
    span, halo, q_ref, g_ref, k_ref, v_ref, edge_ref, low_ref, high_ref, gw_low_ref, gw_high_ref, p_ref, ds_ref,
    row_ref, out_in, dq_in, dk_in, dv_in, tail_in, out_far, dq_far, dk_far, dv_far, tail_ref,
    out_ref, dq_ref, dk_ref, dv_ref, sems,
):
    del out_in, dq_in, dk_in, dv_in, tail_in

    @pl.when(device_index() > 0)
    def _():
        finish(
            span, halo, q_ref, g_ref, k_ref, v_ref, low_ref, high_ref, gw_low_ref, gw_high_ref, row_ref,
            (edge_ref, p_ref, ds_ref), (out_ref, dq_ref, dk_ref, dv_ref, tail_ref),
            (out_far, dq_far, dk_far, dv_far), sems,
        )


def tail_kernel(span, halo, tail_ref, pair_ref, ring_ref, dk_in, dv_in, dk_far, dv_far, dk_ref, dv_ref, sems):
    del dk_in, dv_in
    device = device_index()
    back = jnp.where(device == ring_cut(-1) - 1, pair_ref[...], ring_ref[...]).astype(jnp.float32)
    total = tail_ref[...] + jnp.where(device == device_count() - 1, 0.0, back)
    dk_ref[...] = total[:, :HD].astype(jnp.bfloat16)
    dv_ref[...] = total[:, HD:].astype(jnp.bfloat16)
    last = pl.ds(span - halo, halo)
    for copy in start_all(((dk_ref, dk_far.at[last]), (dv_ref, dv_far.at[last])), sems):
        copy.wait()


def device_count():
    return lax.axis_size("seq") * lax.axis_size("head")


def ring_cut(steps):
    return device_count() // 2 + (2 if steps > 0 else -2)


def passed_on(value, pair_value, steps):
    count = device_count()
    cut = ring_cut(steps)
    rings = [(source, source + 1) for source in range(count)]
    rings[cut - 1] = (cut - 1, 0)
    rings[count - 1] = (count - 1, cut)
    pairs = [(source, source ^ 1) for source in range(count)]
    pairs[cut - 2 : cut + 2] = [(cut - 2, cut - 1), (cut - 1, cut), (cut, cut + 1), (cut + 1, cut - 2)]
    if steps < 0:
        rings, pairs = [[(target, source) for source, target in way] for way in (rings, pairs)]
    by_pair = lax.ppermute(pair_value, ("seq", "head"), pairs)
    return by_pair, lax.ppermute(value, ("seq", "head"), rings)


def span_on_device(queries, key_rows, value_rows, out_grad, doc_start):
    span = queries.shape[0]
    halo = span // 4
    wide, slim = (queries.shape, key_rows.shape)
    f32, bf16 = (jnp.float32, jnp.bfloat16)
    vmem = pl.BlockSpec(memory_space=pltpu.VMEM)
    hbm = pl.BlockSpec(memory_space=pltpu.HBM)
    near = lambda *values: [pltpu.with_memory_space_constraint(value, pltpu.VMEM) for value in values]
    far = lambda *values: [pltpu.with_memory_space_constraint(value, pltpu.HBM) for value in values]
    params = pltpu.CompilerParams(vmem_limit_bytes=VMEM_GRANT)
    results = [pltpu.VMEM(shape, bf16) for shape in (wide, wide, slim, slim)]
    results_far = [pltpu.HBM(shape, bf16) for shape in (wide, wide, slim, slim)]

    last_rows, info = pl.pallas_call(
        lambda *refs: pack_kernel(span, halo, *refs),
        in_specs=[hbm] * 3,
        out_specs=[vmem] * 2,
        out_shape=[pltpu.VMEM((halo, 2 * HD), bf16), pltpu.VMEM((8, HD), jnp.int32)],
        scratch_shapes=[pltpu.SMEM(doc_start.shape, jnp.int32), pltpu.SemaphoreType.DMA((3,))],
        compiler_params=params,
        cost_estimate=pl.CostEstimate(flops=4000000000, bytes_accessed=4 * 1024 * 1024, transcendentals=0),
        name="pack",
    )(*far(doc_start, key_rows, value_rows))
    pair_rows = pl.pallas_call(
        lambda *refs: pair_pack_kernel(span, halo, *refs),
        in_specs=[vmem] * 2,
        out_specs=vmem,
        out_shape=pltpu.VMEM((halo, 2 * HD), bf16),
        compiler_params=params,
        name="pair_pack",
    )(key_rows, value_rows)
    edges = passed_on(last_rows, pair_rows, 1)
    inputs = (queries, out_grad, key_rows, value_rows)
    low, high, gw_low, gw_high, stats, mask, tail, outputs, query_grad, key_grad, value_grad = pl.pallas_call(
        lambda *refs: own_kernel(span, halo, *refs),
        in_specs=[hbm] + [vmem] * 5,
        out_specs=[vmem] * 7 + [hbm] * 4,
        out_shape=[
            pltpu.VMEM((span // 2, GROUP * span), f32),
            pltpu.VMEM((span // 2, GROUP * span // 2), f32),
            pltpu.VMEM((span // 2, GROUP * span), f32),
            pltpu.VMEM((span // 2, GROUP * span // 2), f32),
            pltpu.VMEM((8, GROUP * span), f32),
            pltpu.VMEM((halo, span), f32),
            pltpu.VMEM((halo, 2 * HD), f32),
        ]
        + results_far,
        scratch_shapes=[
            pltpu.SMEM(doc_start.shape, jnp.int32),
            pltpu.VMEM((8, HD), jnp.int32),
            pltpu.VMEM((8, GROUP * span), f32),
        ]
        + results
        + [pltpu.SemaphoreType.DMA(()), pltpu.SemaphoreType.DMA((4,))],
        compiler_params=params,
        name="own_scores",
    )(*far(doc_start), *near(info), *inputs)
    edge, p_edge, ds_edge, rows, back = pl.pallas_call(
        lambda *refs: halo_kernel(span, *refs),
        in_specs=[vmem] * 6,
        out_specs=[vmem] * 5,
        out_shape=[
            pltpu.VMEM((halo, 2 * HD), bf16),
            pltpu.VMEM((halo, GROUP * span), bf16),
            pltpu.VMEM((halo, GROUP * span), bf16),
            pltpu.VMEM((8, GROUP * span), f32),
            pltpu.VMEM((halo, 2 * HD), bf16),
        ],
        compiler_params=params,
        name="halo_grads",
    )(*near(mask, *edges), *inputs[:2], *near(stats))
    returned = passed_on(back, back, -1)
    outputs, query_grad, key_grad, value_grad, tail = pl.pallas_call(
        lambda *refs: rest_kernel(span, halo, *refs),
        in_specs=[vmem] * 12 + [hbm] * 4 + [vmem],
        out_specs=[hbm] * 4 + [vmem],
        out_shape=results_far + [pltpu.VMEM((halo, 2 * HD), f32)],
        scratch_shapes=results + [pltpu.SemaphoreType.DMA((4,))],
        input_output_aliases={12: 0, 13: 1, 14: 2, 15: 3, 16: 4},
        compiler_params=params,
        name="own_grads",
    )(
        *inputs,
        *near(edge, low, high, gw_low, gw_high, p_edge, ds_edge, rows),
        *far(outputs, query_grad, key_grad, value_grad),
        *near(tail),
    )
    key_grad, value_grad = pl.pallas_call(
        lambda *refs: tail_kernel(span, halo, *refs),
        in_specs=[vmem, vmem, vmem, hbm, hbm],
        out_specs=[hbm, hbm],
        out_shape=results_far[2:],
        scratch_shapes=[pltpu.VMEM((halo, HD), bf16)] * 2 + [pltpu.SemaphoreType.DMA((2,))],
        input_output_aliases={3: 0, 4: 1},
        compiler_params=params,
        name="tail_grads",
    )(*near(tail, *returned), *far(key_grad, value_grad))
    return (outputs, query_grad, key_grad, value_grad)


def per_device(queries, key_rows, value_rows, out_grad, doc_start):
    span = queries.shape[0] * lax.axis_size("head") // SPANS_DEV
    whole_span = span == queries.shape[0] and key_rows.shape[1] == HD and queries.shape[1] == GROUP * HD
    whole_span = whole_span and device_count() % 8 == 0 and device_count() >= 16
    plan = span_on_device if whole_span else spans_over_devices
    return plan(queries, key_rows, value_rows, out_grad, doc_start)


def solution(mesh):
    placed = (
        P(("seq", "head"), None),
        P(("seq", "head"), None),
        P(("seq", "head"), None),
        P(("seq", "head"), None),
        P(),
    )
    return jax.shard_map(
        per_device,
        mesh=mesh,
        in_specs=placed,
        out_specs=(
            P(("seq", "head"), None),
            P(("seq", "head"), None),
            P(("seq", "head"), None),
            P(("seq", "head"), None),
        ),
        check_vma=False,
    )
```

```python
import math

import jax
import jax.numpy as jnp
from jax import lax
from jax.experimental import pallas as pl
from jax.experimental.pallas import tpu as pltpu
from jax.sharding import PartitionSpec as P

HD = 128
GROUP = 4
SPANS_DEV = 4
SCALE = 1.0 / math.sqrt(HD)
LOG2_SCALE = SCALE * math.log2(math.e)
VMEM_GRANT = 16 * 1024 * 1024


masked_fill = -1e30


def passed_along(value, axis, steps):
    count = lax.axis_size(axis)
    first, last = (max(0, -steps), min(count, count - steps))
    return lax.ppermute(value, axis, [(source, source + steps) for source in range(first, last)])


def allowed_mask(
    first_row, row_count, key_count, halo_len, span_len, span_start, prev_begin, span_index
):
    row_pos = first_row + lax.broadcasted_iota(jnp.int32, (row_count, key_count), 0)
    col_pos = lax.broadcasted_iota(jnp.int32, (row_count, key_count), 1) - halo_len
    return (
        (col_pos <= row_pos)
        & ((col_pos >= span_start) | (span_start > row_pos))
        & (col_pos >= prev_begin - span_len)
        & ((col_pos >= 0) | (span_index > 0))
    )


def attend(query_rows, grad_rows, key_block, value_block, allowed, head_dim):
    score_scale = 1.0 / math.sqrt(head_dim)
    contract = (((2,), (2,)), ((0,), (0,)))
    forward = (((2,), (1,)), ((0,), (0,)))
    backward = (((1,), (1,)), ((0,), (0,)))
    scores = (
        lax.dot_general(query_rows, key_block, contract, preferred_element_type=jnp.float32)
        * score_scale
    )
    masked = jnp.where(allowed, scores, masked_fill)
    row_max = jnp.max(masked, axis=2, keepdims=True)
    exp_scores = jnp.where(allowed, jnp.exp(masked - row_max), 0.0)
    weights = exp_scores / jnp.sum(exp_scores, axis=2, keepdims=True)
    weights_low = weights.astype(jnp.bfloat16)
    result = lax.dot_general(
        weights_low, value_block, forward, preferred_element_type=jnp.float32
    ).astype(jnp.bfloat16)
    grad_weights = lax.dot_general(
        grad_rows, value_block, contract, preferred_element_type=jnp.float32
    )
    row_delta = jnp.sum(weights * grad_weights, axis=2, keepdims=True)
    grad_scores = (weights * (grad_weights - row_delta) * score_scale).astype(jnp.bfloat16)
    grad_query = lax.dot_general(
        grad_scores, key_block, forward, preferred_element_type=jnp.float32
    )
    grad_key = lax.dot_general(
        grad_scores, query_rows, backward, preferred_element_type=jnp.float32
    )
    grad_value = lax.dot_general(
        weights_low, grad_rows, backward, preferred_element_type=jnp.float32
    )
    return (result, grad_query, grad_key, grad_value)


def spans_over_devices(queries, key_rows, value_rows, out_grad, doc_start):
    tok_count = queries.shape[0]
    head_count = lax.axis_size("head")
    group_rows = tok_count * head_count
    span_len = group_rows // SPANS_DEV
    halo_len = span_len // 4
    half_len = span_len // 2
    rest_len = span_len - halo_len
    head_q, head_grad = (
        lax.all_to_all(queries, "head", split_axis=1, concat_axis=0, tiled=True),
        lax.all_to_all(out_grad, "head", split_axis=1, concat_axis=0, tiled=True),
    )
    full_k, full_v = (
        lax.all_gather(key_rows, "head", axis=0, tiled=True),
        lax.all_gather(value_rows, "head", axis=0, tiled=True),
    )
    column = lax.axis_index("head") // GROUP * HD
    head_k = lax.dynamic_slice_in_dim(full_k, column, HD, 1)
    head_v = lax.dynamic_slice_in_dim(full_v, column, HD, 1)
    query_3 = head_q.reshape(SPANS_DEV, span_len, HD)
    grad_3 = head_grad.reshape(SPANS_DEV, span_len, HD)
    keys_3 = head_k.reshape(SPANS_DEV, span_len, HD)
    values_3 = head_v.reshape(SPANS_DEV, span_len, HD)
    tail_k = keys_3[:, rest_len:]
    tail_v = values_3[:, rest_len:]
    edge_last_k, edge_last_v = passed_along(
        (tail_k[SPANS_DEV - 1], tail_v[SPANS_DEV - 1]), "seq", 1
    )
    edge_k = jnp.concatenate([edge_last_k[None], tail_k[: SPANS_DEV - 1]], axis=0)
    edge_v = jnp.concatenate([edge_last_v[None], tail_v[: SPANS_DEV - 1]], axis=0)
    key_block = jnp.concatenate([edge_k, keys_3], axis=1)
    value_block = jnp.concatenate([edge_v, values_3], axis=1)
    first_span = lax.axis_index("seq") * SPANS_DEV
    span_starts = lax.dynamic_slice_in_dim(doc_start, first_span, SPANS_DEV)
    before_start = lax.dynamic_slice_in_dim(doc_start, jnp.maximum(first_span - 1, 0), 1)
    prev_starts = jnp.concatenate([before_start, span_starts[: SPANS_DEV - 1]], axis=0)
    span_ids = first_span + jnp.arange(SPANS_DEV, dtype=jnp.int32)
    span_starts = span_starts.reshape(SPANS_DEV, 1, 1)
    prev_starts = prev_starts.reshape(SPANS_DEV, 1, 1)
    span_ids = span_ids.reshape(SPANS_DEV, 1, 1)
    grad_key = jnp.zeros((SPANS_DEV, halo_len + span_len, HD), jnp.float32)
    grad_value = jnp.zeros((SPANS_DEV, halo_len + span_len, HD), jnp.float32)
    results = []
    query_grads = []
    for block_index in range(2):
        first_row = block_index * half_len
        key_count = halo_len + first_row + half_len
        allowed = allowed_mask(
            first_row, half_len, key_count, halo_len, span_len, span_starts, prev_starts, span_ids
        )
        result, grad_query, part_key, part_value = attend(
            query_3[:, first_row : first_row + half_len],
            grad_3[:, first_row : first_row + half_len],
            key_block[:, :key_count],
            value_block[:, :key_count],
            allowed,
            HD,
        )
        results.append(result)
        query_grads.append(grad_query.astype(jnp.bfloat16))
        grad_key = grad_key.at[:, :key_count].add(part_key)
        grad_value = grad_value.at[:, :key_count].add(part_value)
    next_last_k, next_last_v = passed_along(
        (grad_key[0, :halo_len], grad_value[0, :halo_len]), "seq", -1
    )
    next_k = jnp.concatenate([grad_key[1:, :halo_len], next_last_k[None]], axis=0)
    next_v = jnp.concatenate([grad_value[1:, :halo_len], next_last_v[None]], axis=0)
    own_k = jnp.concatenate(
        [grad_key[:, halo_len : halo_len + rest_len], grad_key[:, halo_len + rest_len :] + next_k],
        axis=1,
    ).reshape(group_rows, HD)
    own_v = jnp.concatenate(
        [
            grad_value[:, halo_len : halo_len + rest_len],
            grad_value[:, halo_len + rest_len :] + next_v,
        ],
        axis=1,
    ).reshape(group_rows, HD)
    all_results = jnp.concatenate(results, axis=1).reshape(group_rows, HD)
    all_query_grads = jnp.concatenate(query_grads, axis=1).reshape(group_rows, HD)
    outputs, query_grad = (
        lax.all_to_all(all_results, "head", split_axis=0, concat_axis=1, tiled=True),
        lax.all_to_all(all_query_grads, "head", split_axis=0, concat_axis=1, tiled=True),
    )
    wide_gk, wide_gv = (
        lax.all_to_all(own_k, "head", split_axis=0, concat_axis=1, tiled=True),
        lax.all_to_all(own_v, "head", split_axis=0, concat_axis=1, tiled=True),
    )
    group_total = wide_gk.shape[1] // (GROUP * HD)
    key_grad = (
        wide_gk.reshape(tok_count, group_total, GROUP, HD)
        .sum(axis=2)
        .reshape(tok_count, group_total * HD)
        .astype(jnp.bfloat16)
    )
    value_grad = (
        wide_gv.reshape(tok_count, group_total, GROUP, HD)
        .sum(axis=2)
        .reshape(tok_count, group_total * HD)
        .astype(jnp.bfloat16)
    )
    return (outputs, query_grad, key_grad, value_grad)


ROWS_BY_ROWS = (((1,), (1,)), ((), ()))
COLS_BY_COLS = (((0,), (0,)), ((), ()))
PLAIN = (((1,), (0,)), ((), ()))


def dot(left, right, dims):
    return lax.dot_general(left, right, dims, preferred_element_type=jnp.float32)


def head_cols(head):
    return slice(head * HD, (head + 1) * HD)


def device_index():
    return lax.axis_index("seq") * lax.axis_size("head") + lax.axis_index("head")


def start_all(pairs, sems):
    copies = [pltpu.make_async_copy(source, target, sems.at[at]) for at, (source, target) in enumerate(pairs)]
    for copy in copies:
        copy.start()
    return copies


def side_by_side(ref, rows=slice(None)):
    return jnp.concatenate([ref[rows, head_cols(head)] for head in range(GROUP)], axis=0)


def sends_far(device):
    return (device % 2 == 1) & (device < device_count() - 1)


def write_info(span, doc_ref, info_ref):
    device = device_index()
    before = doc_ref[jnp.maximum(device - 1, 0)]
    row = lax.broadcasted_iota(jnp.int32, info_ref.shape, 0)
    first = jnp.where(device > 0, before - span, span)
    info_ref[...] = jnp.where(row == 0, doc_ref[device], first)


def pack_kernel(span, halo, doc_far, k_far, v_far, edge_ref, info_ref, doc_ref, sems):
    sends = sends_far(device_index())

    @pl.when(jnp.logical_not(sends))
    def _():
        edge_ref[...] = jnp.zeros_like(edge_ref)
        info_ref[...] = jnp.zeros_like(info_ref)

    @pl.when(sends)
    def _():
        tail = pl.ds(span - halo, halo)
        pairs = (
            (k_far.at[tail], edge_ref.at[:, :HD]),
            (v_far.at[tail], edge_ref.at[:, HD:]),
            (doc_far, doc_ref),
        )
        for copy in start_all(pairs, sems):
            copy.wait()
        write_info(span, doc_ref, info_ref)


def pair_pack_kernel(span, halo, k_ref, v_ref, edge_ref):
    edge_ref[:, :HD] = k_ref[span - halo :]
    edge_ref[:, HD:] = v_ref[span - halo :]


def own_kernel(
    span, halo, doc_far, far_info_ref, q_ref, g_ref, k_ref, v_ref,
    low_ref, high_ref, gw_low_ref, gw_high_ref, stat_ref, mask_ref, qt_ref, gt_ref, tail_ref, out_far, dq_far, dk_far, dv_far,
    doc_ref, info_ref, row_ref, out_ref, dq_ref, dk_ref, dv_ref, doc_sem, sems,
):
    half = span // 2
    device = device_index()

    @pl.when(sends_far(device))
    def _():
        info_ref[...] = far_info_ref[...]

    @pl.when(jnp.logical_not(sends_far(device)))
    def _():
        copy = pltpu.make_async_copy(doc_far, doc_ref, doc_sem)
        copy.start()
        copy.wait()
        write_info(span, doc_ref, info_ref)

    gw_low = dot(v_ref[:half], side_by_side(g_ref), ROWS_BY_ROWS)
    gw_high = dot(v_ref[half:], side_by_side(g_ref, slice(half, span)), ROWS_BY_ROWS)
    low = dot(k_ref[:half], side_by_side(q_ref), ROWS_BY_ROWS)
    high = dot(k_ref[half:], side_by_side(q_ref, slice(half, span)), ROWS_BY_ROWS)
    start = info_ref[0:1, :1]
    first = info_ref[1:2, :1]
    key_pos = lax.broadcasted_iota(jnp.int32, (half, span), 0)
    row_pos = lax.broadcasted_iota(jnp.int32, (half, span), 1)
    fill_low = jnp.where((key_pos <= row_pos) & ((key_pos >= start) | (start > row_pos)), 0.0, masked_fill)
    key_pos = half + lax.broadcasted_iota(jnp.int32, (half, half), 0)
    row_pos = half + lax.broadcasted_iota(jnp.int32, (half, half), 1)
    fill_high = jnp.where((key_pos <= row_pos) & ((key_pos >= start) | (start > row_pos)), 0.0, masked_fill)
    key_pos = lax.broadcasted_iota(jnp.int32, (halo, span), 0) - halo
    row_pos = lax.broadcasted_iota(jnp.int32, (halo, span), 1)
    halo_ok = ((key_pos >= start) | (start > row_pos)) & (key_pos >= first)
    mask_ref[...] = jnp.where(halo_ok, 0.0, masked_fill)
    for head in range(GROUP):
        wide = slice(head * span, (head + 1) * span)
        slim = slice(head * half, (head + 1) * half)
        part = low[:, wide] * LOG2_SCALE + fill_low
        part_high = high[:, slim] * LOG2_SCALE + fill_high
        top = jnp.max(part, axis=0, keepdims=True)
        top_high = jnp.maximum(top[:, half:], jnp.max(part_high, axis=0, keepdims=True))
        top = jnp.concatenate([top[:, :half], top_high], axis=1)
        part = jnp.exp2(part - top)
        part_high = jnp.exp2(part_high - top_high)
        total = jnp.sum(part, axis=0, keepdims=True)
        inner = jnp.sum(part * gw_low[:, wide], axis=0, keepdims=True)
        total_high = total[:, half:] + jnp.sum(part_high, axis=0, keepdims=True)
        inner_high = inner[:, half:] + jnp.sum(part_high * gw_high[:, slim], axis=0, keepdims=True)
        low_ref[:, wide] = part
        high_ref[:, slim] = part_high
        stat_ref[0:1, wide] = top
        stat_ref[1:2, wide] = jnp.concatenate([total[:, :half], total_high], axis=1)
        stat_ref[2:3, wide] = jnp.concatenate([inner[:, :half], inner_high], axis=1)
    qt_ref[...] = side_by_side(q_ref).T
    gt_ref[...] = side_by_side(g_ref).T
    gw_low_ref[...] = gw_low
    gw_high_ref[...] = gw_high

    @pl.when(device == 0)
    def _():
        share = 1.0 / stat_ref[1:2]
        row_ref[0:1] = share
        row_ref[1:2] = stat_ref[2:3] * share
        finish(
            span, halo, q_ref, g_ref, k_ref, v_ref, low_ref, high_ref, gw_low_ref, gw_high_ref, row_ref, None,
            (out_ref, dq_ref, dk_ref, dv_ref, tail_ref), (out_far, dq_far, dk_far, dv_far), sems,
        )


def halo_kernel(
    span, mask_ref, pair_ref, ring_ref, q_ref, g_ref, qt_ref, gt_ref, stat_ref, edge_ref, p_ref, ds_ref, row_ref, back_ref
):
    queries = side_by_side(q_ref)
    grads = side_by_side(g_ref)
    mask = jnp.concatenate([mask_ref[...]] * GROUP, axis=1)
    device = device_index()
    edge = jnp.where((device % 2 == 1) | (device == ring_cut(1)), pair_ref[...], ring_ref[...])
    edge_ref[...] = edge
    scores = dot(edge[:, :HD], qt_ref[...], PLAIN) * LOG2_SCALE + mask
    grad_weights = dot(edge[:, HD:], gt_ref[...], PLAIN)
    own_top = stat_ref[0:1]
    top = jnp.maximum(jnp.max(scores, axis=0, keepdims=True), own_top)
    weights = jnp.exp2(scores - top)
    shift = jnp.exp2(own_top - top)
    total = stat_ref[1:2] * shift + jnp.sum(weights, axis=0, keepdims=True)
    inner = stat_ref[2:3] * shift + jnp.sum(weights * grad_weights, axis=0, keepdims=True)
    share = 1.0 / total
    delta = inner * share
    p_low = (weights * share).astype(jnp.bfloat16)
    ds_low = (weights * (share * SCALE) * (grad_weights - delta)).astype(jnp.bfloat16)
    back_ref[:, :HD] = dot(ds_low, queries, PLAIN).astype(back_ref.dtype)
    back_ref[:, HD:] = dot(p_low, grads, PLAIN).astype(back_ref.dtype)
    p_ref[...] = p_low
    ds_ref[...] = ds_low
    row_ref[0:1] = shift * share
    row_ref[1:2] = delta


def finish(
    span, halo, q_ref, g_ref, k_ref, v_ref, low_ref, high_ref, gw_low_ref, gw_high_ref, row_ref, edge, near, far, sems
):
    out_ref, dq_ref, dk_ref, dv_ref, tail_ref = near
    half = span // 2
    nothing = jnp.zeros((half, half), jnp.bfloat16)
    share = row_ref[0:1]
    delta = row_ref[1:2]
    later = lambda row: jnp.concatenate(
        [row[:, head * span + half : (head + 1) * span] for head in range(GROUP)], axis=1
    )
    whole = lambda low, high: jnp.concatenate(
        [
            low,
            jnp.concatenate(
                [piece for head in range(GROUP) for piece in (nothing, high[:, head * half : (head + 1) * half])],
                axis=1,
            ),
        ],
        axis=0,
    )
    low = low_ref[...] * share
    high = high_ref[...] * later(share)
    p = whole(low.astype(jnp.bfloat16), high.astype(jnp.bfloat16))
    ds = whole(
        (low * (gw_low_ref[...] - delta) * SCALE).astype(jnp.bfloat16),
        (high * (gw_high_ref[...] - later(delta)) * SCALE).astype(jnp.bfloat16),
    )
    grad_key = dot(ds, side_by_side(q_ref), PLAIN)
    grad_value = dot(p, side_by_side(g_ref), PLAIN)
    keys = k_ref[...]
    values = v_ref[...]
    if edge is not None:
        edge_ref, p_ref, ds_ref = edge
        keys = jnp.concatenate([edge_ref[:, :HD], keys], axis=0)
        values = jnp.concatenate([edge_ref[:, HD:], values], axis=0)
        p = jnp.concatenate([p_ref[...], p], axis=0)
        ds = jnp.concatenate([ds_ref[...], ds], axis=0)
    out = dot(p, values, COLS_BY_COLS).astype(jnp.bfloat16)
    dq = dot(ds, keys, COLS_BY_COLS).astype(jnp.bfloat16)
    for head in range(GROUP):
        out_ref[:, head_cols(head)] = out[head * span : (head + 1) * span]
        dq_ref[:, head_cols(head)] = dq[head * span : (head + 1) * span]
    dk_ref[...] = grad_key.astype(jnp.bfloat16)
    dv_ref[...] = grad_value.astype(jnp.bfloat16)
    tail_ref[:, :HD] = grad_key[span - halo :]
    tail_ref[:, HD:] = grad_value[span - halo :]
    for copy in start_all(zip(near[:4], far), sems):
        copy.wait()


def rest_kernel(
    span, halo, q_ref, g_ref, k_ref, v_ref, edge_ref, low_ref, high_ref, gw_low_ref, gw_high_ref, p_ref, ds_ref,
    row_ref, out_in, dq_in, dk_in, dv_in, tail_in, out_far, dq_far, dk_far, dv_far, tail_ref,
    out_ref, dq_ref, dk_ref, dv_ref, sems,
):
    del out_in, dq_in, dk_in, dv_in, tail_in

    @pl.when(device_index() > 0)
    def _():
        finish(
            span, halo, q_ref, g_ref, k_ref, v_ref, low_ref, high_ref, gw_low_ref, gw_high_ref, row_ref,
            (edge_ref, p_ref, ds_ref), (out_ref, dq_ref, dk_ref, dv_ref, tail_ref),
            (out_far, dq_far, dk_far, dv_far), sems,
        )


def tail_kernel(span, halo, tail_ref, pair_ref, ring_ref, dk_in, dv_in, dk_far, dv_far, dk_ref, dv_ref, sems):
    del dk_in, dv_in
    device = device_index()
    back = jnp.where(device == ring_cut(-1) - 1, pair_ref[...], ring_ref[...]).astype(jnp.float32)
    total = tail_ref[...] + jnp.where(device == device_count() - 1, 0.0, back)
    dk_ref[...] = total[:, :HD].astype(jnp.bfloat16)
    dv_ref[...] = total[:, HD:].astype(jnp.bfloat16)
    last = pl.ds(span - halo, halo)
    for copy in start_all(((dk_ref, dk_far.at[last]), (dv_ref, dv_far.at[last])), sems):
        copy.wait()


def device_count():
    return lax.axis_size("seq") * lax.axis_size("head")


def ring_cut(steps):
    return device_count() // 2 + (2 if steps > 0 else -2)


def passed_on(value, pair_value, steps):
    count = device_count()
    cut = ring_cut(steps)
    rings = [(source, source + 1) for source in range(count)]
    rings[cut - 1] = (cut - 1, 0)
    rings[count - 1] = (count - 1, cut)
    pairs = [(source, source ^ 1) for source in range(count)]
    pairs[cut - 2 : cut + 2] = [(cut - 2, cut - 1), (cut - 1, cut), (cut, cut + 1), (cut + 1, cut - 2)]
    if steps < 0:
        rings, pairs = [[(target, source) for source, target in way] for way in (rings, pairs)]
    by_pair = lax.ppermute(pair_value, ("seq", "head"), pairs)
    return by_pair, lax.ppermute(value, ("seq", "head"), rings)


def span_on_device(queries, key_rows, value_rows, out_grad, doc_start):
    span = queries.shape[0]
    halo = span // 4
    wide, slim = (queries.shape, key_rows.shape)
    f32, bf16 = (jnp.float32, jnp.bfloat16)
    vmem = pl.BlockSpec(memory_space=pltpu.VMEM)
    hbm = pl.BlockSpec(memory_space=pltpu.HBM)
    near = lambda *values: [pltpu.with_memory_space_constraint(value, pltpu.VMEM) for value in values]
    far = lambda *values: [pltpu.with_memory_space_constraint(value, pltpu.HBM) for value in values]
    params = pltpu.CompilerParams(vmem_limit_bytes=VMEM_GRANT)
    results = [pltpu.VMEM(shape, bf16) for shape in (wide, wide, slim, slim)]
    results_far = [pltpu.HBM(shape, bf16) for shape in (wide, wide, slim, slim)]

    last_rows, info = pl.pallas_call(
        lambda *refs: pack_kernel(span, halo, *refs),
        in_specs=[hbm] * 3,
        out_specs=[vmem] * 2,
        out_shape=[pltpu.VMEM((halo, 2 * HD), bf16), pltpu.VMEM((8, HD), jnp.int32)],
        scratch_shapes=[pltpu.SMEM(doc_start.shape, jnp.int32), pltpu.SemaphoreType.DMA((3,))],
        compiler_params=params,
        cost_estimate=pl.CostEstimate(flops=4000000000, bytes_accessed=4 * 1024 * 1024, transcendentals=0),
        name="pack",
    )(*far(doc_start, key_rows, value_rows))
    pair_rows = pl.pallas_call(
        lambda *refs: pair_pack_kernel(span, halo, *refs),
        in_specs=[vmem] * 2,
        out_specs=vmem,
        out_shape=pltpu.VMEM((halo, 2 * HD), bf16),
        compiler_params=params,
        name="pair_pack",
    )(key_rows, value_rows)
    edges = passed_on(last_rows, pair_rows, 1)
    inputs = (queries, out_grad, key_rows, value_rows)
    low, high, gw_low, gw_high, stats, mask, near_qt, near_gt, tail, outputs, query_grad, key_grad, value_grad = pl.pallas_call(
        lambda *refs: own_kernel(span, halo, *refs),
        in_specs=[hbm] + [vmem] * 5,
        out_specs=[vmem] * 9 + [hbm] * 4,
        out_shape=[
            pltpu.VMEM((span // 2, GROUP * span), f32),
            pltpu.VMEM((span // 2, GROUP * span // 2), f32),
            pltpu.VMEM((span // 2, GROUP * span), f32),
            pltpu.VMEM((span // 2, GROUP * span // 2), f32),
            pltpu.VMEM((8, GROUP * span), f32),
            pltpu.VMEM((halo, span), f32),
            pltpu.VMEM((HD, GROUP * span), bf16),
            pltpu.VMEM((HD, GROUP * span), bf16),
            pltpu.VMEM((halo, 2 * HD), f32),
        ]
        + results_far,
        scratch_shapes=[
            pltpu.SMEM(doc_start.shape, jnp.int32),
            pltpu.VMEM((8, HD), jnp.int32),
            pltpu.VMEM((8, GROUP * span), f32),
        ]
        + results
        + [pltpu.SemaphoreType.DMA(()), pltpu.SemaphoreType.DMA((4,))],
        compiler_params=params,
        name="own_scores",
    )(*far(doc_start), *near(info), *inputs)
    edge, p_edge, ds_edge, rows, back = pl.pallas_call(
        lambda *refs: halo_kernel(span, *refs),
        in_specs=[vmem] * 8,
        out_specs=[vmem] * 5,
        out_shape=[
            pltpu.VMEM((halo, 2 * HD), bf16),
            pltpu.VMEM((halo, GROUP * span), bf16),
            pltpu.VMEM((halo, GROUP * span), bf16),
            pltpu.VMEM((8, GROUP * span), f32),
            pltpu.VMEM((halo, 2 * HD), bf16),
        ],
        compiler_params=params,
        name="halo_grads",
    )(*near(mask, *edges), *inputs[:2], *near(near_qt, near_gt, stats))
    returned = passed_on(back, back, -1)
    outputs, query_grad, key_grad, value_grad, tail = pl.pallas_call(
        lambda *refs: rest_kernel(span, halo, *refs),
        in_specs=[vmem] * 12 + [hbm] * 4 + [vmem],
        out_specs=[hbm] * 4 + [vmem],
        out_shape=results_far + [pltpu.VMEM((halo, 2 * HD), f32)],
        scratch_shapes=results + [pltpu.SemaphoreType.DMA((4,))],
        input_output_aliases={12: 0, 13: 1, 14: 2, 15: 3, 16: 4},
        compiler_params=params,
        name="own_grads",
    )(
        *inputs,
        *near(edge, low, high, gw_low, gw_high, p_edge, ds_edge, rows),
        *far(outputs, query_grad, key_grad, value_grad),
        *near(tail),
    )
    key_grad, value_grad = pl.pallas_call(
        lambda *refs: tail_kernel(span, halo, *refs),
        in_specs=[vmem, vmem, vmem, hbm, hbm],
        out_specs=[hbm, hbm],
        out_shape=results_far[2:],
        scratch_shapes=[pltpu.VMEM((halo, HD), bf16)] * 2 + [pltpu.SemaphoreType.DMA((2,))],
        input_output_aliases={3: 0, 4: 1},
        compiler_params=params,
        name="tail_grads",
    )(*near(tail, *returned), *far(key_grad, value_grad))
    return (outputs, query_grad, key_grad, value_grad)


def per_device(queries, key_rows, value_rows, out_grad, doc_start):
    span = queries.shape[0] * lax.axis_size("head") // SPANS_DEV
    whole_span = span == queries.shape[0] and key_rows.shape[1] == HD and queries.shape[1] == GROUP * HD
    whole_span = whole_span and device_count() % 8 == 0 and device_count() >= 16
    plan = span_on_device if whole_span else spans_over_devices
    return plan(queries, key_rows, value_rows, out_grad, doc_start)


def solution(mesh):
    placed = (
        P(("seq", "head"), None),
        P(("seq", "head"), None),
        P(("seq", "head"), None),
        P(("seq", "head"), None),
        P(),
    )
    return jax.shard_map(
        per_device,
        mesh=mesh,
        in_specs=placed,
        out_specs=(
            P(("seq", "head"), None),
            P(("seq", "head"), None),
            P(("seq", "head"), None),
            P(("seq", "head"), None),
        ),
        check_vma=False,
    )
```
